512 devices in a mesh: tm: 128 (over y, z, core), batch: 4 (over x).
Axes of the slice: x: 4, y: 8, z: 8, core: 2. Of those that a mesh axis runs over, the one named last changes fastest.
Arguments:
- latents: bfloat16 [4, 32768, 512], P('batch', 'tm'), may hold values from -6 to 6
- w_now: bfloat16 [512, 1024], replicated, may hold values from -0.1875 to 0.1875
- w_delay: bfloat16 [512, 1024], replicated, may hold values from -0.1875 to 0.1875
- w_pred: bfloat16 [512, 512], replicated, may hold values from -0.25 to 0.25
- neg_owner: int32 [4, 32768, 4], P('batch', 'tm'), may hold values from 0 to 127, all different within a row; in each aligned block of 256 rows (0 to 255, 256 to 511, ..., all dimensions but the last counted through in order) at most 16 rows name the same one
- neg_block: int32 [4, 32768, 4], P('batch', 'tm'), may hold values from 0 to 1
Outputs:
- grad_delay: float32 [512, 1024], P('tm')
- grad_pred: float32 [512, 512], P('tm')
- frame_loss: float32 [4, 32768], P('batch', 'tm')
The draws below stay inside these ranges and needn't reach their ends.
Inputs may be any that keep to these rules, and one draw needn't show every extreme that they name: `neg_owner`: A frame's 4 entries are different. Among the 256 frames of one tm index of one recording, no shard is named more than 16 times, and in some such group one shard is named exactly 16 times.
All inputs are finite; a program needn't handle non-finite values.
Results may differ from the reference program's by a relative error of at most 0.011.
Values may be sent and summed in bfloat16 or wider, within the bound.
A program may use at most 64 MiB of HBM per device.

```python
import math
import jax
import jax.numpy as jnp
import numpy as np
from jax import lax

LATENT_CHANNELS = 512
F = 256
BLOCK = 128
NNEG = 4
KSTEP = 12
FB = 2
FRAMES = 32768
NREC = 4
DILATION_FRAMES = 1152
CAP = 16
NVALID = 131024
N_TM = 128


def touch_ends(entries, rng, low, largest):
    extent = entries.shape
    place = [jax.random.randint(jax.random.fold_in(rng, axis), (), 0, extent[axis]) for axis in range(len(extent))]
    entries = entries.at[tuple(place)].set(low)
    longest = extent.index(max(extent))
    place[longest] = (place[longest] + 1) % extent[longest]
    return entries.at[tuple(place)].set(largest)


def shard_levels(stream_key, extent, shards, least, high):
    level, own = 1.0, jax.random.fold_in(stream_key, 6)
    for axis_at, blocks in shards:
        heights = jnp.exp(jax.random.uniform(jax.random.fold_in(own, axis_at), (blocks,), jnp.float32, least / len(shards), high / len(shards)))
        level = level * jnp.repeat(heights, extent[axis_at] // blocks).reshape([-1 if axis == axis_at else 1 for axis in range(len(extent))])
    return level


def shared_out(stream_key, own, number, rows, count, top, most, slope):
    ranking = jax.random.permutation(stream_key, count)
    heavy_load, usual = shares(count, rows * top, most, slope, True), shares(count, rows * top, most, slope, False)
    places = jnp.arange(count)

    def named(tallies, turn):
        used = int((tallies > 0).sum())
        fixed = max(1, used // 4)
        shifted = fixed + (places - fixed + turn * (used - fixed)) % max(1, count - fixed)
        return jnp.zeros((count,), jnp.int32).at[ranking[jnp.where(places < fixed, places, shifted)]].set(jnp.asarray(tallies, jnp.int32))

    tallies = jnp.where(number % 4 == 0, named(heavy_load, number // 4), named(usual, number - number // 4 - 1))
    mixed = jax.random.permutation(jax.random.fold_in(own, 3), count)
    donor, sink = mixed[0:count // 2 * 2:2], mixed[1:count // 2 * 2:2]
    room = jnp.minimum(tallies[donor] - 1, most - tallies[sink]) // 2
    room = jnp.where((donor == ranking[0]) | (sink == ranking[0]) | (tallies[sink] == 0), 0, jnp.maximum(room, 0))
    shifted = jax.random.randint(jax.random.fold_in(own, 4), (count // 2,), 0, 1 << 20) % (room + 1)
    tallies = tallies.at[donor].add(-shifted).at[sink].add(shifted)
    members = jnp.searchsorted(jnp.cumsum(tallies), jnp.arange(rows * top), side="right").astype(jnp.int32)
    listing = members.reshape(top, rows).T
    listing = listing[jax.random.permutation(jax.random.fold_in(own, 1), rows)]
    turn = jax.random.randint(jax.random.fold_in(own, 2), (rows, 1), 0, top)
    return jnp.take_along_axis(listing, (jnp.arange(top)[None, :] + turn) % top, axis=1)


def shares(number_of, total, reach, skew, full):
    loads = [(1 << 20) // math.isqrt(standing ** skew) + 1 for standing in range(1, number_of + 1)]
    largest = reach if full else min(reach, max(-(-total // number_of), total * loads[0] // sum(loads)))
    least = 1 if total - largest >= number_of - 1 else 0
    holding, rest = [largest] + [least] * (number_of - 1), total - largest - least * (number_of - 1)
    while rest > 0:
        movable = [i for i in range(1, number_of) if holding[i] < largest] or [i for i in range(1, number_of) if holding[i] < reach]
        pool, budget = sum([loads[i] for i in movable]), rest
        for i in movable:
            extra = min(reach - holding[i], max(1, budget * loads[i] // pool), rest)
            holding[i] = holding[i] + extra
            rest = rest - extra
    return np.array(holding)


def noise(own_key, extent, width, most, cuts=(), kind=jnp.bfloat16):
    array = jax.random.normal(own_key, extent, jnp.float32) * width
    if len(cuts) > 0:
        array = shard_levels(own_key, extent, cuts, -0.22, 0.18) * array
    return jnp.clip(array, min=-most, max=most).astype(kind)


def setup_inputs(seed: int = 0) -> dict:
    keys = jax.random.split(jax.random.key(seed), 7)
    latents = noise(keys[0], (NREC, FRAMES, LATENT_CHANNELS), 1.0, 6.0, ((0, 4), (1, 128)))
    w_now = noise(keys[1], (LATENT_CHANNELS, 2 * LATENT_CHANNELS), (2 * LATENT_CHANNELS) ** -0.5, 0.1875)
    w_delay = noise(keys[2], (LATENT_CHANNELS, 2 * LATENT_CHANNELS), (2 * LATENT_CHANNELS) ** -0.5, 0.1875)
    w_pred = noise(keys[3], (LATENT_CHANNELS, LATENT_CHANNELS), LATENT_CHANNELS ** -0.5, 0.25)
    neg_owner_keys = jax.random.split(jax.random.fold_in(keys[4], 1), NREC * FRAMES // F)
    neg_owner_turns = jax.random.permutation(jax.random.fold_in(keys[4], 3), NREC * FRAMES // F)
    neg_owner = jax.vmap(lambda own, number: shared_out(jax.random.fold_in(keys[4], 2), own, number, F, N_TM, NNEG, CAP, 2))(neg_owner_keys, neg_owner_turns).reshape((NREC, FRAMES, NNEG))
    neg_block = touch_ends(jax.random.randint(keys[5], (NREC, FRAMES, NNEG), 0, FB), jax.random.fold_in(keys[5], 1), 0, FB - 1).astype(jnp.int32)
    return dict(latents=latents, w_now=w_now, w_delay=w_delay, w_pred=w_pred, neg_owner=neg_owner, neg_block=neg_block)


rho_radius = 16.0
norm_eps = 1e-06

def contract_rows(left, right):
    return lax.dot_general(left, right, (((0,), (0,)), ((), ())), preferred_element_type=jnp.float32)

def one_recording(latent_codes, owners, blocks, w_now, delay_weight, pred_weight):
    loss_total = latent_codes.shape[0]
    inv_root = LATENT_CHANNELS ** (-0.5)
    loss_weight = (LATENT_CHANNELS / NVALID) ** 0.5
    delayed_latent = jnp.concatenate([jnp.zeros((DILATION_FRAMES, LATENT_CHANNELS), latent_codes.dtype), latent_codes[:loss_total - DILATION_FRAMES]], 0)
    preact = jnp.dot(latent_codes, w_now, preferred_element_type=jnp.float32) + jnp.dot(delayed_latent, delay_weight, preferred_element_type=jnp.float32)
    tanh_part = jnp.tanh(preact[:, :LATENT_CHANNELS])
    gate_part = jax.nn.sigmoid(preact[:, LATENT_CHANNELS:])
    context = (latent_codes.astype(jnp.float32) + tanh_part * gate_part).astype(jnp.bfloat16)
    predicted = jnp.dot(context, pred_weight, preferred_element_type=jnp.float32).astype(jnp.bfloat16)
    target = jnp.concatenate([latent_codes[KSTEP:], jnp.zeros((KSTEP, LATENT_CHANNELS), latent_codes.dtype)], 0)
    positions = jnp.arange(loss_total, dtype=jnp.int32)
    valid_mask = (positions < loss_total - KSTEP).astype(jnp.float32)
    frame_index = (owners * F + blocks * BLOCK + (positions % BLOCK)[:, None]).astype(jnp.int32)
    first_hot = (jnp.arange(NNEG + 1) == 0).astype(jnp.float32)
    block_count = loss_total // F

    def per_block(packed):
        pred_rows, positive_target_rows, index_rows, mask_rows = packed
        negatives = latent_codes[index_rows]
        pred_float = pred_rows.astype(jnp.float32)
        neg_float = negatives.astype(jnp.float32)
        target_float = positive_target_rows.astype(jnp.float32)
        positive = lax.optimization_barrier(jnp.sum(pred_float * target_float, axis=-1)) * inv_root
        against = jnp.einsum('fc,fnc->fn', pred_float, neg_float) * inv_root
        scores = jnp.concatenate([positive[:, None], against], 1)
        top_score = lax.optimization_barrier(jnp.max(scores, axis=1))
        log_total = top_score + jnp.log(lax.optimization_barrier(jnp.sum(jnp.exp(scores - top_score[:, None]), axis=1)))
        probs = jnp.exp(scores - log_total[:, None])
        frame_loss_terms = mask_rows * (log_total - positive)
        dscores = loss_weight * mask_rows[:, None] * (probs - first_hot[None, :])
        accum = dscores[:, :1] * target_float
        for which in range(NNEG):
            accum = accum + dscores[:, which + 1:which + 2] * neg_float[:, which]
        pred_grad = (accum * inv_root).astype(jnp.bfloat16)
        return (pred_grad, frame_loss_terms)
    pred_grad, frame_loss_terms = lax.map(per_block, (predicted.reshape(block_count, F, LATENT_CHANNELS), target.reshape(block_count, F, LATENT_CHANNELS), frame_index.reshape(block_count, F, NNEG), valid_mask.reshape(block_count, F)))
    pred_grad = pred_grad.reshape(loss_total, LATENT_CHANNELS)
    frame_loss_terms = frame_loss_terms.reshape(loss_total)
    context_grad = jnp.dot(pred_grad, pred_weight.T, preferred_element_type=jnp.float32)
    filt_grad = context_grad * (1.0 - tanh_part * tanh_part) * gate_part
    gate_grad = context_grad * tanh_part * gate_part * (1.0 - gate_part)
    preact_grad = jnp.concatenate([filt_grad, gate_grad], 1).astype(jnp.bfloat16)
    return (contract_rows(delayed_latent, preact_grad), contract_rows(context, pred_grad), frame_loss_terms)

def reference(latents, w_now, w_delay, w_pred, neg_owner, neg_block):

    def gradient(delay_weight, pred_weight):
        sum_delay = jnp.zeros((LATENT_CHANNELS, 2 * LATENT_CHANNELS), jnp.float32)
        sum_pred = jnp.zeros((LATENT_CHANNELS, LATENT_CHANNELS), jnp.float32)
        losses = []
        for record in range(NREC):
            term_delay, term_pred, frame_loss_terms = one_recording(latents[record], neg_owner[record], neg_block[record], w_now, delay_weight, pred_weight)
            sum_delay = sum_delay + term_delay
            sum_pred = sum_pred + term_pred
            losses.append(frame_loss_terms)
        return (sum_delay, sum_pred, jnp.stack(losses, 0))
    first_delay, first_pred, unused = gradient(w_delay, w_pred)
    grad_norm = jnp.sqrt(jnp.sum(first_delay * first_delay) + jnp.sum(first_pred * first_pred))
    step_scale = rho_radius / (grad_norm + norm_eps)
    delay_up = (w_delay.astype(jnp.float32) + step_scale * first_delay).astype(jnp.bfloat16)
    pred_up = (w_pred.astype(jnp.float32) + step_scale * first_pred).astype(jnp.bfloat16)
    grad_delay, grad_pred, frame_loss = gradient(delay_up, pred_up)
    return (grad_delay, grad_pred, frame_loss)
```

```python
import jax
import jax.numpy as jnp
from jax import lax
from jax.sharding import PartitionSpec as P

BLOCK = 128
KSTEP = 12
LAG = 9
RHO = 16.0
EPS = 1e-06


def contract_rows(left, right):
    return lax.dot_general(left, right, (((0,), (0,)), ((), ())), preferred_element_type=jnp.float32)


def times_transposed(left, right):
    return lax.dot_general(left, right, (((1,), (1,)), ((), ())), preferred_element_type=jnp.float32)


def down(value, rows):
    return jnp.concatenate([jnp.zeros((rows, value.shape[1]), value.dtype), value[:-rows]], 0)


def up(value):
    return jnp.concatenate([value[1:], jnp.zeros((1, value.shape[1]), value.dtype)], 0)


def body(latents, w_now, w_delay, w_pred, neg_owner, neg_block):
    codes = latents[0]
    frames, channels = codes.shape
    shards = lax.axis_size("tm")
    blocks = frames // BLOCK
    residue = lax.axis_index("tm")
    neg_count = neg_owner.shape[2]
    inv_root = channels ** (-0.5)
    loss_weight = (channels / (lax.axis_size("batch") * (frames * shards - KSTEP))) ** 0.5

    by_residue = jnp.swapaxes(codes.reshape(blocks, BLOCK, channels), 0, 1)
    later = jnp.roll(by_residue, -KSTEP, axis=0)
    names = (neg_owner[0] * blocks + neg_block[0]).astype(jnp.bfloat16)
    names = jnp.swapaxes(names.reshape(blocks, BLOCK, neg_count), 0, 1)
    packed = jnp.concatenate(
        [
            by_residue.reshape(BLOCK, -1),
            later.reshape(BLOCK, -1),
            names.reshape(BLOCK, -1),
            jnp.zeros((BLOCK, BLOCK - blocks * neg_count), jnp.bfloat16),
        ],
        1,
    )
    came = lax.all_to_all(packed, "tm", split_axis=0, concat_axis=0, tiled=True)
    rows = shards * blocks
    wide = blocks * channels
    mine = came[:, :wide].reshape(rows, channels)
    target = came[:, wide : 2 * wide].reshape(rows, channels)
    chosen = came[:, 2 * wide : 2 * wide + blocks * neg_count].reshape(rows, neg_count)
    wraps = residue >= BLOCK - KSTEP
    target = jnp.where(wraps, up(target), target)
    delayed = down(mine, LAG)
    valid = jnp.where(wraps & (jnp.arange(rows) == rows - 1), 0.0, 1.0).astype(jnp.float32)
    hot = chosen.astype(jnp.int32)[:, :, None] == jnp.arange(rows, dtype=jnp.int32)[None, None, :]
    pre_now = jnp.dot(mine, w_now, preferred_element_type=jnp.float32)

    def gradient_terms(delay_weight, pred_weight):
        preact = pre_now + jnp.dot(delayed, delay_weight, preferred_element_type=jnp.float32)
        tanh_part = jnp.tanh(preact[:, :channels])
        gate_part = jax.nn.sigmoid(preact[:, channels:])
        context = (mine.astype(jnp.float32) + tanh_part * gate_part).astype(jnp.bfloat16)
        predicted = jnp.dot(context, pred_weight, preferred_element_type=jnp.float32).astype(jnp.bfloat16)
        positive = jnp.sum(predicted.astype(jnp.float32) * target.astype(jnp.float32), axis=1) * inv_root
        pairs = times_transposed(predicted, mine)
        against = jnp.sum(jnp.where(hot, pairs[:, None, :], 0.0), axis=2) * inv_root
        scores = jnp.concatenate([positive[:, None], against], 1)
        top = jnp.max(scores, axis=1)
        lse = top + jnp.log(jnp.sum(jnp.exp(scores - top[:, None]), axis=1))
        losses = valid * (lse - positive)
        probs = jnp.exp(scores - lse[:, None])
        scale = (loss_weight * valid)[:, None]
        d_pos = scale * (probs[:, :1] - 1.0)
        d_neg = scale * probs[:, 1:]
        spread = jnp.sum(jnp.where(hot, d_neg[:, :, None], 0.0), axis=1)
        high = spread.astype(jnp.bfloat16)
        low = (spread - high.astype(jnp.float32)).astype(jnp.bfloat16)
        pulled = jnp.dot(high, mine, preferred_element_type=jnp.float32) + jnp.dot(
            low, mine, preferred_element_type=jnp.float32
        )
        d_pred = ((d_pos * target.astype(jnp.float32) + pulled) * inv_root).astype(jnp.bfloat16)
        d_context = times_transposed(d_pred, pred_weight)
        d_filt = d_context * (1.0 - tanh_part * tanh_part) * gate_part
        d_gate = d_context * tanh_part * gate_part * (1.0 - gate_part)
        d_preact = jnp.concatenate([d_filt, d_gate], 1).astype(jnp.bfloat16)
        return contract_rows(delayed, d_preact), contract_rows(context, d_pred), losses

    def scattered(part_delay, part_pred):
        part = jnp.concatenate([part_delay, part_pred], 1).astype(jnp.bfloat16)
        pieces = lax.all_to_all(part, "tm", split_axis=0, concat_axis=0, tiled=True)
        pieces = pieces.reshape(shards, channels // shards, part.shape[1]).astype(jnp.float32)
        return lax.psum(jnp.sum(pieces, axis=0), "batch")

    first_delay, first_pred, _ = gradient_terms(w_delay, w_pred)
    mean_up = scattered(first_delay, first_pred)
    first = lax.all_gather(mean_up.astype(jnp.bfloat16), "tm", axis=0, tiled=True).astype(jnp.float32)
    step = RHO / (jnp.sqrt(jnp.sum(first * first)) + EPS)
    delay_up = (w_delay.astype(jnp.float32) + step * first[:, : 2 * channels]).astype(jnp.bfloat16)
    pred_up = (w_pred.astype(jnp.float32) + step * first[:, 2 * channels :]).astype(jnp.bfloat16)
    second_delay, second_pred, losses = gradient_terms(delay_up, pred_up)
    summed = scattered(second_delay, second_pred)
    back = lax.all_to_all(losses.reshape(shards, blocks), "tm", split_axis=0, concat_axis=0, tiled=True)
    frame_loss = jnp.swapaxes(back, 0, 1).reshape(1, frames)
    return summed[:, : 2 * channels], summed[:, 2 * channels :], frame_loss


def solution(mesh):
    return jax.shard_map(
        body,
        mesh=mesh,
        in_specs=(P("batch", "tm", None), P(), P(), P(), P("batch", "tm", None), P("batch", "tm", None)),
        out_specs=(P("tm", None), P("tm", None), P("batch", "tm")),
        check_vma=False,
    )
```

```python
import jax
import jax.numpy as jnp
from jax import lax
from jax.experimental import pallas as pl
from jax.experimental.pallas import tpu as pltpu
from jax.sharding import PartitionSpec as P

BLOCK = 128
KSTEP = 12
LAG = 9
NNEG = 4
RHO = 16.0
EPS = 1e-06
NY = NZ = 8
NX = 4
CH = 512
WIDE = 384
F32 = jnp.float32
BF16 = jnp.bfloat16


def contract_rows(left, right):
    return lax.dot_general(left, right, (((0,), (0,)), ((), ())), preferred_element_type=F32)


def times_transposed(left, right):
    return lax.dot_general(left, right, (((1,), (1,)), ((), ())), preferred_element_type=F32)


def product(left, right):
    return jnp.dot(left, right, preferred_element_type=F32)


def send(src, dst, sems, index, tm, batch):
    copy = pltpu.make_async_remote_copy(
        src_ref=src,
        dst_ref=dst,
        send_sem=sems.at[0, index],
        recv_sem=sems.at[1, index],
        device_id={"tm": tm, "batch": batch},
        device_id_type=pl.DeviceIdType.MESH,
    )
    copy.start()
    return copy


def step_kernel(
    mine_ref,
    target_ref,
    chosen_ref,
    w_now_ref,
    w_delay_ref,
    w_pred_ref,
    grad_delay_ref,
    grad_pred_ref,
    loss_ref,
    delayed_ref,
    pre_now_ref,
    tanh_ref,
    gate_ref,
    context_ref,
    d_pred_ref,
    d_pre_ref,
    delay_up_ref,
    pred_up_ref,
    part_ref,
    core_ref,
    sum_ref,
    wide_ref,
    half_ref,
    thin_ref,
    across_ref,
    whole_ref,
    core_sems,
    wide_sems,
    thin_sems,
    across_sems,
    gather_sems,
    spread_sems,
    pair_sems,
):
    me = lax.axis_index("tm")
    x = lax.axis_index("batch")
    y, z, c = me // (2 * NZ), (me // 2) % NZ, me % 2

    def place(yy, zz, cc):
        return (yy * NZ + zz) * 2 + cc

    others_y = [lax.rem(y + k, NY) for k in range(1, NY)]
    others_z = [lax.rem(z + k, NZ) for k in range(1, NZ)]
    u = x * 2 + c
    others_u = [lax.rem(u + k, 2 * NX) for k in range(1, 2 * NX)]

    barrier = pltpu.get_barrier_semaphore()

    def greet(tm, batch):
        pl.semaphore_signal(
            barrier, inc=1, device_id={"tm": tm, "batch": batch}, device_id_type=pl.DeviceIdType.MESH
        )

    for yy in others_y:
        greet(place(yy, z, c), x)
    for zz in others_z:
        greet(place(y, zz, c), x)
    for uu in others_u:
        greet(place(y, z, uu % 2), uu // 2)

    rows, channels = mine_ref.shape
    inv_root = channels ** (-0.5)
    loss_weight = (channels / (NX * (BLOCK * rows - KSTEP))) ** 0.5
    row_of = lax.broadcasted_iota(jnp.int32, (rows, 1), 0)
    valid = jnp.where((me >= BLOCK - KSTEP) & (row_of == rows - 1), 0.0, 1.0).astype(F32)
    column_of = lax.broadcasted_iota(jnp.int32, (rows, rows), 1)

    shifted = pltpu.roll(mine_ref[...].astype(F32), LAG, 0)
    delayed_ref[...] = jnp.where(row_of >= LAG, shifted, 0.0).astype(BF16)
    pre_now_ref[...] = product(mine_ref[...], w_now_ref[...])

    def gradient(delay_ref, pred_ref, keep_loss, turn):
        filt = pre_now_ref[:, :channels] + product(delayed_ref[...], delay_ref[:, :channels])
        gate = pre_now_ref[:, channels:] + product(delayed_ref[...], delay_ref[:, channels:])
        tanh_part = jnp.tanh(filt)
        gate_part = jax.nn.sigmoid(gate)
        tanh_ref[...] = tanh_part
        gate_ref[...] = gate_part
        context_ref[...] = (mine_ref[...].astype(F32) + tanh_part * gate_part).astype(BF16)
        predicted = product(context_ref[...], pred_ref[...]).astype(BF16)
        goal = target_ref[...].astype(F32)
        positive = jnp.sum(predicted.astype(F32) * goal, axis=1, keepdims=True) * inv_root
        pairs = times_transposed(predicted, mine_ref[...])
        names = chosen_ref[...]
        hot = [column_of == names[:, n : n + 1] for n in range(NNEG)]
        against = [
            jnp.sum(jnp.where(hot[n], pairs, 0.0), axis=1, keepdims=True) * inv_root for n in range(NNEG)
        ]
        top = positive
        for score in against:
            top = jnp.maximum(top, score)
        total = jnp.exp(positive - top)
        for score in against:
            total = total + jnp.exp(score - top)
        lse = top + jnp.log(total)
        if keep_loss:
            loss_ref[...] = valid * (lse - positive)
        scale = loss_weight * valid
        d_pos = scale * (jnp.exp(positive - lse) - 1.0)
        spread = jnp.zeros((rows, rows), F32)
        for n in range(NNEG):
            spread = spread + jnp.where(hot[n], scale * jnp.exp(against[n] - lse), 0.0)
        high = spread.astype(BF16)
        low = (spread - high.astype(F32)).astype(BF16)
        pulled = product(high, mine_ref[...]) + product(low, mine_ref[...])
        d_pred_ref[...] = ((d_pos * goal + pulled) * inv_root).astype(BF16)
        d_context = times_transposed(d_pred_ref[...], pred_ref[...])
        tanh_part = tanh_ref[...]
        gate_part = gate_ref[...]
        d_pre_ref[:, :channels] = (d_context * (1.0 - tanh_part * tanh_part) * gate_part).astype(BF16)
        d_pre_ref[:, channels:] = (d_context * tanh_part * gate_part * (1.0 - gate_part)).astype(BF16)

        def store(h, value, low_col, high_col):
            part_ref[turn, h, :, :, low_col:high_col] = value.astype(BF16).reshape(
                NY * NZ, 8, high_col - low_col
            )

        store(0, contract_rows(delayed_ref[...], d_pre_ref[:, :WIDE]), 0, WIDE)
        store(1, contract_rows(delayed_ref[...], d_pre_ref[:, WIDE : 2 * WIDE]), 0, WIDE)
        store(2, contract_rows(delayed_ref[...], d_pre_ref[:, 2 * WIDE :]), 0, 256)
        store(2, contract_rows(context_ref[...], d_pred_ref[:, :128]), 256, WIDE)
        store(3, contract_rows(context_ref[...], d_pred_ref[:, 128:]), 0, WIDE)

    def reduce(turn):
        mate = place(y, z, 1 - c)
        swaps = [
            send(part_ref.at[turn, 2 * (1 - c) + j], core_ref.at[turn, j], core_sems.at[turn], j, mate, x)
            for j in range(2)
        ]
        wide = []
        for j in range(2):
            swaps[j].wait()
            both = part_ref[turn, 2 * c + j].astype(F32) + core_ref[turn, j].astype(F32)
            sum_ref[turn, j] = both.astype(BF16).reshape(NY, NZ, 8, WIDE)
            for k in range(1, 8):
                if j == 0:
                    there = others_y[k - 1]
                    src, tm = sum_ref.at[turn, j, there], place(there, z, c)
                else:
                    there = others_z[k - 1]
                    src, tm = sum_ref.at[turn, j, :, there], place(y, there, c)
                wide.append(
                    send(src, wide_ref.at[turn, j, k - 1], wide_sems.at[turn, j], k - 1, tm, x)
                )
        thin = []
        for j in range(2):
            own = sum_ref[turn, j, y] if j == 0 else sum_ref[turn, j, :, z]
            total = own.astype(F32)
            for k in range(7):
                wide[7 * j + k].wait()
                total = total + wide_ref[turn, j, k].astype(F32)
            half_ref[turn, j] = total.astype(BF16)
            for k in range(1, 8):
                if j == 0:
                    there = others_z[k - 1]
                    tm = place(y, there, c)
                else:
                    there = others_y[k - 1]
                    tm = place(there, z, c)
                thin.append(
                    send(
                        half_ref.at[turn, j, there],
                        thin_ref.at[turn, j, k - 1],
                        thin_sems.at[turn, j],
                        k - 1,
                        tm,
                        x,
                    )
                )
        for j in range(2):
            total = half_ref[turn, j, z if j == 0 else y].astype(F32)
            for k in range(7):
                thin[7 * j + k].wait()
                total = total + thin_ref[turn, j, k].astype(F32)
            across_ref[turn, u, :, j * WIDE : (j + 1) * WIDE] = total

    def cross(turn):
        copies = [
            send(
                across_ref.at[turn, u],
                across_ref.at[turn, u],
                across_sems.at[turn],
                k,
                place(y, z, uu % 2),
                uu // 2,
            )
            for k, uu in enumerate(others_u)
        ]
        for copy in copies:
            copy.wait()

    gradient(w_delay_ref, w_pred_ref, False, 0)
    pl.semaphore_wait(barrier, 21)
    reduce(0)
    cross(0)

    total = across_ref[0, c]
    for xx in range(1, NX):
        total = total + across_ref[0, 2 * xx + c]
    whole_ref[2 * c, y, z] = total[:, :WIDE].astype(BF16)
    whole_ref[2 * c + 1, y, z] = total[:, WIDE:].astype(BF16)
    first = []
    for j in range(2):
        for k in range(7):
            there = others_z[k] if j == 0 else others_y[k]
            tm = place(y, there, c) if j == 0 else place(there, z, c)
            spot = whole_ref.at[2 * c + j, y, z]
            first.append(send(spot, spot, gather_sems.at[j], k, tm, x))
    second = []
    for j in range(2):
        for k in range(7):
            first[7 * j + k].wait()
        for k in range(7):
            there = others_y[k] if j == 0 else others_z[k]
            tm = place(there, z, c) if j == 0 else place(y, there, c)
            spot = whole_ref.at[2 * c + j, y] if j == 0 else whole_ref.at[2 * c + j, :, z]
            second.append(send(spot, spot, spread_sems.at[j], k, tm, x))
    third = []
    for j in range(2):
        for k in range(7):
            second[7 * j + k].wait()
        spot = whole_ref.at[2 * c + j]
        third.append(send(spot, spot, pair_sems, j, place(y, z, 1 - c), x))
    for copy in third:
        copy.wait()

    squares = jnp.zeros((8, 128), F32)
    for h in range(4):
        piece = whole_ref[h].astype(F32).reshape(channels, WIDE)
        squares = squares + jnp.sum((piece * piece).reshape(channels // 8, 8, 3, 128), axis=(0, 2))
    norm = jnp.sqrt(jnp.sum(squares))
    step = RHO / (norm + EPS)
    for h in range(4):
        piece = whole_ref[h].astype(F32).reshape(channels, WIDE) * step
        low, high = h * WIDE, (h + 1) * WIDE
        cut = min(max(2 * channels, low), high)
        if cut > low:
            delay_up_ref[:, low:cut] = (w_delay_ref[:, low:cut].astype(F32) + piece[:, : cut - low]).astype(BF16)
        if cut < high:
            at, to = cut - 2 * channels, high - 2 * channels
            pred_up_ref[:, at:to] = (w_pred_ref[:, at:to].astype(F32) + piece[:, cut - low :]).astype(BF16)

    gradient(delay_up_ref, pred_up_ref, True, 1)
    reduce(1)
    cross(1)
    for j in range(2):
        total = across_ref[1, j]
        for xx in range(1, NX):
            total = total + across_ref[1, 2 * xx + j]
        kept = jnp.where(c == 0, total[:4], total[4:])
        low, high = j * 2 * WIDE, (j + 1) * 2 * WIDE
        cut = min(high, 2 * channels)
        grad_delay_ref[:, low:cut] = kept[:, : cut - low]
        if cut < high:
            grad_pred_ref[:, cut - 2 * channels : high - 2 * channels] = kept[:, cut - low :]


def body(latents, w_now, w_delay, w_pred, neg_owner, neg_block):
    codes = latents[0]
    frames, channels = codes.shape
    shards = lax.axis_size("tm")
    blocks = frames // BLOCK
    residue = lax.axis_index("tm")
    by_residue = jnp.swapaxes(codes.reshape(blocks, BLOCK, channels), 0, 1)
    later = jnp.roll(by_residue, -KSTEP, axis=0)
    names = (neg_owner[0] * blocks + neg_block[0]).astype(BF16)
    names = jnp.swapaxes(names.reshape(blocks, BLOCK, NNEG), 0, 1)
    packed = jnp.concatenate(
        [
            by_residue.reshape(BLOCK, -1),
            later.reshape(BLOCK, -1),
            names.reshape(BLOCK, -1),
            jnp.zeros((BLOCK, BLOCK - blocks * NNEG), BF16),
        ],
        1,
    )
    came = lax.all_to_all(packed, "tm", split_axis=0, concat_axis=0, tiled=True)
    rows = shards * blocks
    wide = blocks * channels
    mine = came[:, :wide].reshape(rows, channels)
    target = came[:, wide : 2 * wide].reshape(rows, channels)
    chosen = came[:, 2 * wide : 2 * wide + blocks * NNEG].reshape(rows, NNEG).astype(jnp.int32)
    next_target = jnp.concatenate([target[1:], jnp.zeros((1, channels), BF16)], 0)
    target = jnp.where(residue >= BLOCK - KSTEP, next_target, target)

    vmem = pl.BlockSpec(memory_space=pltpu.VMEM)
    dma = pltpu.SemaphoreType.DMA
    grad_delay, grad_pred, losses = pl.pallas_call(
        step_kernel,
        out_shape=(
            jax.ShapeDtypeStruct((4, 2 * channels), F32),
            jax.ShapeDtypeStruct((4, channels), F32),
            jax.ShapeDtypeStruct((rows, 1), F32),
        ),
        in_specs=[vmem] * 6,
        out_specs=(vmem, vmem, vmem),
        scratch_shapes=[
            pltpu.VMEM((rows, channels), BF16),
            pltpu.VMEM((rows, 2 * channels), F32),
            pltpu.VMEM((rows, channels), F32),
            pltpu.VMEM((rows, channels), F32),
            pltpu.VMEM((rows, channels), BF16),
            pltpu.VMEM((rows, channels), BF16),
            pltpu.VMEM((rows, 2 * channels), BF16),
            pltpu.VMEM((channels, 2 * channels), BF16),
            pltpu.VMEM((channels, channels), BF16),
            pltpu.VMEM((2, 4, NY * NZ, 8, WIDE), BF16),
            pltpu.VMEM((2, 2, NY * NZ, 8, WIDE), BF16),
            pltpu.VMEM((2, 2, NY, NZ, 8, WIDE), BF16),
            pltpu.VMEM((2, 2, 7, 8, 8, WIDE), BF16),
            pltpu.VMEM((2, 2, 8, 8, WIDE), BF16),
            pltpu.VMEM((2, 2, 7, 8, WIDE), BF16),
            pltpu.VMEM((2, 2 * NX, 8, 2 * WIDE), F32),
            pltpu.VMEM((4, NY, NZ, 8, WIDE), BF16),
            dma((2, 2, 2)),
            dma((2, 2, 2, 7)),
            dma((2, 2, 2, 7)),
            dma((2, 2, 7)),
            dma((2, 2, 7)),
            dma((2, 2, 7)),
            dma((2, 2)),
        ],
        compiler_params=pltpu.CompilerParams(
            collective_id=0, has_side_effects=True, vmem_limit_bytes=48 * 1024 * 1024
        ),
    )(mine, target, chosen, w_now, w_delay, w_pred)
    back = lax.all_to_all(losses.reshape(shards, blocks), "tm", split_axis=0, concat_axis=0, tiled=True)
    frame_loss = jnp.swapaxes(back, 0, 1).reshape(1, frames)
    return grad_delay, grad_pred, frame_loss


def solution(mesh):
    return jax.shard_map(
        body,
        mesh=mesh,
        in_specs=(P("batch", "tm", None), P(), P(), P(), P("batch", "tm", None), P("batch", "tm", None)),
        out_specs=(P("tm", None), P("tm", None), P("batch", "tm")),
        check_vma=False,
    )
```

```python
import jax
import jax.numpy as jnp
from jax import lax
from jax.experimental import pallas as pl
from jax.experimental.pallas import tpu as pltpu
from jax.sharding import PartitionSpec as P

BLOCK = 128
KSTEP = 12
LAG = 9
NNEG = 4
RHO = 16.0
EPS = 1e-06
NY = NZ = 8
NX = 4
CH = 512
WIDE = 384
F32 = jnp.float32
BF16 = jnp.bfloat16


def contract_rows(left, right):
    return lax.dot_general(left, right, (((0,), (0,)), ((), ())), preferred_element_type=F32)


def times_transposed(left, right):
    return lax.dot_general(left, right, (((1,), (1,)), ((), ())), preferred_element_type=F32)


def product(left, right):
    return jnp.dot(left, right, preferred_element_type=F32)


def send(src, dst, sems, index, tm, batch):
    copy = pltpu.make_async_remote_copy(
        src_ref=src,
        dst_ref=dst,
        send_sem=sems.at[0, index],
        recv_sem=sems.at[1, index],
        device_id={"tm": tm, "batch": batch},
        device_id_type=pl.DeviceIdType.MESH,
    )
    copy.start()
    return copy


def residue_of(yy, zz, cc):
    turn = jnp.where((yy & 1) == 0, zz, 2 * NZ - 1 - zz)
    return ((yy >> 1) + KSTEP * (2 * turn + cc)) & (BLOCK - 1)


def ring_place(row, spot):
    chip, cc = spot // 2, spot % 2
    back = chip // NZ
    zz = jnp.where(back == 0, chip, 2 * NZ - 1 - chip)
    return ((2 * row + back) * NZ + zz) * 2 + cc


def picker(picked, count):
    return jnp.where(lax.broadcasted_iota(jnp.int32, (count, count), 1) == picked, 1.0, 0.0).astype(BF16)


def step_kernel(
    codes_ref,
    owner_ref,
    block_ref,
    w_now_hbm,
    w_delay_hbm,
    w_pred_hbm,
    grad_delay_ref,
    grad_pred_ref,
    frame_loss_ref,
    w_now_ref,
    w_delay_ref,
    w_pred_ref,
    mine_ref,
    target_ref,
    chosen_ref,
    names_ref,
    out_a1_ref,
    in_a1_ref,
    out_a2_ref,
    in_a2_ref,
    out_b1_ref,
    in_b1_ref,
    out_b2_ref,
    in_b2_ref,
    loss_y_ref,
    loss_y_in_ref,
    loss_z_ref,
    loss_z_in_ref,
    loss_c_ref,
    loss_c_in_ref,
    delayed_ref,
    pre_now_ref,
    tanh_ref,
    gate_ref,
    context_ref,
    d_pred_ref,
    d_pre_ref,
    delay_up_ref,
    pred_up_ref,
    part_ref,
    core_ref,
    sum_ref,
    wide_ref,
    half_ref,
    thin_ref,
    across_ref,
    whole_ref,
    weight_sems,
    rows_y_sems,
    rows_v_sems,
    ring_sems,
    loss_sems,
    loss_core_sems,
    core_sems,
    wide_sems,
    thin_sems,
    across_sems,
    gather_sems,
    spread_sems,
    pair_sems,
):
    me = lax.axis_index("tm")
    x = lax.axis_index("batch")
    y, z, c = me // (2 * NZ), (me // 2) % NZ, me % 2

    def place(yy, zz, cc):
        return (yy * NZ + zz) * 2 + cc

    others_y = [lax.rem(y + k, NY) for k in range(1, NY)]
    others_z = [lax.rem(z + k, NZ) for k in range(1, NZ)]
    u = x * 2 + c
    others_u = [lax.rem(u + k, 2 * NX) for k in range(1, 2 * NX)]
    v = z * 2 + c
    others_v = [lax.rem(v + k, 2 * NZ) for k in range(1, 2 * NZ)]
    row = y // 2
    spot = 2 * jnp.where(y % 2 == 0, z, 2 * NZ - 1 - z) + c
    ring_before = ring_place(row, lax.rem(spot + 4 * NZ - 1, 4 * NZ))
    ring_after = ring_place(row, lax.rem(spot + 1, 4 * NZ))
    residue = residue_of(y, z, c)

    barrier = pltpu.get_barrier_semaphore()

    def greet(tm, batch):
        pl.semaphore_signal(
            barrier, inc=1, device_id={"tm": tm, "batch": batch}, device_id_type=pl.DeviceIdType.MESH
        )

    for yy in others_y:
        greet(place(yy, z, c), x)
    for vv in others_v:
        greet(y * 2 * NZ + vv, x)
    for k in range(1, NX):
        for cc in range(2):
            greet(place(y, z, cc), lax.rem(x + k, NX))
    greet(ring_before, x)
    greet(ring_after, x)

    loads = [
        pltpu.make_async_copy(src, dst, weight_sems.at[i])
        for i, (src, dst) in enumerate(
            [(w_now_hbm, w_now_ref), (w_delay_hbm, w_delay_ref), (w_pred_hbm, w_pred_ref)]
        )
    ]
    for load in loads:
        load.start()

    rows, channels = codes_ref.shape
    cut_a = WIDE
    order = lax.broadcasted_iota(jnp.int32, (rows, 1), 0)
    flag = order & 1
    from_vy = picker((((order >> 2) & 7) << 5) + (((order >> 1) & 1) << 4) + ((order >> 5) << 1) + flag, rows)
    from_yv = picker((((order >> 1) & 7) << 5) + ((order >> 5) << 2) + (((order >> 4) & 1) << 1) + flag, rows)
    to_yv = picker(flag * BLOCK + residue_of(order >> 5, (order >> 2) & 7, (order >> 1) & 1), rows)
    to_vy = picker(flag * BLOCK + residue_of((order >> 1) & 7, order >> 5, (order >> 4) & 1), rows)

    names_ref[...] = jnp.zeros(names_ref.shape, F32)
    names_ref[:, :NNEG] = (owner_ref[...] * 2 + block_ref[...]).astype(F32)
    out_a1_ref[...] = product(to_yv, codes_ref[:, :cut_a]).astype(BF16).reshape(out_a1_ref.shape)
    out_b1_ref[:, :, :128] = product(to_vy, codes_ref[:, cut_a:]).astype(BF16).reshape(2 * NZ, 2 * NY, 128)
    out_b1_ref[:, :, 128:] = product(to_vy, names_ref[...].astype(BF16)).astype(BF16).reshape(2 * NZ, 2 * NY, 128)
    pl.semaphore_wait(barrier, 30)

    def over_y(src_ref, dst_ref, turn):
        dst_ref[y] = src_ref[y]
        return [
            send(src_ref.at[yy], dst_ref.at[y], rows_y_sems.at[turn], k, place(yy, z, c), x)
            for k, yy in enumerate(others_y)
        ]

    def over_v(src_ref, dst_ref, turn):
        dst_ref[v] = src_ref[v]
        return [
            send(src_ref.at[vv], dst_ref.at[v], rows_v_sems.at[turn], k, y * 2 * NZ + vv, x)
            for k, vv in enumerate(others_v)
        ]

    def finish(copies):
        for copy in copies:
            copy.wait()

    going_a = over_y(out_a1_ref, in_a1_ref, 0)
    going_b = over_v(out_b1_ref, in_b1_ref, 0)
    finish(going_a)
    out_a2_ref[...] = product(from_yv, in_a1_ref[...].reshape(rows, cut_a)).astype(BF16).reshape(out_a2_ref.shape)
    going_a = over_v(out_a2_ref, in_a2_ref, 1)
    finish(going_b)
    out_b2_ref[...] = product(from_vy, in_b1_ref[...].reshape(rows, 256)).astype(BF16).reshape(out_b2_ref.shape)
    going_b = over_y(out_b2_ref, in_b2_ref, 1)
    finish(going_a)
    mine_ref[:, :cut_a] = product(from_vy, in_a2_ref[...].reshape(rows, cut_a)).astype(BF16)
    finish(going_b)
    mine_ref[:, cut_a:] = in_b2_ref[:, :, :128].reshape(rows, 128)
    chosen_ref[...] = in_b2_ref[:, :, 128:].reshape(rows, 128).astype(F32).astype(jnp.int32)
    ahead = send(mine_ref, target_ref, ring_sems, 0, ring_before, x)

    inv_root = channels ** (-0.5)
    loss_weight = (channels / (NX * (BLOCK * rows - KSTEP))) ** 0.5
    row_of = lax.broadcasted_iota(jnp.int32, (rows, 1), 0)
    wraps = residue >= BLOCK - KSTEP
    valid = jnp.where(wraps & (row_of == rows - 1), 0.0, 1.0).astype(F32)
    column_of = lax.broadcasted_iota(jnp.int32, (rows, rows), 1)

    shifted = pltpu.roll(mine_ref[...].astype(F32), LAG, 0)
    delayed_ref[...] = jnp.where(row_of >= LAG, shifted, 0.0).astype(BF16)
    for load in loads:
        load.wait()
    pre_now_ref[...] = product(mine_ref[...], w_now_ref[...])
    lane = lax.broadcasted_iota(jnp.int32, (8, 128), 1)

    def gradient(delay_ref, pred_ref, turn):
        filt = pre_now_ref[:, :channels] + product(delayed_ref[...], delay_ref[:, :channels])
        gate = pre_now_ref[:, channels:] + product(delayed_ref[...], delay_ref[:, channels:])
        tanh_part = jnp.tanh(filt)
        gate_part = jax.nn.sigmoid(gate)
        tanh_ref[...] = tanh_part
        gate_ref[...] = gate_part
        context_ref[...] = (mine_ref[...].astype(F32) + tanh_part * gate_part).astype(BF16)
        predicted = product(context_ref[...], pred_ref[...]).astype(BF16)
        if turn == 0:
            ahead.wait()
            raw = target_ref[...].astype(F32)
            moved = jnp.where(row_of < rows - 1, pltpu.roll(raw, rows - 1, 0), 0.0)
            target_ref[...] = jnp.where(wraps, moved, raw).astype(BF16)
        goal = target_ref[...].astype(F32)
        positive = jnp.sum(predicted.astype(F32) * goal, axis=1, keepdims=True) * inv_root
        pairs = times_transposed(predicted, mine_ref[...])
        names = chosen_ref[...]
        hot = [column_of == names[:, n : n + 1] for n in range(NNEG)]
        against = [
            jnp.sum(jnp.where(hot[n], pairs, 0.0), axis=1, keepdims=True) * inv_root for n in range(NNEG)
        ]
        top = positive
        for score in against:
            top = jnp.maximum(top, score)
        total = jnp.exp(positive - top)
        for score in against:
            total = total + jnp.exp(score - top)
        lse = top + jnp.log(total)
        if turn == 1:
            losses = jnp.broadcast_to(valid * (lse - positive), (rows, 128))
            loss_y_ref[...] = losses.reshape(NY, 32, 128)
            for k, yy in enumerate(others_y):
                loss_going.append(
                    send(loss_y_ref.at[yy], loss_y_in_ref.at[k], loss_sems.at[0], k, place(yy, z, c), x)
                )
        scale = loss_weight * valid
        d_pos = scale * (jnp.exp(positive - lse) - 1.0)
        spread = jnp.zeros((rows, rows), F32)
        for n in range(NNEG):
            spread = spread + jnp.where(hot[n], scale * jnp.exp(against[n] - lse), 0.0)
        high = spread.astype(BF16)
        low = (spread - high.astype(F32)).astype(BF16)
        pulled = product(high, mine_ref[...]) + product(low, mine_ref[...])
        d_pred_ref[...] = ((d_pos * goal + pulled) * inv_root).astype(BF16)
        d_context = times_transposed(d_pred_ref[...], pred_ref[...])
        tanh_part = tanh_ref[...]
        gate_part = gate_ref[...]
        d_pre_ref[:, :channels] = (d_context * (1.0 - tanh_part * tanh_part) * gate_part).astype(BF16)
        d_pre_ref[:, channels:] = (d_context * tanh_part * gate_part * (1.0 - gate_part)).astype(BF16)

        def store(h, value, low_col, high_col):
            part_ref[turn, h, :, :, low_col:high_col] = value.astype(BF16).reshape(
                NY * NZ, 8, high_col - low_col
            )

        store(0, contract_rows(delayed_ref[...], d_pre_ref[:, :WIDE]), 0, WIDE)
        store(1, contract_rows(delayed_ref[...], d_pre_ref[:, WIDE : 2 * WIDE]), 0, WIDE)
        store(2, contract_rows(delayed_ref[...], d_pre_ref[:, 2 * WIDE :]), 0, 256)
        store(2, contract_rows(context_ref[...], d_pred_ref[:, :128]), 256, WIDE)
        store(3, contract_rows(context_ref[...], d_pred_ref[:, 128:]), 0, WIDE)

    loss_going = []

    def loss_to_z():
        finish(loss_going)
        own = jnp.broadcast_to(((lane & 7) == y)[:1], (32, 128))
        held = jnp.where(own, loss_y_ref[y], 0.0)
        for k in range(7):
            source = lax.rem(y + 7 - k, NY)
            came = jnp.broadcast_to(((lane & 7) == source)[:1], (32, 128))
            held = jnp.where(came, loss_y_in_ref[k], held)
        loss_z_ref[...] = jnp.zeros(loss_z_ref.shape, F32)
        for zz in range(NZ):
            loss_z_ref[zz, :4] = held[4 * zz : 4 * zz + 4]
        loss_going[:] = [
            send(loss_z_ref.at[zz], loss_z_in_ref.at[k], loss_sems.at[1], k, place(y, zz, c), x)
            for k, zz in enumerate(others_z)
        ]

    def loss_to_core():
        finish(loss_going)
        held = jnp.where((lane >> 3) == z, loss_z_ref[z], 0.0)
        for k in range(7):
            source = lax.rem(z + 7 - k, NZ)
            held = jnp.where((lane >> 3) == source, loss_z_in_ref[k], held)
        loss_c_ref[...] = held
        loss_going[:] = [send(loss_c_ref, loss_c_in_ref, loss_core_sems, 0, place(y, z, 1 - c), x)]

    def nothing():
        pass

    def reduce(turn, between=nothing, after=nothing):
        mate = place(y, z, 1 - c)
        swaps = [
            send(part_ref.at[turn, 2 * (1 - c) + j], core_ref.at[turn, j], core_sems.at[turn], j, mate, x)
            for j in range(2)
        ]
        wide = []
        for j in range(2):
            swaps[j].wait()
            both = part_ref[turn, 2 * c + j].astype(F32) + core_ref[turn, j].astype(F32)
            sum_ref[turn, j] = both.astype(BF16).reshape(NY, NZ, 8, WIDE)
            for k in range(1, 8):
                if j == 0:
                    there = others_y[k - 1]
                    src, tm = sum_ref.at[turn, j, there], place(there, z, c)
                else:
                    there = others_z[k - 1]
                    src, tm = sum_ref.at[turn, j, :, there], place(y, there, c)
                wide.append(
                    send(src, wide_ref.at[turn, j, k - 1], wide_sems.at[turn, j], k - 1, tm, x)
                )
        between()
        thin = []
        for j in range(2):
            own = sum_ref[turn, j, y] if j == 0 else sum_ref[turn, j, :, z]
            total = own.astype(F32)
            for k in range(7):
                wide[7 * j + k].wait()
                total = total + wide_ref[turn, j, k].astype(F32)
            half_ref[turn, j] = total.astype(BF16)
            for k in range(1, 8):
                if j == 0:
                    there = others_z[k - 1]
                    tm = place(y, there, c)
                else:
                    there = others_y[k - 1]
                    tm = place(there, z, c)
                thin.append(
                    send(
                        half_ref.at[turn, j, there],
                        thin_ref.at[turn, j, k - 1],
                        thin_sems.at[turn, j],
                        k - 1,
                        tm,
                        x,
                    )
                )
        after()
        for j in range(2):
            total = half_ref[turn, j, z if j == 0 else y].astype(F32)
            for k in range(7):
                thin[7 * j + k].wait()
                total = total + thin_ref[turn, j, k].astype(F32)
            across_ref[turn, u, :, j * WIDE : (j + 1) * WIDE] = total

    def cross(turn):
        copies = [
            send(
                across_ref.at[turn, u],
                across_ref.at[turn, u],
                across_sems.at[turn],
                k,
                place(y, z, uu % 2),
                uu // 2,
            )
            for k, uu in enumerate(others_u)
        ]
        for copy in copies:
            copy.wait()

    gradient(w_delay_ref, w_pred_ref, 0)
    reduce(0)
    cross(0)

    total = across_ref[0, c]
    for xx in range(1, NX):
        total = total + across_ref[0, 2 * xx + c]
    whole_ref[2 * c, y, z] = total[:, :WIDE].astype(BF16)
    whole_ref[2 * c + 1, y, z] = total[:, WIDE:].astype(BF16)
    first = []
    for j in range(2):
        for k in range(7):
            there = others_z[k] if j == 0 else others_y[k]
            tm = place(y, there, c) if j == 0 else place(there, z, c)
            spot = whole_ref.at[2 * c + j, y, z]
            first.append(send(spot, spot, gather_sems.at[j], k, tm, x))
    second = []
    for j in range(2):
        for k in range(7):
            first[7 * j + k].wait()
        for k in range(7):
            there = others_y[k] if j == 0 else others_z[k]
            tm = place(there, z, c) if j == 0 else place(y, there, c)
            spot = whole_ref.at[2 * c + j, y] if j == 0 else whole_ref.at[2 * c + j, :, z]
            second.append(send(spot, spot, spread_sems.at[j], k, tm, x))
    third = []
    for j in range(2):
        for k in range(7):
            second[7 * j + k].wait()
        spot = whole_ref.at[2 * c + j]
        third.append(send(spot, spot, pair_sems, j, place(y, z, 1 - c), x))
    for copy in third:
        copy.wait()

    squares = jnp.zeros((8, 128), F32)
    for h in range(4):
        piece = whole_ref[h].astype(F32).reshape(channels, WIDE)
        squares = squares + jnp.sum((piece * piece).reshape(channels // 8, 8, 3, 128), axis=(0, 2))
    norm = jnp.sqrt(jnp.sum(squares))
    step = RHO / (norm + EPS)
    for h in range(4):
        piece = whole_ref[h].astype(F32).reshape(channels, WIDE) * step
        low, high = h * WIDE, (h + 1) * WIDE
        cut = min(max(2 * channels, low), high)
        if cut > low:
            delay_up_ref[:, low:cut] = (w_delay_ref[:, low:cut].astype(F32) + piece[:, : cut - low]).astype(BF16)
        if cut < high:
            at, to = cut - 2 * channels, high - 2 * channels
            pred_up_ref[:, at:to] = (w_pred_ref[:, at:to].astype(F32) + piece[:, cut - low :]).astype(BF16)

    gradient(delay_up_ref, pred_up_ref, 1)
    reduce(1, loss_to_z, loss_to_core)
    cross(1)
    finish(loss_going)
    for j in range(2):
        total = across_ref[1, j]
        for xx in range(1, NX):
            total = total + across_ref[1, 2 * xx + j]
        kept = jnp.where(c == 0, total[:4], total[4:])
        low, high = j * 2 * WIDE, (j + 1) * 2 * WIDE
        cut = min(high, 2 * channels)
        grad_delay_ref[:, low:cut] = kept[:, : cut - low]
        if cut < high:
            grad_pred_ref[:, cut - 2 * channels : high - 2 * channels] = kept[:, cut - low :]

    seat = lax.broadcasted_iota(jnp.int32, (128, 128), 0)
    column = lax.broadcasted_iota(jnp.int32, (128, 128), 1)
    back = jnp.zeros((8, 128), F32)
    for held_ref, cc in ((loss_c_ref, c), (loss_c_in_ref, 1 - c)):
        spread = (seat < NY * NZ) & (residue_of(seat & 7, (seat >> 3) & 7, cc) == column)
        back = back + jnp.dot(
            held_ref[...],
            jnp.where(spread, 1.0, 0.0),
            preferred_element_type=F32,
            precision=lax.Precision.HIGHEST,
        )
    kept = jnp.where(c == 0, back[:2], back[2:4])
    frame_loss_ref[:, :BLOCK] = kept[:1]
    frame_loss_ref[:, BLOCK:] = kept[1:2]


def body(latents, w_now, w_delay, w_pred, neg_owner, neg_block):
    codes = latents[0]
    rows, channels = codes.shape
    vmem = pl.BlockSpec(memory_space=pltpu.VMEM)
    anywhere = pl.BlockSpec(memory_space=pl.ANY)
    dma = pltpu.SemaphoreType.DMA
    return pl.pallas_call(
        step_kernel,
        out_shape=(
            jax.ShapeDtypeStruct((4, 2 * channels), F32),
            jax.ShapeDtypeStruct((4, channels), F32),
            jax.ShapeDtypeStruct((1, rows), F32),
        ),
        in_specs=[vmem] * 3 + [anywhere] * 3,
        out_specs=(vmem, vmem, vmem),
        scratch_shapes=[
            pltpu.VMEM((channels, 2 * channels), BF16),
            pltpu.VMEM((channels, 2 * channels), BF16),
            pltpu.VMEM((channels, channels), BF16),
            pltpu.VMEM((rows, channels), BF16),
            pltpu.VMEM((rows, channels), BF16),
            pltpu.VMEM((rows, 128), jnp.int32),
            pltpu.VMEM((rows, 128), F32),
            pltpu.VMEM((8, 32, WIDE), BF16),
            pltpu.VMEM((8, 32, WIDE), BF16),
            pltpu.VMEM((16, 16, WIDE), BF16),
            pltpu.VMEM((16, 16, WIDE), BF16),
            pltpu.VMEM((16, 16, 256), BF16),
            pltpu.VMEM((16, 16, 256), BF16),
            pltpu.VMEM((8, 32, 256), BF16),
            pltpu.VMEM((8, 32, 256), BF16),
            pltpu.VMEM((8, 32, 128), F32),
            pltpu.VMEM((7, 32, 128), F32),
            pltpu.VMEM((8, 8, 128), F32),
            pltpu.VMEM((7, 8, 128), F32),
            pltpu.VMEM((8, 128), F32),
            pltpu.VMEM((8, 128), F32),
            pltpu.VMEM((rows, channels), BF16),
            pltpu.VMEM((rows, 2 * channels), F32),
            pltpu.VMEM((rows, channels), F32),
            pltpu.VMEM((rows, channels), F32),
            pltpu.VMEM((rows, channels), BF16),
            pltpu.VMEM((rows, channels), BF16),
            pltpu.VMEM((rows, 2 * channels), BF16),
            pltpu.VMEM((channels, 2 * channels), BF16),
            pltpu.VMEM((channels, channels), BF16),
            pltpu.VMEM((2, 4, NY * NZ, 8, WIDE), BF16),
            pltpu.VMEM((2, 2, NY * NZ, 8, WIDE), BF16),
            pltpu.VMEM((2, 2, NY, NZ, 8, WIDE), BF16),
            pltpu.VMEM((2, 2, 7, 8, 8, WIDE), BF16),
            pltpu.VMEM((2, 2, 8, 8, WIDE), BF16),
            pltpu.VMEM((2, 2, 7, 8, WIDE), BF16),
            pltpu.VMEM((2, 2 * NX, 8, 2 * WIDE), F32),
            pltpu.VMEM((4, NY, NZ, 8, WIDE), BF16),
            dma((3,)),
            dma((2, 2, 7)),
            dma((2, 2, 15)),
            dma((2, 1)),
            dma((2, 2, 7)),
            dma((2, 1)),
            dma((2, 2, 2)),
            dma((2, 2, 2, 7)),
            dma((2, 2, 2, 7)),
            dma((2, 2, 7)),
            dma((2, 2, 7)),
            dma((2, 2, 7)),
            dma((2, 2)),
        ],
        compiler_params=pltpu.CompilerParams(
            collective_id=0, has_side_effects=True, vmem_limit_bytes=48 * 1024 * 1024
        ),
    )(codes, neg_owner[0], neg_block[0], w_now, w_delay, w_pred)


def solution(mesh):
    return jax.shard_map(
        body,
        mesh=mesh,
        in_specs=(P("batch", "tm", None), P(), P(), P(), P("batch", "tm", None), P("batch", "tm", None)),
        out_specs=(P("tm", None), P("tm", None), P("batch", "tm")),
        check_vma=False,
    )
```

```python
import jax
import jax.numpy as jnp
from jax import lax
from jax.experimental import pallas as pl
from jax.experimental.pallas import tpu as pltpu
from jax.sharding import PartitionSpec as P

BLOCK = 128
KSTEP = 12
LAG = 9
NNEG = 4
RHO = 16.0
EPS = 1e-06
NY = NZ = 8
NX = 4
CH = 512
WIDE = 384
FAR_FIRST = (4, 3, 5, 2, 6, 1, 7)
NEAR_FIRST = (1, 7, 2, 6, 3, 5, 4)
FAR_FIRST_WIDE = (8, 9, 7, 6, 10, 11, 5, 4, 12, 13, 3, 2, 14, 15, 1)
F32 = jnp.float32
BF16 = jnp.bfloat16


def contract_rows(left, right):
    return lax.dot_general(left, right, (((0,), (0,)), ((), ())), preferred_element_type=F32)


def times_transposed(left, right):
    return lax.dot_general(left, right, (((1,), (1,)), ((), ())), preferred_element_type=F32)


def product(left, right):
    return jnp.dot(left, right, preferred_element_type=F32)


def send(src, dst, sems, index, tm, batch):
    copy = pltpu.make_async_remote_copy(
        src_ref=src,
        dst_ref=dst,
        send_sem=sems.at[0, index],
        recv_sem=sems.at[1, index],
        device_id={"tm": tm, "batch": batch},
        device_id_type=pl.DeviceIdType.MESH,
    )
    copy.start()
    return copy


def residue_of(yy, zz, cc):
    turn = jnp.where((yy & 1) == 0, zz, 2 * NZ - 1 - zz)
    return ((yy >> 1) + KSTEP * (2 * turn + cc)) & (BLOCK - 1)


def ring_place(row, spot):
    chip, cc = spot // 2, spot % 2
    back = chip // NZ
    zz = jnp.where(back == 0, chip, 2 * NZ - 1 - chip)
    return ((2 * row + back) * NZ + zz) * 2 + cc


def picker(picked, count):
    return jnp.where(lax.broadcasted_iota(jnp.int32, (count, count), 1) == picked, 1.0, 0.0).astype(BF16)


def step_kernel(
    codes_hbm,
    owner_hbm,
    block_hbm,
    w_now_hbm,
    w_delay_hbm,
    w_pred_hbm,
    grad_delay_ref,
    grad_pred_ref,
    frame_loss_ref,
    codes_ref,
    owner_ref,
    block_ref,
    w_now_ref,
    w_delay_ref,
    w_pred_ref,
    mine_ref,
    target_ref,
    chosen_ref,
    out_a1_ref,
    in_a1_ref,
    out_a2_ref,
    in_a2_ref,
    out_b1_ref,
    in_b1_ref,
    out_b2_ref,
    in_b2_ref,
    loss_y_ref,
    loss_y_in_ref,
    loss_z_ref,
    loss_z_in_ref,
    loss_c_ref,
    loss_c_in_ref,
    delayed_ref,
    pre_now_ref,
    tanh_ref,
    gate_ref,
    context_ref,
    d_pred_ref,
    d_pre_ref,
    delay_up_ref,
    pred_up_ref,
    part_ref,
    own_ref,
    core_ref,
    sum_ref,
    wide_ref,
    half_ref,
    thin_ref,
    across_ref,
    whole_ref,
    weight_sems,
    rows_y_sems,
    rows_v_sems,
    ring_sems,
    loss_sems,
    loss_core_sems,
    core_sems,
    wide_sems,
    thin_sems,
    across_sems,
    gather_sems,
    spread_sems,
    pair_sems,
):
    me = lax.axis_index("tm")
    x = lax.axis_index("batch")
    y, z, c = me // (2 * NZ), (me // 2) % NZ, me % 2

    def place(yy, zz, cc):
        return (yy * NZ + zz) * 2 + cc

    others_y = [lax.rem(y + k, NY) for k in range(1, NY)]
    others_z = [lax.rem(z + k, NZ) for k in range(1, NZ)]
    u = x * 2 + c
    others_u = [lax.rem(u + k, 2 * NX) for k in range(1, 2 * NX)]
    v = z * 2 + c
    others_v = [lax.rem(v + k, 2 * NZ) for k in range(1, 2 * NZ)]
    row = y // 2
    spot = 2 * jnp.where(y % 2 == 0, z, 2 * NZ - 1 - z) + c
    ring_before = ring_place(row, lax.rem(spot + 4 * NZ - 1, 4 * NZ))
    ring_after = ring_place(row, lax.rem(spot + 1, 4 * NZ))
    residue = residue_of(y, z, c)

    barrier = pltpu.get_barrier_semaphore()

    def greet(tm, batch):
        pl.semaphore_signal(
            barrier, inc=1, device_id={"tm": tm, "batch": batch}, device_id_type=pl.DeviceIdType.MESH
        )

    for k in FAR_FIRST:
        greet(place(others_y[k - 1], z, c), x)
    for k in FAR_FIRST_WIDE:
        greet(y * 2 * NZ + others_v[k - 1], x)
    for k in range(1, NX):
        for cc in range(2):
            greet(place(y, z, cc), lax.rem(x + k, NX))
    greet(ring_before, x)
    greet(ring_after, x)

    loads = [
        pltpu.make_async_copy(src, dst, weight_sems.at[i])
        for i, (src, dst) in enumerate(
            [
                (codes_hbm, codes_ref),
                (owner_hbm, owner_ref),
                (block_hbm, block_ref),
                (w_now_hbm, w_now_ref),
                (w_delay_hbm, w_delay_ref),
                (w_pred_hbm, w_pred_ref),
            ]
        )
    ]
    for load in loads:
        load.start()

    rows, channels = codes_hbm.shape
    cut_a = WIDE
    order = lax.broadcasted_iota(jnp.int32, (rows, 1), 0)
    flag = order & 1
    from_vy = picker((((order >> 2) & 7) << 5) + (((order >> 1) & 1) << 4) + ((order >> 5) << 1) + flag, rows)
    from_yv = picker((((order >> 1) & 7) << 5) + ((order >> 5) << 2) + (((order >> 4) & 1) << 1) + flag, rows)
    to_yv = picker(flag * BLOCK + residue_of(order >> 5, (order >> 2) & 7, (order >> 1) & 1), rows)
    to_vy = picker(flag * BLOCK + residue_of((order >> 1) & 7, order >> 5, (order >> 4) & 1), rows)

    for load in loads[:3]:
        load.wait()
    names = (owner_ref[...] * 2 + block_ref[...]).astype(F32)
    names = jnp.concatenate([names, jnp.zeros((128 - NNEG, rows), F32)], 0).astype(BF16)
    out_a1_ref[...] = product(to_yv, codes_ref[:, :cut_a]).astype(BF16).reshape(out_a1_ref.shape)
    out_b1_ref[:, :, :128] = product(to_vy, codes_ref[:, cut_a:]).astype(BF16).reshape(2 * NZ, 2 * NY, 128)
    out_b1_ref[:, :, 128:] = times_transposed(to_vy, names).astype(BF16).reshape(2 * NZ, 2 * NY, 128)
    pl.semaphore_wait(barrier, 30)

    def over_y(src_ref, dst_ref, turn):
        dst_ref[y] = src_ref[y]
        return [
            send(
                src_ref.at[others_y[k - 1]],
                dst_ref.at[y],
                rows_y_sems.at[turn],
                k - 1,
                place(others_y[k - 1], z, c),
                x,
            )
            for k in FAR_FIRST
        ]

    def over_v(src_ref, dst_ref, turn):
        dst_ref[v] = src_ref[v]
        return [
            send(
                src_ref.at[others_v[k - 1]],
                dst_ref.at[v],
                rows_v_sems.at[turn],
                k - 1,
                y * 2 * NZ + others_v[k - 1],
                x,
            )
            for k in FAR_FIRST_WIDE
        ]

    def finish(copies):
        for copy in copies:
            copy.wait()

    going_a = over_y(out_a1_ref, in_a1_ref, 0)
    going_b = over_v(out_b1_ref, in_b1_ref, 0)
    finish(going_a)
    out_a2_ref[...] = product(from_yv, in_a1_ref[...].reshape(rows, cut_a)).astype(BF16).reshape(out_a2_ref.shape)
    going_a = over_v(out_a2_ref, in_a2_ref, 1)
    finish(going_b)
    out_b2_ref[...] = product(from_vy, in_b1_ref[...].reshape(rows, 256)).astype(BF16).reshape(out_b2_ref.shape)
    going_b = over_y(out_b2_ref, in_b2_ref, 1)
    finish(going_a)
    mine_ref[:, :cut_a] = product(from_vy, in_a2_ref[...].reshape(rows, cut_a)).astype(BF16)
    ahead = [send(mine_ref.at[:, :cut_a], target_ref.at[:, :cut_a], ring_sems, 0, ring_before, x)]
    finish(going_b)
    mine_ref[:, cut_a:] = in_b2_ref[:, :, :128].reshape(rows, 128)
    chosen_ref[...] = in_b2_ref[:, :, 128:].reshape(rows, 128).astype(F32).astype(jnp.int32)
    ahead.append(send(mine_ref.at[:, cut_a:], target_ref.at[:, cut_a:], ring_sems, 1, ring_before, x))

    inv_root = channels ** (-0.5)
    loss_weight = (channels / (NX * (BLOCK * rows - KSTEP))) ** 0.5
    row_of = lax.broadcasted_iota(jnp.int32, (rows, 1), 0)
    wraps = residue >= BLOCK - KSTEP
    valid = jnp.where(wraps & (row_of == rows - 1), 0.0, 1.0).astype(F32)
    column_of = lax.broadcasted_iota(jnp.int32, (rows, rows), 1)

    shifted = pltpu.roll(mine_ref[...].astype(F32), LAG, 0)
    delayed_ref[...] = jnp.where(row_of >= LAG, shifted, 0.0).astype(BF16)
    for load in loads[3:]:
        load.wait()
    pre_now_ref[...] = product(mine_ref[...], w_now_ref[...])
    lane = lax.broadcasted_iota(jnp.int32, (8, 128), 1)

    def gradient(delay_ref, pred_ref, turn):
        filt = pre_now_ref[:, :channels] + product(delayed_ref[...], delay_ref[:, :channels])
        gate = pre_now_ref[:, channels:] + product(delayed_ref[...], delay_ref[:, channels:])
        tanh_part = jnp.tanh(filt)
        gate_part = jax.nn.sigmoid(gate)
        tanh_ref[...] = tanh_part
        gate_ref[...] = gate_part
        context_ref[...] = (mine_ref[...].astype(F32) + tanh_part * gate_part).astype(BF16)
        predicted = product(context_ref[...], pred_ref[...]).astype(BF16)
        pairs = times_transposed(predicted, mine_ref[...])
        names = chosen_ref[...]
        hot = [column_of == names[:, n : n + 1] for n in range(NNEG)]
        against = [
            jnp.sum(jnp.where(hot[n], pairs, 0.0), axis=1, keepdims=True) * inv_root for n in range(NNEG)
        ]
        if turn == 0:
            finish(ahead)
            raw = target_ref[...].astype(F32)
            moved = jnp.where(row_of < rows - 1, pltpu.roll(raw, rows - 1, 0), 0.0)
            target_ref[...] = jnp.where(wraps, moved, raw).astype(BF16)
        goal = target_ref[...].astype(F32)
        positive = jnp.sum(predicted.astype(F32) * goal, axis=1, keepdims=True) * inv_root
        top = positive
        for score in against:
            top = jnp.maximum(top, score)
        total = jnp.exp(positive - top)
        for score in against:
            total = total + jnp.exp(score - top)
        lse = top + jnp.log(total)
        if turn == 1:
            losses = jnp.broadcast_to(valid * (lse - positive), (rows, 128))
            loss_y_ref[...] = losses.reshape(NY, 32, 128)
            for k, yy in enumerate(others_y):
                loss_going.append(
                    send(loss_y_ref.at[yy], loss_y_in_ref.at[k], loss_sems.at[0], k, place(yy, z, c), x)
                )
        scale = loss_weight * valid
        d_pos = scale * (jnp.exp(positive - lse) - 1.0)
        spread = jnp.zeros((rows, rows), F32)
        for n in range(NNEG):
            spread = spread + jnp.where(hot[n], scale * jnp.exp(against[n] - lse), 0.0)
        high = spread.astype(BF16)
        low = (spread - high.astype(F32)).astype(BF16)
        pulled = product(high, mine_ref[...]) + product(low, mine_ref[...])
        d_pred_ref[...] = ((d_pos * goal + pulled) * inv_root).astype(BF16)
        d_context = times_transposed(d_pred_ref[...], pred_ref[...])
        tanh_part = tanh_ref[...]
        gate_part = gate_ref[...]
        d_pre_ref[:, :channels] = (d_context * (1.0 - tanh_part * tanh_part) * gate_part).astype(BF16)
        d_pre_ref[:, channels:] = (d_context * tanh_part * gate_part * (1.0 - gate_part)).astype(BF16)

        def fill(h, put):
            low, high = h * WIDE, (h + 1) * WIDE
            cut = min(max(2 * channels, low), high)
            if cut > low:
                put(0, cut - low, contract_rows(delayed_ref[...], d_pre_ref[:, low:cut]))
            if cut < high:
                at, to = cut - 2 * channels, high - 2 * channels
                put(cut - low, WIDE, contract_rows(context_ref[...], d_pred_ref[:, at:to]))

        for j in range(2):
            for cc in range(2):

                @pl.when(c == cc)
                def _(j=j, cc=cc):
                    def put(low, high, value):
                        part_ref[turn, j, :, :, low:high] = value.astype(BF16).reshape(NY * NZ, 8, high - low)

                    fill(2 * (1 - cc) + j, put)

            swaps.append(
                send(part_ref.at[turn, j], core_ref.at[turn, j], core_sems.at[turn], j, place(y, z, 1 - c), x)
            )
        for j in range(2):
            for cc in range(2):

                @pl.when(c == cc)
                def _(j=j, cc=cc):
                    def put(low, high, value):
                        own_ref[j, :, low:high] = value

                    fill(2 * cc + j, put)

            swaps[2 * turn + j].wait()
            both = own_ref[j].reshape(NY * NZ, 8, WIDE) + core_ref[turn, j].astype(F32)
            sum_ref[turn, j] = both.astype(BF16).reshape(NY, NZ, 8, WIDE)
            for k in FAR_FIRST:
                if j == 0:
                    there = others_y[k - 1]
                    src, tm = sum_ref.at[turn, j, there], place(there, z, c)
                else:
                    there = others_z[k - 1]
                    src, tm = sum_ref.at[turn, j, :, there], place(y, there, c)
                wide[turn, j, k] = send(src, wide_ref.at[turn, j, k - 1], wide_sems.at[turn, j], k - 1, tm, x)

    swaps = []
    wide = {}
    loss_going = []

    def loss_to_z():
        finish(loss_going)
        own = jnp.broadcast_to(((lane & 7) == y)[:1], (32, 128))
        held = jnp.where(own, loss_y_ref[y], 0.0)
        for k in range(7):
            source = lax.rem(y + 7 - k, NY)
            came = jnp.broadcast_to(((lane & 7) == source)[:1], (32, 128))
            held = jnp.where(came, loss_y_in_ref[k], held)
        loss_z_ref[...] = jnp.zeros(loss_z_ref.shape, F32)
        for zz in range(NZ):
            loss_z_ref[zz, :4] = held[4 * zz : 4 * zz + 4]
        loss_going[:] = [
            send(loss_z_ref.at[zz], loss_z_in_ref.at[k], loss_sems.at[1], k, place(y, zz, c), x)
            for k, zz in enumerate(others_z)
        ]

    def loss_to_core():
        finish(loss_going)
        held = jnp.where((lane >> 3) == z, loss_z_ref[z], 0.0)
        for k in range(7):
            source = lax.rem(z + 7 - k, NZ)
            held = jnp.where((lane >> 3) == source, loss_z_in_ref[k], held)
        loss_c_ref[...] = held
        loss_going[:] = [send(loss_c_ref, loss_c_in_ref, loss_core_sems, 0, place(y, z, 1 - c), x)]

    def nothing():
        pass

    def reduce(turn, between=nothing, after=nothing):
        between()
        thin = {}
        for j in range(2):
            own = sum_ref[turn, j, y] if j == 0 else sum_ref[turn, j, :, z]
            total = own.astype(F32)
            for k in NEAR_FIRST:
                wide[turn, j, k].wait()
                total = total + wide_ref[turn, j, k - 1].astype(F32)
            half_ref[turn, j] = total.astype(BF16)
            for k in FAR_FIRST:
                there = others_z[k - 1] if j == 0 else others_y[k - 1]
                tm = place(y, there, c) if j == 0 else place(there, z, c)
                thin[j, k] = send(
                    half_ref.at[turn, j, there],
                    thin_ref.at[turn, j, k - 1],
                    thin_sems.at[turn, j],
                    k - 1,
                    tm,
                    x,
                )
        after()
        for j in range(2):
            total = half_ref[turn, j, z if j == 0 else y].astype(F32)
            for k in NEAR_FIRST:
                thin[j, k].wait()
                total = total + thin_ref[turn, j, k - 1].astype(F32)
            across_ref[turn, u, :, j * WIDE : (j + 1) * WIDE] = total

    def cross(turn, peers):
        return [
            send(across_ref.at[turn, u], across_ref.at[turn, u], across_sems.at[turn], k, place(y, z, cc), xx)
            for k, (cc, xx) in enumerate(peers)
        ]

    gradient(w_delay_ref, w_pred_ref, 0)
    reduce(0)
    finish(cross(0, [(c, lax.rem(x + k, NX)) for k in (2, 1, 3)]))

    total = across_ref[0, c]
    for xx in range(1, NX):
        total = total + across_ref[0, 2 * xx + c]
    whole_ref[2 * c, y, z] = total[:, :WIDE].astype(BF16)
    whole_ref[2 * c + 1, y, z] = total[:, WIDE:].astype(BF16)
    first = {}
    for k in FAR_FIRST:
        for j in range(2):
            there = others_z[k - 1] if j == 0 else others_y[k - 1]
            tm = place(y, there, c) if j == 0 else place(there, z, c)
            spot = whole_ref.at[2 * c + j, y, z]
            first[j, k] = send(spot, spot, gather_sems.at[j], k - 1, tm, x)

    def spot_of(j, hop, half=None):
        along = lax.rem((y if j == 0 else z) + NY + hop, NY)
        rest = slice(None) if half is None else pl.ds(4 * half, 4)
        return whole_ref.at[2 * c, along, rest] if j == 0 else whole_ref.at[2 * c + 1, rest, along]

    def pass_on(j, hop, away, index, half=None):
        to = lax.rem((y if j == 0 else z) + NY + away, NY)
        tm = place(to, z, c) if j == 0 else place(y, to, c)
        spot = spot_of(j, hop, half)
        return send(spot, spot, spread_sems.at[j], index, tm, x)

    def to_mate(j, hop, index):
        spot = spot_of(j, hop)
        third.append(send(spot, spot, pair_sems.at[j], index, place(y, z, 1 - c), x))

    third = []
    second = {}
    for j in range(2):
        for k in NEAR_FIRST:
            first[j, k].wait()
        for index, away in enumerate((2, -2, 1, -1)):
            second[j, index] = pass_on(j, 0, away, index)
        to_mate(j, 0, 0)
    for j in range(2):
        second[j, 0].wait()
        second[j, 4] = pass_on(j, -2, 2, 4, 0)
        second[j, 5] = pass_on(j, -2, 1, 5)
        second[j, 1].wait()
        second[j, 6] = pass_on(j, 2, -2, 6, 1)
        second[j, 7] = pass_on(j, 2, -1, 7)
        second[j, 2].wait()
        to_mate(j, -1, 1)
        second[j, 3].wait()
        to_mate(j, 1, 2)
        to_mate(j, -2, 3)
        to_mate(j, 2, 4)
    for j in range(2):
        second[j, 5].wait()
        to_mate(j, -3, 5)
        second[j, 7].wait()
        to_mate(j, 3, 6)
        second[j, 4].wait()
        second[j, 6].wait()
        to_mate(j, 4, 7)
    finish(third)

    squares = jnp.zeros((8, 128), F32)
    for h in range(4):
        piece = whole_ref[h].astype(F32).reshape(channels, WIDE)
        squares = squares + jnp.sum((piece * piece).reshape(channels // 8, 8, 3, 128), axis=(0, 2))
    norm = jnp.sqrt(jnp.sum(squares))
    step = RHO / (norm + EPS)
    for h in range(4):
        piece = whole_ref[h].astype(F32).reshape(channels, WIDE) * step
        low, high = h * WIDE, (h + 1) * WIDE
        cut = min(max(2 * channels, low), high)
        if cut > low:
            delay_up_ref[:, low:cut] = (w_delay_ref[:, low:cut].astype(F32) + piece[:, : cut - low]).astype(BF16)
        if cut < high:
            at, to = cut - 2 * channels, high - 2 * channels
            pred_up_ref[:, at:to] = (w_pred_ref[:, at:to].astype(F32) + piece[:, cut - low :]).astype(BF16)

    gradient(delay_up_ref, pred_up_ref, 1)
    reduce(1, loss_to_z, loss_to_core)
    crossing = cross(1, [(uu % 2, uu // 2) for uu in others_u])
    finish(loss_going)
    seat = lax.broadcasted_iota(jnp.int32, (128, 128), 0)
    column = lax.broadcasted_iota(jnp.int32, (128, 128), 1)
    back = jnp.zeros((8, 128), F32)
    for held_ref, cc in ((loss_c_ref, c), (loss_c_in_ref, 1 - c)):
        spread = (seat < NY * NZ) & (residue_of(seat & 7, (seat >> 3) & 7, cc) == column)
        back = back + jnp.dot(
            held_ref[...],
            jnp.where(spread, 1.0, 0.0),
            preferred_element_type=F32,
            precision=lax.Precision.HIGHEST,
        )
    kept = jnp.where(c == 0, back[:2], back[2:4])
    frame_loss_ref[:, :BLOCK] = kept[:1]
    frame_loss_ref[:, BLOCK:] = kept[1:2]
    finish(crossing)
    for j in range(2):
        total = across_ref[1, j]
        for xx in range(1, NX):
            total = total + across_ref[1, 2 * xx + j]
        kept = jnp.where(c == 0, total[:4], total[4:])
        low, high = j * 2 * WIDE, (j + 1) * 2 * WIDE
        cut = min(high, 2 * channels)
        grad_delay_ref[:, low:cut] = kept[:, : cut - low]
        if cut < high:
            grad_pred_ref[:, cut - 2 * channels : high - 2 * channels] = kept[:, cut - low :]


def body(latents, w_now, w_delay, w_pred, neg_owner, neg_block):
    codes = latents[0]
    rows, channels = codes.shape
    vmem = pl.BlockSpec(memory_space=pltpu.VMEM)
    stay = pl.BlockSpec(memory_space=pltpu.HBM)
    dma = pltpu.SemaphoreType.DMA
    return pl.pallas_call(
        step_kernel,
        out_shape=(
            jax.ShapeDtypeStruct((4, 2 * channels), F32),
            jax.ShapeDtypeStruct((4, channels), F32),
            jax.ShapeDtypeStruct((1, rows), F32),
        ),
        in_specs=[stay] * 6,
        out_specs=(vmem, vmem, vmem),
        scratch_shapes=[
            pltpu.VMEM((rows, channels), BF16),
            pltpu.VMEM((NNEG, rows), jnp.int32),
            pltpu.VMEM((NNEG, rows), jnp.int32),
            pltpu.VMEM((channels, 2 * channels), BF16),
            pltpu.VMEM((channels, 2 * channels), BF16),
            pltpu.VMEM((channels, channels), BF16),
            pltpu.VMEM((rows, channels), BF16),
            pltpu.VMEM((rows, channels), BF16),
            pltpu.VMEM((rows, 128), jnp.int32),
            pltpu.VMEM((8, 32, WIDE), BF16),
            pltpu.VMEM((8, 32, WIDE), BF16),
            pltpu.VMEM((16, 16, WIDE), BF16),
            pltpu.VMEM((16, 16, WIDE), BF16),
            pltpu.VMEM((16, 16, 256), BF16),
            pltpu.VMEM((16, 16, 256), BF16),
            pltpu.VMEM((8, 32, 256), BF16),
            pltpu.VMEM((8, 32, 256), BF16),
            pltpu.VMEM((8, 32, 128), F32),
            pltpu.VMEM((7, 32, 128), F32),
            pltpu.VMEM((8, 8, 128), F32),
            pltpu.VMEM((7, 8, 128), F32),
            pltpu.VMEM((8, 128), F32),
            pltpu.VMEM((8, 128), F32),
            pltpu.VMEM((rows, channels), BF16),
            pltpu.VMEM((rows, 2 * channels), F32),
            pltpu.VMEM((rows, channels), F32),
            pltpu.VMEM((rows, channels), F32),
            pltpu.VMEM((rows, channels), BF16),
            pltpu.VMEM((rows, channels), BF16),
            pltpu.VMEM((rows, 2 * channels), BF16),
            pltpu.VMEM((channels, 2 * channels), BF16),
            pltpu.VMEM((channels, channels), BF16),
            pltpu.VMEM((2, 2, NY * NZ, 8, WIDE), BF16),
            pltpu.VMEM((2, channels, WIDE), F32),
            pltpu.VMEM((2, 2, NY * NZ, 8, WIDE), BF16),
            pltpu.VMEM((2, 2, NY, NZ, 8, WIDE), BF16),
            pltpu.VMEM((2, 2, 7, 8, 8, WIDE), BF16),
            pltpu.VMEM((2, 2, 8, 8, WIDE), BF16),
            pltpu.VMEM((2, 2, 7, 8, WIDE), BF16),
            pltpu.VMEM((2, 2 * NX, 8, 2 * WIDE), F32),
            pltpu.VMEM((4, NY, NZ, 8, WIDE), BF16),
            dma((6,)),
            dma((2, 2, 7)),
            dma((2, 2, 15)),
            dma((2, 2)),
            dma((2, 2, 7)),
            dma((2, 1)),
            dma((2, 2, 2)),
            dma((2, 2, 2, 7)),
            dma((2, 2, 2, 7)),
            dma((2, 2, 7)),
            dma((2, 2, 7)),
            dma((2, 2, 8)),
            dma((2, 2, 8)),
        ],
        compiler_params=pltpu.CompilerParams(
            collective_id=0, has_side_effects=True, vmem_limit_bytes=60 * 1024 * 1024
        ),
    )(codes, jnp.swapaxes(neg_owner[0], 0, 1), jnp.swapaxes(neg_block[0], 0, 1), w_now, w_delay, w_pred)


def solution(mesh):
    return jax.shard_map(
        body,
        mesh=mesh,
        in_specs=(P("batch", "tm", None), P(), P(), P(), P("batch", "tm", None), P("batch", "tm", None)),
        out_specs=(P("tm", None), P("tm", None), P("batch", "tm")),
        check_vma=False,
    )
```

```python
import jax
import jax.numpy as jnp
from jax import lax
from jax.experimental import pallas as pl
from jax.experimental.pallas import tpu as pltpu
from jax.sharding import PartitionSpec as P

BLOCK = 128
KSTEP = 12
LAG = 9
NNEG = 4
RHO = 16.0
EPS = 1e-06
NY = NZ = 8
NX = 4
CH = 512
WIDE = 384
FAR_FIRST = (4, 3, 5, 2, 6, 1, 7)
NEAR_FIRST = (1, 7, 2, 6, 3, 5, 4)
FAR_FIRST_WIDE = (8, 9, 7, 6, 10, 11, 5, 4, 12, 13, 3, 2, 14, 15, 1)
F32 = jnp.float32
BF16 = jnp.bfloat16


def contract_rows(left, right):
    return lax.dot_general(left, right, (((0,), (0,)), ((), ())), preferred_element_type=F32)


def times_transposed(left, right):
    return lax.dot_general(left, right, (((1,), (1,)), ((), ())), preferred_element_type=F32)


def product(left, right):
    return jnp.dot(left, right, preferred_element_type=F32)


def send(src, dst, sems, index, tm, batch):
    copy = pltpu.make_async_remote_copy(
        src_ref=src,
        dst_ref=dst,
        send_sem=sems.at[0, index],
        recv_sem=sems.at[1, index],
        device_id={"tm": tm, "batch": batch},
        device_id_type=pl.DeviceIdType.MESH,
    )
    copy.start()
    return copy


def residue_of(yy, zz, cc):
    turn = jnp.where((yy & 1) == 0, zz, 2 * NZ - 1 - zz)
    return ((yy >> 1) + KSTEP * (2 * turn + cc)) & (BLOCK - 1)


def ring_place(row, spot):
    chip, cc = spot // 2, spot % 2
    back = chip // NZ
    zz = jnp.where(back == 0, chip, 2 * NZ - 1 - chip)
    return ((2 * row + back) * NZ + zz) * 2 + cc


def picker(wanted, count):
    return jnp.where(lax.broadcasted_iota(jnp.int32, (count, count), 0) == wanted, 1.0, 0.0).astype(BF16)


def step_kernel(
    codes_hbm,
    owner_hbm,
    block_hbm,
    w_now_hbm,
    w_delay_hbm,
    w_pred_hbm,
    grad_delay_ref,
    grad_pred_ref,
    frame_loss_ref,
    codes_ref,
    owner_ref,
    block_ref,
    w_now_ref,
    w_delay_ref,
    w_pred_ref,
    mine_ref,
    target_ref,
    chosen_ref,
    out_a1_ref,
    in_a1_ref,
    out_a2_ref,
    in_a2_ref,
    out_b1_ref,
    in_b1_ref,
    out_b2_ref,
    in_b2_ref,
    loss_y_ref,
    loss_y_in_ref,
    loss_z_ref,
    loss_z_in_ref,
    loss_c_ref,
    loss_c_in_ref,
    delayed_ref,
    pre_now_ref,
    tanh_ref,
    gate_ref,
    context_ref,
    d_pred_ref,
    d_pre_ref,
    delay_up_ref,
    pred_up_ref,
    part_ref,
    core_ref,
    sum_ref,
    wide_ref,
    half_ref,
    thin_ref,
    across_ref,
    whole_ref,
    weight_sems,
    rows_y_sems,
    rows_v_sems,
    ring_sems,
    loss_sems,
    loss_core_sems,
    core_sems,
    wide_sems,
    thin_sems,
    across_sems,
    first_sems,
    second_sems,
    third_sems,
):
    me = lax.axis_index("tm")
    x = lax.axis_index("batch")
    y, z, c = me // (2 * NZ), (me // 2) % NZ, me % 2

    def place(yy, zz, cc):
        return (yy * NZ + zz) * 2 + cc

    others_y = [lax.rem(y + k, NY) for k in range(1, NY)]
    others_z = [lax.rem(z + k, NZ) for k in range(1, NZ)]
    u = x * 2 + c
    others_u = [lax.rem(u + k, 2 * NX) for k in range(1, 2 * NX)]
    v = z * 2 + c
    others_v = [lax.rem(v + k, 2 * NZ) for k in range(1, 2 * NZ)]
    row = y // 2
    spot = 2 * jnp.where(y % 2 == 0, z, 2 * NZ - 1 - z) + c
    ring_before = ring_place(row, lax.rem(spot + 4 * NZ - 1, 4 * NZ))
    ring_after = ring_place(row, lax.rem(spot + 1, 4 * NZ))
    residue = residue_of(y, z, c)

    barrier = pltpu.get_barrier_semaphore()

    def greet(tm, batch):
        pl.semaphore_signal(
            barrier, inc=1, device_id={"tm": tm, "batch": batch}, device_id_type=pl.DeviceIdType.MESH
        )

    for k in FAR_FIRST:
        greet(place(others_y[k - 1], z, c), x)
    for k in FAR_FIRST_WIDE:
        greet(y * 2 * NZ + others_v[k - 1], x)
    for k in range(1, NX):
        for cc in range(2):
            greet(place(y, z, cc), lax.rem(x + k, NX))
    greet(ring_before, x)
    greet(ring_after, x)

    loads = [
        pltpu.make_async_copy(src, dst, weight_sems.at[i])
        for i, (src, dst) in enumerate(
            [
                (codes_hbm, codes_ref),
                (owner_hbm, owner_ref),
                (block_hbm, block_ref),
                (w_now_hbm, w_now_ref),
                (w_delay_hbm, w_delay_ref),
                (w_pred_hbm, w_pred_ref),
            ]
        )
    ]
    for load in loads:
        load.start()

    rows, channels = codes_hbm.shape
    cut_a = WIDE
    order = lax.broadcasted_iota(jnp.int32, (1, rows), 1)
    flag = order & 1
    from_vy = picker((((order >> 1) & 7) << 5) + ((order >> 5) << 2) + (((order >> 4) & 1) << 1) + flag, rows)
    from_yv = picker((((order >> 2) & 7) << 5) + (((order >> 1) & 1) << 4) + ((order >> 5) << 1) + flag, rows)
    seat = (11 * ((order & (BLOCK - 1)) >> 2)) & 31
    chip, side, half = seat >> 1, seat & 1, order >> 7
    back = chip >> 3
    goal_y = 2 * (order & 3) + back
    goal_z = jnp.where(back == 0, chip, 2 * NZ - 1 - chip)
    to_yv = picker((goal_y << 5) + (goal_z << 2) + (side << 1) + half, rows)
    to_vy = picker((goal_z << 5) + (side << 4) + (goal_y << 1) + half, rows)

    for load in loads[:3]:
        load.wait()
    names = (owner_ref[...] * 2 + block_ref[...]).astype(F32)
    names = jnp.concatenate([names, jnp.zeros((128 - NNEG, rows), F32)], 0).astype(BF16)
    out_a1_ref[...] = product(to_yv, codes_ref[:, :cut_a]).astype(BF16).reshape(out_a1_ref.shape)
    out_b1_ref[:, :, :128] = product(to_vy, codes_ref[:, cut_a:]).astype(BF16).reshape(2 * NZ, 2 * NY, 128)
    out_b1_ref[:, :, 128:] = times_transposed(to_vy, names).astype(BF16).reshape(2 * NZ, 2 * NY, 128)
    pl.semaphore_wait(barrier, 30)

    def over_y(src_ref, dst_ref, turn):
        dst_ref[y] = src_ref[y]
        return [
            send(
                src_ref.at[others_y[k - 1]],
                dst_ref.at[y],
                rows_y_sems.at[turn],
                k - 1,
                place(others_y[k - 1], z, c),
                x,
            )
            for k in FAR_FIRST
        ]

    def over_v(src_ref, dst_ref, turn):
        dst_ref[v] = src_ref[v]
        return [
            send(
                src_ref.at[others_v[k - 1]],
                dst_ref.at[v],
                rows_v_sems.at[turn],
                k - 1,
                y * 2 * NZ + others_v[k - 1],
                x,
            )
            for k in FAR_FIRST_WIDE
        ]

    def finish(copies):
        for copy in copies:
            copy.wait()

    going_a = over_y(out_a1_ref, in_a1_ref, 0)
    going_b = over_v(out_b1_ref, in_b1_ref, 0)
    finish(going_a)
    out_a2_ref[...] = product(from_yv, in_a1_ref[...].reshape(rows, cut_a)).astype(BF16).reshape(out_a2_ref.shape)
    going_a = over_v(out_a2_ref, in_a2_ref, 1)
    finish(going_b)
    out_b2_ref[...] = product(from_vy, in_b1_ref[...].reshape(rows, 256)).astype(BF16).reshape(out_b2_ref.shape)
    going_b = over_y(out_b2_ref, in_b2_ref, 1)
    finish(going_a)
    mine_ref[:, :cut_a] = product(from_vy, in_a2_ref[...].reshape(rows, cut_a)).astype(BF16)
    ahead = [send(mine_ref.at[:, :cut_a], target_ref.at[:, :cut_a], ring_sems, 0, ring_before, x)]
    finish(going_b)
    mine_ref[:, cut_a:] = in_b2_ref[:, :, :128].reshape(rows, 128)
    chosen_ref[...] = in_b2_ref[:, :, 128:].reshape(rows, 128).astype(F32).astype(jnp.int32)
    ahead.append(send(mine_ref.at[:, cut_a:], target_ref.at[:, cut_a:], ring_sems, 1, ring_before, x))

    inv_root = channels ** (-0.5)
    loss_weight = (channels / (NX * (BLOCK * rows - KSTEP))) ** 0.5
    row_of = lax.broadcasted_iota(jnp.int32, (rows, 1), 0)
    wraps = residue >= BLOCK - KSTEP
    valid = jnp.where(wraps & (row_of == rows - 1), 0.0, 1.0).astype(F32)
    column_of = lax.broadcasted_iota(jnp.int32, (rows, rows), 1)

    shifted = pltpu.roll(mine_ref[...].astype(F32), LAG, 0)
    delayed_ref[...] = jnp.where(row_of >= LAG, shifted, 0.0).astype(BF16)
    for load in loads[3:]:
        load.wait()
    pre_now_ref[...] = product(mine_ref[...], w_now_ref[...])
    lane = lax.broadcasted_iota(jnp.int32, (8, 128), 1)

    def gradient(delay_ref, pred_ref, turn):
        filt = pre_now_ref[:, :channels] + product(delayed_ref[...], delay_ref[:, :channels])
        gate = pre_now_ref[:, channels:] + product(delayed_ref[...], delay_ref[:, channels:])
        tanh_part = jnp.tanh(filt)
        gate_part = jax.nn.sigmoid(gate)
        tanh_ref[...] = tanh_part
        gate_ref[...] = gate_part
        context_ref[...] = (mine_ref[...].astype(F32) + tanh_part * gate_part).astype(BF16)
        predicted = product(context_ref[...], pred_ref[...]).astype(BF16)
        pairs = times_transposed(predicted, mine_ref[...])
        names = chosen_ref[...]
        hot = [column_of == names[:, n : n + 1] for n in range(NNEG)]
        against = [
            jnp.sum(jnp.where(hot[n], pairs, 0.0), axis=1, keepdims=True) * inv_root for n in range(NNEG)
        ]
        if turn == 0:
            finish(ahead)
            raw = target_ref[...].astype(F32)
            moved = jnp.where(row_of < rows - 1, pltpu.roll(raw, rows - 1, 0), 0.0)
            target_ref[...] = jnp.where(wraps, moved, raw).astype(BF16)
        goal = target_ref[...].astype(F32)
        positive = jnp.sum(predicted.astype(F32) * goal, axis=1, keepdims=True) * inv_root
        top = positive
        for score in against:
            top = jnp.maximum(top, score)
        total = jnp.exp(positive - top)
        for score in against:
            total = total + jnp.exp(score - top)
        lse = top + jnp.log(total)
        if turn == 1:
            losses = jnp.broadcast_to(valid * (lse - positive), (rows, 128))
            loss_y_ref[...] = losses.reshape(NY, 32, 128)
            for k, yy in enumerate(others_y):
                loss_going.append(
                    send(loss_y_ref.at[yy], loss_y_in_ref.at[k], loss_sems.at[0], k, place(yy, z, c), x)
                )
        scale = loss_weight * valid
        d_pos = scale * (jnp.exp(positive - lse) - 1.0)
        spread = jnp.zeros((rows, rows), F32)
        for n in range(NNEG):
            spread = spread + jnp.where(hot[n], scale * jnp.exp(against[n] - lse), 0.0)
        high = spread.astype(BF16)
        low = (spread - high.astype(F32)).astype(BF16)
        pulled = product(high, mine_ref[...]) + product(low, mine_ref[...])
        d_pred_ref[...] = ((d_pos * goal + pulled) * inv_root).astype(BF16)
        swap(turn, 0)
        mine_first = own_part(0)
        d_context = times_transposed(d_pred_ref[...], pred_ref[...])
        tanh_part = tanh_ref[...]
        gate_part = gate_ref[...]
        d_pre_ref[:, :channels] = (d_context * (1.0 - tanh_part * tanh_part) * gate_part).astype(BF16)
        d_pre_ref[:, channels:] = (d_context * tanh_part * gate_part * (1.0 - gate_part)).astype(BF16)
        swap(turn, 1)
        swap(turn, 2)
        start_wide(turn, 0, mine_first)
        for t in (1, 2):
            start_wide(turn, t, own_part(t))

    def own_part(t, cc=c):
        if t == 0:
            cols = pl.ds(pl.multiple_of(256 * cc, 256), 256)
            return contract_rows(context_ref[...], d_pred_ref[:, cols])
        cols = pl.ds(pl.multiple_of(512 * cc + 256 * (t - 1), 256), 256)
        return contract_rows(delayed_ref[...], d_pre_ref[:, cols])

    mate = place(y, z, 1 - c)
    swaps = {}
    wide = {}
    thin = {}
    crossing = {}

    def swap(turn, t):
        value = own_part(t, 1 - c).astype(BF16).reshape(NY * NZ, 8, 256)
        for j in range(2):
            part_ref[turn, t, j] = value[:, :, 128 * j : 128 * (j + 1)]
        swaps[turn, t] = send(part_ref.at[turn, t], core_ref.at[turn, t], core_sems.at[turn], t, mate, x)

    def start_wide(turn, t, value):
        swaps[turn, t].wait()
        value = value.reshape(NY * NZ, 8, 256)
        for j in range(2):
            both = value[:, :, 128 * j : 128 * (j + 1)] + core_ref[turn, t, j].astype(F32)
            sum_ref[turn, t, j] = both.astype(BF16).reshape(NY, NZ, 8, 128)
            for k in FAR_FIRST:
                if j == 0:
                    there = others_y[k - 1]
                    src, tm = sum_ref.at[turn, t, j, there], place(there, z, c)
                else:
                    there = others_z[k - 1]
                    src, tm = sum_ref.at[turn, t, j, :, there], place(y, there, c)
                wide[turn, t, j, k] = send(
                    src, wide_ref.at[turn, t, j, k - 1], wide_sems.at[turn, t, j], k - 1, tm, x
                )

    def settle_wide(turn, t):
        for j in range(2):
            own = sum_ref[turn, t, j, y] if j == 0 else sum_ref[turn, t, j, :, z]
            total = own.astype(F32)
            for k in NEAR_FIRST:
                wide[turn, t, j, k].wait()
                total = total + wide_ref[turn, t, j, k - 1].astype(F32)
            half_ref[turn, t, j] = total.astype(BF16)
            for k in FAR_FIRST:
                there = others_z[k - 1] if j == 0 else others_y[k - 1]
                tm = place(y, there, c) if j == 0 else place(there, z, c)
                thin[turn, t, j, k] = send(
                    half_ref.at[turn, t, j, there],
                    thin_ref.at[turn, t, j, k - 1],
                    thin_sems.at[turn, t, j],
                    k - 1,
                    tm,
                    x,
                )

    def settle_thin(turn, t):
        for j in range(2):
            total = half_ref[turn, t, j, z if j == 0 else y].astype(F32)
            for k in NEAR_FIRST:
                thin[turn, t, j, k].wait()
                total = total + thin_ref[turn, t, j, k - 1].astype(F32)
            across_ref[turn, t, u, :, 128 * j : 128 * (j + 1)] = total
        if turn == 0:
            peers = [(c, lax.rem(x + k, NX)) for k in (2, 1, 3)]
        else:
            peers = [(uu % 2, uu // 2) for uu in others_u]
        spot = across_ref.at[turn, t, u]
        crossing[turn, t] = [
            send(spot, spot, across_sems.at[turn, t], k, place(y, z, cc), xx) for k, (cc, xx) in enumerate(peers)
        ]

    def summed(turn, t, cc):
        finish(crossing[turn, t])
        crossing[turn, t] = []
        total = across_ref[turn, t, cc]
        for xx in range(1, NX):
            total = total + across_ref[turn, t, 2 * xx + cc]
        return total

    first = {}
    second = {}
    third = {}

    def settle_cross(t):
        total = summed(0, t, c).astype(BF16)
        for j in range(2):
            whole_ref[c, t, j, y, z] = total[:, 128 * j : 128 * (j + 1)]
        for k in FAR_FIRST:
            for j in range(2):
                there = others_z[k - 1] if j == 0 else others_y[k - 1]
                tm = place(y, there, c) if j == 0 else place(there, z, c)
                spot = whole_ref.at[c, t, j, y, z]
                first[t, j, k] = send(spot, spot, first_sems.at[t, j], k - 1, tm, x)

    def stripe(t, j, along):
        return whole_ref.at[c, t, j, along] if j == 0 else whole_ref.at[c, t, j, :, along]

    def settle_first(t):
        for j in range(2):
            for k in NEAR_FIRST:
                first[t, j, k].wait()
            for k in FAR_FIRST:
                there = others_y[k - 1] if j == 0 else others_z[k - 1]
                tm = place(there, z, c) if j == 0 else place(y, there, c)
                spot = stripe(t, j, y if j == 0 else z)
                second[t, j, k] = send(spot, spot, second_sems.at[t, j], k - 1, tm, x)

    def settle_second(t):
        third[t] = []
        if t < 2:
            for k in NEAR_FIRST:
                for j in range(2):
                    second[t, j, k].wait()
            spot = whole_ref.at[c, t]
            third[t].append(send(spot, spot, third_sems.at[t, 0], 0, mate, x))
            return
        for j in range(2):
            spot = stripe(t, j, y if j == 0 else z)
            third[t].append(send(spot, spot, third_sems.at[t, j], 0, mate, x))
        for k in NEAR_FIRST:
            for j in range(2):
                second[t, j, k].wait()
                spot = stripe(t, j, lax.rem((y if j == 0 else z) + 8 - k, 8))
                third[t].append(send(spot, spot, third_sems.at[t, j], k, mate, x))

    loss_going = []

    def loss_to_z():
        finish(loss_going)
        own = jnp.broadcast_to(((lane & 7) == y)[:1], (32, 128))
        held = jnp.where(own, loss_y_ref[y], 0.0)
        for k in range(7):
            source = lax.rem(y + 7 - k, NY)
            came = jnp.broadcast_to(((lane & 7) == source)[:1], (32, 128))
            held = jnp.where(came, loss_y_in_ref[k], held)
        loss_z_ref[...] = jnp.zeros(loss_z_ref.shape, F32)
        for zz in range(NZ):
            loss_z_ref[zz, :4] = held[4 * zz : 4 * zz + 4]
        loss_going[:] = [
            send(loss_z_ref.at[zz], loss_z_in_ref.at[k], loss_sems.at[1], k, place(y, zz, c), x)
            for k, zz in enumerate(others_z)
        ]

    def loss_to_core():
        finish(loss_going)
        held = jnp.where((lane >> 3) == z, loss_z_ref[z], 0.0)
        for k in range(7):
            source = lax.rem(z + 7 - k, NZ)
            held = jnp.where((lane >> 3) == source, loss_z_in_ref[k], held)
        loss_c_ref[...] = held
        loss_going[:] = [send(loss_c_ref, loss_c_in_ref, loss_core_sems, 0, place(y, z, 1 - c), x)]

    gradient(w_delay_ref, w_pred_ref, 0)
    settle_wide(0, 0)
    settle_wide(0, 1)
    settle_wide(0, 2)
    settle_thin(0, 0)
    settle_thin(0, 1)
    settle_cross(0)
    settle_thin(0, 2)
    settle_cross(1)
    settle_first(0)
    settle_cross(2)
    settle_first(1)
    settle_second(0)
    settle_first(2)
    settle_second(1)

    squares = jnp.zeros((8, 128), F32)
    for t in range(3):
        if t == 2:
            settle_second(2)
        finish(third[t])
        for cc in range(2):
            for j in range(2):
                piece = whole_ref[cc, t, j].astype(F32).reshape(NY * NZ, 8, 128)
                squares = squares + jnp.sum(piece * piece, axis=0)
    norm = jnp.sqrt(jnp.sum(squares))
    step = RHO / (norm + EPS)
    for t in range(3):
        for cc in range(2):
            for j in range(2):
                piece = whole_ref[cc, t, j].astype(F32).reshape(channels, 128) * step
                low = 256 * cc + 128 * j if t == 0 else 512 * cc + 256 * (t - 1) + 128 * j
                old_ref, new_ref = (w_pred_ref, pred_up_ref) if t == 0 else (w_delay_ref, delay_up_ref)
                new_ref[:, low : low + 128] = (old_ref[:, low : low + 128].astype(F32) + piece).astype(BF16)

    gradient(delay_up_ref, pred_up_ref, 1)
    settle_wide(1, 0)
    settle_wide(1, 1)
    loss_to_z()
    settle_wide(1, 2)
    settle_thin(1, 0)
    settle_thin(1, 1)
    loss_to_core()
    settle_thin(1, 2)
    finish(loss_going)
    seat = lax.broadcasted_iota(jnp.int32, (128, 128), 0)
    column = lax.broadcasted_iota(jnp.int32, (128, 128), 1)
    back = jnp.zeros((8, 128), F32)
    for held_ref, cc in ((loss_c_ref, c), (loss_c_in_ref, 1 - c)):
        spread = (seat < NY * NZ) & (residue_of(seat & 7, (seat >> 3) & 7, cc) == column)
        back = back + jnp.dot(
            held_ref[...],
            jnp.where(spread, 1.0, 0.0),
            preferred_element_type=F32,
            precision=lax.Precision.HIGHEST,
        )
    kept = jnp.where(c == 0, back[:2], back[2:4])
    frame_loss_ref[:, :BLOCK] = kept[:1]
    frame_loss_ref[:, BLOCK:] = kept[1:2]
    for t in range(3):
        for cc in range(2):
            total = summed(1, t, cc)
            kept = jnp.where(c == 0, total[:4], total[4:])
            if t == 0:
                grad_pred_ref[:, 256 * cc : 256 * (cc + 1)] = kept
            else:
                low = 512 * cc + 256 * (t - 1)
                grad_delay_ref[:, low : low + 256] = kept


def body(latents, w_now, w_delay, w_pred, neg_owner, neg_block):
    codes = latents[0]
    rows, channels = codes.shape
    vmem = pl.BlockSpec(memory_space=pltpu.VMEM)
    stay = pl.BlockSpec(memory_space=pltpu.HBM)
    dma = pltpu.SemaphoreType.DMA
    return pl.pallas_call(
        step_kernel,
        out_shape=(
            jax.ShapeDtypeStruct((4, 2 * channels), F32),
            jax.ShapeDtypeStruct((4, channels), F32),
            jax.ShapeDtypeStruct((1, rows), F32),
        ),
        in_specs=[stay] * 6,
        out_specs=(vmem, vmem, vmem),
        scratch_shapes=[
            pltpu.VMEM((rows, channels), BF16),
            pltpu.VMEM((NNEG, rows), jnp.int32),
            pltpu.VMEM((NNEG, rows), jnp.int32),
            pltpu.VMEM((channels, 2 * channels), BF16),
            pltpu.VMEM((channels, 2 * channels), BF16),
            pltpu.VMEM((channels, channels), BF16),
            pltpu.VMEM((rows, channels), BF16),
            pltpu.VMEM((rows, channels), BF16),
            pltpu.VMEM((rows, 128), jnp.int32),
            pltpu.VMEM((8, 32, WIDE), BF16),
            pltpu.VMEM((8, 32, WIDE), BF16),
            pltpu.VMEM((16, 16, WIDE), BF16),
            pltpu.VMEM((16, 16, WIDE), BF16),
            pltpu.VMEM((16, 16, 256), BF16),
            pltpu.VMEM((16, 16, 256), BF16),
            pltpu.VMEM((8, 32, 256), BF16),
            pltpu.VMEM((8, 32, 256), BF16),
            pltpu.VMEM((8, 32, 128), F32),
            pltpu.VMEM((7, 32, 128), F32),
            pltpu.VMEM((8, 8, 128), F32),
            pltpu.VMEM((7, 8, 128), F32),
            pltpu.VMEM((8, 128), F32),
            pltpu.VMEM((8, 128), F32),
            pltpu.VMEM((rows, channels), BF16),
            pltpu.VMEM((rows, 2 * channels), F32),
            pltpu.VMEM((rows, channels), F32),
            pltpu.VMEM((rows, channels), F32),
            pltpu.VMEM((rows, channels), BF16),
            pltpu.VMEM((rows, channels), BF16),
            pltpu.VMEM((rows, 2 * channels), BF16),
            pltpu.VMEM((channels, 2 * channels), BF16),
            pltpu.VMEM((channels, channels), BF16),
            pltpu.VMEM((2, 3, 2, NY * NZ, 8, 128), BF16),
            pltpu.VMEM((2, 3, 2, NY * NZ, 8, 128), BF16),
            pltpu.VMEM((2, 3, 2, NY, NZ, 8, 128), BF16),
            pltpu.VMEM((2, 3, 2, 7, 8, 8, 128), BF16),
            pltpu.VMEM((2, 3, 2, 8, 8, 128), BF16),
            pltpu.VMEM((2, 3, 2, 7, 8, 128), BF16),
            pltpu.VMEM((2, 3, 2 * NX, 8, 256), F32),
            pltpu.VMEM((2, 3, 2, NY, NZ, 8, 128), BF16),
            dma((6,)),
            dma((2, 2, 7)),
            dma((2, 2, 15)),
            dma((2, 2)),
            dma((2, 2, 7)),
            dma((2, 1)),
            dma((2, 2, 3)),
            dma((2, 3, 2, 2, 7)),
            dma((2, 3, 2, 2, 7)),
            dma((2, 3, 2, 7)),
            dma((3, 2, 2, 7)),
            dma((3, 2, 2, 7)),
            dma((3, 2, 2, 8)),
        ],
        compiler_params=pltpu.CompilerParams(
            collective_id=0, has_side_effects=True, vmem_limit_bytes=60 * 1024 * 1024
        ),
    )(codes, jnp.swapaxes(neg_owner[0], 0, 1), jnp.swapaxes(neg_block[0], 0, 1), w_now, w_delay, w_pred)


def solution(mesh):
    return jax.shard_map(
        body,
        mesh=mesh,
        in_specs=(P("batch", "tm", None), P(), P(), P(), P("batch", "tm", None), P("batch", "tm", None)),
        out_specs=(P("tm", None), P("tm", None), P("batch", "tm")),
        check_vma=False,
    )
```

```python
import jax
import jax.numpy as jnp
from jax import lax
from jax.experimental import pallas as pl
from jax.experimental.pallas import tpu as pltpu
from jax.sharding import PartitionSpec as P

BLOCK = 128
KSTEP = 12
LAG = 9
NNEG = 4
RHO = 16.0
EPS = 1e-06
NY = NZ = 8
NX = 4
CH = 512
WIDE = 384
FAR_FIRST = (4, 3, 5, 2, 6, 1, 7)
NEAR_FIRST = (1, 7, 2, 6, 3, 5, 4)
FAR_FIRST_WIDE = (8, 9, 7, 6, 10, 11, 5, 4, 12, 13, 3, 2, 14, 15, 1)
F32 = jnp.float32
BF16 = jnp.bfloat16


def contract_rows(left, right):
    return lax.dot_general(left, right, (((0,), (0,)), ((), ())), preferred_element_type=F32)


def times_transposed(left, right):
    return lax.dot_general(left, right, (((1,), (1,)), ((), ())), preferred_element_type=F32)


def product(left, right):
    return jnp.dot(left, right, preferred_element_type=F32)


def send(src, dst, sems, index, tm, batch):
    copy = pltpu.make_async_remote_copy(
        src_ref=src,
        dst_ref=dst,
        send_sem=sems.at[0, index],
        recv_sem=sems.at[1, index],
        device_id={"tm": tm, "batch": batch},
        device_id_type=pl.DeviceIdType.MESH,
    )
    copy.start()
    return copy


def residue_of(yy, zz, cc):
    turn = jnp.where((yy & 1) == 0, zz, 2 * NZ - 1 - zz)
    return ((yy >> 1) + KSTEP * (2 * turn + cc)) & (BLOCK - 1)


def ring_place(row, spot):
    chip, cc = spot // 2, spot % 2
    back = chip // NZ
    zz = jnp.where(back == 0, chip, 2 * NZ - 1 - chip)
    return ((2 * row + back) * NZ + zz) * 2 + cc


def picker(wanted, count):
    return jnp.where(lax.broadcasted_iota(jnp.int32, (count, count), 0) == wanted, 1.0, 0.0).astype(BF16)


def step_kernel(
    codes_hbm,
    owner_hbm,
    block_hbm,
    w_now_hbm,
    w_delay_hbm,
    w_pred_hbm,
    grad_delay_ref,
    grad_pred_ref,
    frame_loss_ref,
    codes_ref,
    owner_ref,
    block_ref,
    w_now_ref,
    w_delay_ref,
    w_pred_ref,
    mine_ref,
    target_ref,
    chosen_ref,
    out_a1_ref,
    in_a1_ref,
    out_a2_ref,
    in_a2_ref,
    out_b1_ref,
    in_b1_ref,
    out_b2_ref,
    in_b2_ref,
    loss_y_ref,
    loss_y_in_ref,
    loss_z_ref,
    loss_z_in_ref,
    loss_c_ref,
    loss_c_in_ref,
    delayed_ref,
    pre_now_ref,
    tanh_ref,
    gate_ref,
    context_ref,
    d_pred_ref,
    d_pre_ref,
    delay_up_ref,
    pred_up_ref,
    pred_part_ref,
    pred_core_ref,
    pred_sum_ref,
    pred_wide_ref,
    pred_half_ref,
    pred_thin_ref,
    tail_ref,
    pred_whole_ref,
    pred_last_ref,
    part_ref,
    core_ref,
    sum_ref,
    wide_ref,
    half_ref,
    thin_ref,
    across_ref,
    final_ref,
    whole_ref,
    weight_sems,
    rows_y_sems,
    rows_v_sems,
    ring_sems,
    loss_sems,
    loss_core_sems,
    core_sems,
    pred_wide_sems,
    pred_thin_sems,
    tail_sems,
    pred_first_sems,
    pred_second_sems,
    pred_third_sems,
    wide_sems,
    thin_sems,
    across_sems,
    final_sems,
    first_sems,
    second_sems,
    third_sems,
):
    me = lax.axis_index("tm")
    x = lax.axis_index("batch")
    y, z, c = me // (2 * NZ), (me // 2) % NZ, me % 2

    def place(yy, zz, cc):
        return (yy * NZ + zz) * 2 + cc

    others_y = [lax.rem(y + k, NY) for k in range(1, NY)]
    others_z = [lax.rem(z + k, NZ) for k in range(1, NZ)]
    u = x * 2 + c
    others_u = [lax.rem(u + k, 2 * NX) for k in range(1, 2 * NX)]
    v = z * 2 + c
    others_v = [lax.rem(v + k, 2 * NZ) for k in range(1, 2 * NZ)]
    row = y // 2
    spot = 2 * jnp.where(y % 2 == 0, z, 2 * NZ - 1 - z) + c
    ring_before = ring_place(row, lax.rem(spot + 4 * NZ - 1, 4 * NZ))
    ring_after = ring_place(row, lax.rem(spot + 1, 4 * NZ))
    residue = residue_of(y, z, c)

    barrier = pltpu.get_barrier_semaphore()

    def greet(tm, batch):
        pl.semaphore_signal(
            barrier, inc=1, device_id={"tm": tm, "batch": batch}, device_id_type=pl.DeviceIdType.MESH
        )

    for k in FAR_FIRST:
        greet(place(others_y[k - 1], z, c), x)
    for k in FAR_FIRST_WIDE:
        greet(y * 2 * NZ + others_v[k - 1], x)
    for k in range(1, NX):
        for cc in range(2):
            greet(place(y, z, cc), lax.rem(x + k, NX))
    greet(ring_before, x)
    greet(ring_after, x)

    loads = [
        pltpu.make_async_copy(src, dst, weight_sems.at[i])
        for i, (src, dst) in enumerate(
            [
                (codes_hbm, codes_ref),
                (owner_hbm, owner_ref),
                (block_hbm, block_ref),
                (w_now_hbm, w_now_ref),
                (w_delay_hbm, w_delay_ref),
                (w_pred_hbm, w_pred_ref),
            ]
        )
    ]
    for load in loads:
        load.start()

    rows, channels = codes_hbm.shape
    cut_a = WIDE
    order = lax.broadcasted_iota(jnp.int32, (1, rows), 1)
    flag = order & 1
    from_vy = picker((((order >> 1) & 7) << 5) + ((order >> 5) << 2) + (((order >> 4) & 1) << 1) + flag, rows)
    from_yv = picker((((order >> 2) & 7) << 5) + (((order >> 1) & 1) << 4) + ((order >> 5) << 1) + flag, rows)
    seat = (11 * ((order & (BLOCK - 1)) >> 2)) & 31
    chip, side, half = seat >> 1, seat & 1, order >> 7
    back = chip >> 3
    goal_y = 2 * (order & 3) + back
    goal_z = jnp.where(back == 0, chip, 2 * NZ - 1 - chip)
    to_yv = picker((goal_y << 5) + (goal_z << 2) + (side << 1) + half, rows)
    to_vy = picker((goal_z << 5) + (side << 4) + (goal_y << 1) + half, rows)

    for load in loads[:3]:
        load.wait()
    names = (owner_ref[...] * 2 + block_ref[...]).astype(F32)
    names = jnp.concatenate([names, jnp.zeros((128 - NNEG, rows), F32)], 0).astype(BF16)
    out_a1_ref[...] = product(to_yv, codes_ref[:, :cut_a]).astype(BF16).reshape(out_a1_ref.shape)
    out_b1_ref[:, :, :128] = product(to_vy, codes_ref[:, cut_a:]).astype(BF16).reshape(2 * NZ, 2 * NY, 128)
    out_b1_ref[:, :, 128:] = times_transposed(to_vy, names).astype(BF16).reshape(2 * NZ, 2 * NY, 128)
    pl.semaphore_wait(barrier, 30)

    def over_y(src_ref, dst_ref, turn):
        dst_ref[y] = src_ref[y]
        return [
            send(
                src_ref.at[others_y[k - 1]],
                dst_ref.at[y],
                rows_y_sems.at[turn],
                k - 1,
                place(others_y[k - 1], z, c),
                x,
            )
            for k in FAR_FIRST
        ]

    def over_v(src_ref, dst_ref, turn):
        dst_ref[v] = src_ref[v]
        return [
            send(
                src_ref.at[others_v[k - 1]],
                dst_ref.at[v],
                rows_v_sems.at[turn],
                k - 1,
                y * 2 * NZ + others_v[k - 1],
                x,
            )
            for k in FAR_FIRST_WIDE
        ]

    def finish(copies):
        for copy in copies:
            copy.wait()

    going_a = over_y(out_a1_ref, in_a1_ref, 0)
    going_b = over_v(out_b1_ref, in_b1_ref, 0)
    finish(going_a)
    out_a2_ref[...] = product(from_yv, in_a1_ref[...].reshape(rows, cut_a)).astype(BF16).reshape(out_a2_ref.shape)
    going_a = over_v(out_a2_ref, in_a2_ref, 1)
    finish(going_b)
    out_b2_ref[...] = product(from_vy, in_b1_ref[...].reshape(rows, 256)).astype(BF16).reshape(out_b2_ref.shape)
    going_b = over_y(out_b2_ref, in_b2_ref, 1)
    finish(going_a)
    mine_ref[:, :cut_a] = product(from_vy, in_a2_ref[...].reshape(rows, cut_a)).astype(BF16)
    ahead = [send(mine_ref.at[:, :cut_a], target_ref.at[:, :cut_a], ring_sems, 0, ring_before, x)]
    finish(going_b)
    mine_ref[:, cut_a:] = in_b2_ref[:, :, :128].reshape(rows, 128)
    chosen_ref[...] = in_b2_ref[:, :, 128:].reshape(rows, 128).astype(F32).astype(jnp.int32)
    ahead.append(send(mine_ref.at[:, cut_a:], target_ref.at[:, cut_a:], ring_sems, 1, ring_before, x))

    inv_root = channels ** (-0.5)
    loss_weight = (channels / (NX * (BLOCK * rows - KSTEP))) ** 0.5
    row_of = lax.broadcasted_iota(jnp.int32, (rows, 1), 0)
    wraps = residue >= BLOCK - KSTEP
    valid = jnp.where(wraps & (row_of == rows - 1), 0.0, 1.0).astype(F32)
    column_of = lax.broadcasted_iota(jnp.int32, (rows, rows), 1)

    shifted = pltpu.roll(mine_ref[...].astype(F32), LAG, 0)
    delayed_ref[...] = jnp.where(row_of >= LAG, shifted, 0.0).astype(BF16)
    for load in loads[3:]:
        load.wait()
    pre_now_ref[...] = product(mine_ref[...], w_now_ref[...])
    lane = lax.broadcasted_iota(jnp.int32, (8, 128), 1)

    def gradient(delay_ref, pred_ref, turn):
        filt = pre_now_ref[:, :channels] + product(delayed_ref[...], delay_ref[:, :channels])
        gate = pre_now_ref[:, channels:] + product(delayed_ref[...], delay_ref[:, channels:])
        tanh_part = jnp.tanh(filt)
        gate_part = jax.nn.sigmoid(gate)
        tanh_ref[...] = tanh_part
        gate_ref[...] = gate_part
        context_ref[...] = (mine_ref[...].astype(F32) + tanh_part * gate_part).astype(BF16)
        predicted = product(context_ref[...], pred_ref[...]).astype(BF16)
        pairs = times_transposed(predicted, mine_ref[...])
        names = chosen_ref[...]
        hot = [column_of == names[:, n : n + 1] for n in range(NNEG)]
        against = [
            jnp.sum(jnp.where(hot[n], pairs, 0.0), axis=1, keepdims=True) * inv_root for n in range(NNEG)
        ]
        if turn == 0:
            finish(ahead)
            raw = target_ref[...].astype(F32)
            moved = jnp.where(row_of < rows - 1, pltpu.roll(raw, rows - 1, 0), 0.0)
            target_ref[...] = jnp.where(wraps, moved, raw).astype(BF16)
        goal = target_ref[...].astype(F32)
        positive = jnp.sum(predicted.astype(F32) * goal, axis=1, keepdims=True) * inv_root
        top = positive
        for score in against:
            top = jnp.maximum(top, score)
        total = jnp.exp(positive - top)
        for score in against:
            total = total + jnp.exp(score - top)
        lse = top + jnp.log(total)
        if turn == 1:
            losses = jnp.broadcast_to(valid * (lse - positive), (rows, 128))
            loss_y_ref[...] = losses.reshape(NY, 32, 128)
            for k, yy in enumerate(others_y):
                loss_going.append(
                    send(loss_y_ref.at[yy], loss_y_in_ref.at[k], loss_sems.at[0], k, place(yy, z, c), x)
                )
        scale = loss_weight * valid
        d_pos = scale * (jnp.exp(positive - lse) - 1.0)
        spread = jnp.zeros((rows, rows), F32)
        for n in range(NNEG):
            spread = spread + jnp.where(hot[n], scale * jnp.exp(against[n] - lse), 0.0)
        high = spread.astype(BF16)
        low = (spread - high.astype(F32)).astype(BF16)
        pulled = product(high, mine_ref[...]) + product(low, mine_ref[...])
        d_pred_ref[...] = ((d_pos * goal + pulled) * inv_root).astype(BF16)
        swap_pred(turn)
        own_pred = pred_part(c)
        d_context = times_transposed(d_pred_ref[...], pred_ref[...])
        tanh_part = tanh_ref[...]
        gate_part = gate_ref[...]
        d_pre_ref[:, :channels] = (d_context * (1.0 - tanh_part * tanh_part) * gate_part).astype(BF16)
        d_pre_ref[:, channels:] = (d_context * tanh_part * gate_part * (1.0 - gate_part)).astype(BF16)
        swap_delay(turn, 0)
        swap_delay(turn, 1)
        start_pred(turn, own_pred)
        for j in range(2):
            start_wide(turn, j, delay_part(j, c))

    def pred_part(cc):
        cols = pl.ds(pl.multiple_of(256 * cc, 256), 256)
        return contract_rows(context_ref[...], d_pred_ref[:, cols])

    def delay_part(j, cc):
        cols = pl.ds(pl.multiple_of(512 * cc + 256 * j, 256), 256)
        return contract_rows(delayed_ref[...], d_pre_ref[:, cols])

    mate = place(y, z, 1 - c)
    swaps = {}
    wide = {}
    thin = {}

    def swap_pred(turn):
        pred_part_ref[turn] = pred_part(1 - c).astype(BF16).reshape(NX, 2, NZ, 8, 256)
        swaps[turn, 2] = send(pred_part_ref.at[turn], pred_core_ref.at[turn], core_sems.at[turn], 2, mate, x)

    def swap_delay(turn, j):
        part_ref[turn, j] = delay_part(j, 1 - c).astype(BF16).reshape(NY * NZ, 8, 256)
        swaps[turn, j] = send(part_ref.at[turn, j], core_ref.at[turn, j], core_sems.at[turn], j, mate, x)

    def start_pred(turn, value):
        swaps[turn, 2].wait()
        both = value.reshape(NX, 2, NZ, 8, 256) + pred_core_ref[turn].astype(F32)
        pred_sum_ref[turn] = both.astype(BF16)
        for k in (2, 1, 3):
            there = lax.rem(x + k, NX)
            wide[turn, 2, k] = send(
                pred_sum_ref.at[turn, there], pred_wide_ref.at[turn, k - 1], pred_wide_sems.at[turn], k - 1, me, there
            )

    def start_wide(turn, j, value):
        swaps[turn, j].wait()
        both = value.reshape(NY * NZ, 8, 256) + core_ref[turn, j].astype(F32)
        sum_ref[turn, j] = both.astype(BF16).reshape(NY, NZ, 8, 256)
        for k in FAR_FIRST:
            if j == 0:
                there = others_y[k - 1]
                src, tm = sum_ref.at[turn, j, there], place(there, z, c)
            else:
                there = others_z[k - 1]
                src, tm = sum_ref.at[turn, j, :, there], place(y, there, c)
            wide[turn, j, k] = send(src, wide_ref.at[turn, j, k - 1], wide_sems.at[turn, j], k - 1, tm, x)

    def settle_pred_wide(turn):
        total = pred_sum_ref[turn, x].astype(F32)
        for k in (1, 3, 2):
            wide[turn, 2, k].wait()
            total = total + pred_wide_ref[turn, k - 1].astype(F32)
        pred_half_ref[turn] = total.astype(BF16)
        for k in FAR_FIRST:
            there = others_z[k - 1]
            thin[turn, 2, k] = send(
                pred_half_ref.at[turn, :, there],
                pred_thin_ref.at[turn, k - 1],
                pred_thin_sems.at[turn],
                k - 1,
                place(y, there, c),
                x,
            )

    tail = {}

    def settle_pred_thin(turn):
        total = pred_half_ref[turn, :, z].astype(F32)
        for k in NEAR_FIRST:
            thin[turn, 2, k].wait()
            total = total + pred_thin_ref[turn, k - 1].astype(F32)
        tail_ref[turn, y] = total.astype(BF16)
        for k in FAR_FIRST:
            there = others_y[k - 1]
            spot = tail_ref.at[turn, y]
            tail[turn, k] = send(spot, spot, tail_sems.at[turn], k - 1, place(there, z, c), x)

    def pred_total(turn):
        for k in NEAR_FIRST:
            tail[turn, k].wait()
        total = tail_ref[turn, 0].astype(F32)
        for yy in range(1, NY):
            total = total + tail_ref[turn, yy].astype(F32)
        return total

    def settle_wide(turn):
        for j in range(2):
            own = sum_ref[turn, j, y] if j == 0 else sum_ref[turn, j, :, z]
            total = own.astype(F32)
            for k in NEAR_FIRST:
                wide[turn, j, k].wait()
                total = total + wide_ref[turn, j, k - 1].astype(F32)
            half_ref[turn, j] = total.astype(BF16)
            for k in FAR_FIRST:
                there = others_z[k - 1] if j == 0 else others_y[k - 1]
                tm = place(y, there, c) if j == 0 else place(there, z, c)
                thin[turn, j, k] = send(
                    half_ref.at[turn, j, there],
                    thin_ref.at[turn, j, k - 1],
                    thin_sems.at[turn, j],
                    k - 1,
                    tm,
                    x,
                )

    def settle_thin(turn, keep_ref):
        for j in range(2):
            total = half_ref[turn, j, z if j == 0 else y].astype(F32)
            for k in NEAR_FIRST:
                thin[turn, j, k].wait()
                total = total + thin_ref[turn, j, k - 1].astype(F32)
            keep_ref[u, :, 256 * j : 256 * (j + 1)] = total

    def cross(keep_ref, sems, peers):
        spot = keep_ref.at[u]
        return [send(spot, spot, sems, k, place(y, z, cc), xx) for k, (cc, xx) in enumerate(peers)]

    def along(j, at, spare):
        return place(at, z, c) if (j == 0) == spare else place(y, at, c)

    loss_going = []

    def loss_to_z():
        finish(loss_going)
        own = jnp.broadcast_to(((lane & 7) == y)[:1], (32, 128))
        held = jnp.where(own, loss_y_ref[y], 0.0)
        for k in range(7):
            source = lax.rem(y + 7 - k, NY)
            came = jnp.broadcast_to(((lane & 7) == source)[:1], (32, 128))
            held = jnp.where(came, loss_y_in_ref[k], held)
        loss_z_ref[...] = jnp.zeros(loss_z_ref.shape, F32)
        for zz in range(NZ):
            loss_z_ref[zz, :4] = held[4 * zz : 4 * zz + 4]
        loss_going[:] = [
            send(loss_z_ref.at[zz], loss_z_in_ref.at[k], loss_sems.at[1], k, place(y, zz, c), x)
            for k, zz in enumerate(others_z)
        ]

    def loss_to_core():
        finish(loss_going)
        held = jnp.where((lane >> 3) == z, loss_z_ref[z], 0.0)
        for k in range(7):
            source = lax.rem(z + 7 - k, NZ)
            held = jnp.where((lane >> 3) == source, loss_z_in_ref[k], held)
        loss_c_ref[...] = held
        loss_going[:] = [send(loss_c_ref, loss_c_in_ref, loss_core_sems, 0, place(y, z, 1 - c), x)]

    gradient(w_delay_ref, w_pred_ref, 0)
    settle_pred_wide(0)
    settle_wide(0)
    settle_pred_thin(0)
    settle_thin(0, across_ref)
    crossing = cross(across_ref, across_sems, [(c, lax.rem(x + k, NX)) for k in (2, 1, 3)])

    first = {}
    second = {}
    pred_whole_ref[c, x, :, z] = pred_total(0).astype(BF16)
    for k in FAR_FIRST:
        spot = pred_whole_ref.at[c, x, :, z]
        first[2, k] = send(spot, spot, pred_first_sems, k - 1, place(y, others_z[k - 1], c), x)
    finish(crossing)
    total = across_ref[c]
    for xx in range(1, NX):
        total = total + across_ref[2 * xx + c]
    for j in range(2):
        whole_ref[c, j, y, z] = total[:, 256 * j : 256 * (j + 1)].astype(BF16)
    for k in FAR_FIRST:
        for j in range(2):
            there = others_z[k - 1] if j == 0 else others_y[k - 1]
            spot = whole_ref.at[c, j, y, z]
            first[j, k] = send(spot, spot, first_sems.at[j], k - 1, along(j, there, False), x)
    for k in NEAR_FIRST:
        first[2, k].wait()
    for k in (2, 1, 3):
        spot = pred_whole_ref.at[c, x]
        second[2, k] = send(spot, spot, pred_second_sems, k - 1, me, lax.rem(x + k, NX))

    def stripe(j, at):
        return whole_ref.at[c, j, at] if j == 0 else whole_ref.at[c, j, :, at]

    for j in range(2):
        for k in NEAR_FIRST:
            first[j, k].wait()
        for k in FAR_FIRST:
            there = others_y[k - 1] if j == 0 else others_z[k - 1]
            spot = stripe(j, y if j == 0 else z)
            second[j, k] = send(spot, spot, second_sems.at[j], k - 1, along(j, there, True), x)
    third = []
    for j in range(2):
        spot = stripe(j, y if j == 0 else z)
        third.append(send(spot, spot, third_sems.at[j], 0, mate, x))
    for k in (1, 3, 2):
        second[2, k].wait()
    pred_third = send(pred_whole_ref.at[c], pred_whole_ref.at[c], pred_third_sems, 0, mate, x)
    for k in NEAR_FIRST:
        for j in range(2):
            second[j, k].wait()
            spot = stripe(j, lax.rem((y if j == 0 else z) + 8 - k, 8))
            third.append(send(spot, spot, third_sems.at[j], k, mate, x))

    pred_third.wait()
    squares = jnp.zeros((8, 256), F32)
    for cc in range(2):
        piece = pred_whole_ref[cc].astype(F32).reshape(NY * NZ, 8, 256)
        squares = squares + jnp.sum(piece * piece, axis=0)
    finish(third)
    for cc in range(2):
        for j in range(2):
            piece = whole_ref[cc, j].astype(F32).reshape(NY * NZ, 8, 256)
            squares = squares + jnp.sum(piece * piece, axis=0)
    norm = jnp.sqrt(jnp.sum(squares))
    step = RHO / (norm + EPS)
    for cc in range(2):
        for j in range(2):
            piece = whole_ref[cc, j].astype(F32).reshape(channels, 256) * step
            low = 512 * cc + 256 * j
            delay_up_ref[:, low : low + 256] = (w_delay_ref[:, low : low + 256].astype(F32) + piece).astype(BF16)
        piece = pred_whole_ref[cc].astype(F32).reshape(channels, 256) * step
        low = 256 * cc
        pred_up_ref[:, low : low + 256] = (w_pred_ref[:, low : low + 256].astype(F32) + piece).astype(BF16)

    gradient(delay_up_ref, pred_up_ref, 1)
    settle_pred_wide(1)
    settle_wide(1)
    settle_pred_thin(1)
    loss_to_z()
    settle_thin(1, final_ref)
    loss_to_core()
    pred_last_ref[...] = pred_total(1)
    final_ref[u, :, 512:] = pred_last_ref[y & 1]
    crossing = cross(final_ref, final_sems, [(uu % 2, uu // 2) for uu in others_u])
    finish(loss_going)
    seat = lax.broadcasted_iota(jnp.int32, (128, 128), 0)
    column = lax.broadcasted_iota(jnp.int32, (128, 128), 1)
    back = jnp.zeros((8, 128), F32)
    for held_ref, cc in ((loss_c_ref, c), (loss_c_in_ref, 1 - c)):
        spread = (seat < NY * NZ) & (residue_of(seat & 7, (seat >> 3) & 7, cc) == column)
        back = back + jnp.dot(
            held_ref[...],
            jnp.where(spread, 1.0, 0.0),
            preferred_element_type=F32,
            precision=lax.Precision.HIGHEST,
        )
    kept = jnp.where(c == 0, back[:2], back[2:4])
    frame_loss_ref[:, :BLOCK] = kept[:1]
    frame_loss_ref[:, BLOCK:] = kept[1:2]
    finish(crossing)
    for cc in range(2):
        total = final_ref[cc, :, :512]
        for xx in range(1, NX):
            total = total + final_ref[2 * xx + cc, :, :512]
        kept = jnp.where(c == 0, total[:4], total[4:])
        grad_delay_ref[:, 512 * cc : 512 * (cc + 1)] = kept
        total = final_ref[2 * (y // 2) + cc, :, 512:]
        kept = jnp.where(c == 0, total[:4], total[4:])
        grad_pred_ref[:, 256 * cc : 256 * (cc + 1)] = kept


def body(latents, w_now, w_delay, w_pred, neg_owner, neg_block):
    codes = latents[0]
    rows, channels = codes.shape
    vmem = pl.BlockSpec(memory_space=pltpu.VMEM)
    stay = pl.BlockSpec(memory_space=pltpu.HBM)
    dma = pltpu.SemaphoreType.DMA
    return pl.pallas_call(
        step_kernel,
        out_shape=(
            jax.ShapeDtypeStruct((4, 2 * channels), F32),
            jax.ShapeDtypeStruct((4, channels), F32),
            jax.ShapeDtypeStruct((1, rows), F32),
        ),
        in_specs=[stay] * 6,
        out_specs=(vmem, vmem, vmem),
        scratch_shapes=[
            pltpu.VMEM((rows, channels), BF16),
            pltpu.VMEM((NNEG, rows), jnp.int32),
            pltpu.VMEM((NNEG, rows), jnp.int32),
            pltpu.VMEM((channels, 2 * channels), BF16),
            pltpu.VMEM((channels, 2 * channels), BF16),
            pltpu.VMEM((channels, channels), BF16),
            pltpu.VMEM((rows, channels), BF16),
            pltpu.VMEM((rows, channels), BF16),
            pltpu.VMEM((rows, 128), jnp.int32),
            pltpu.VMEM((8, 32, WIDE), BF16),
            pltpu.VMEM((8, 32, WIDE), BF16),
            pltpu.VMEM((16, 16, WIDE), BF16),
            pltpu.VMEM((16, 16, WIDE), BF16),
            pltpu.VMEM((16, 16, 256), BF16),
            pltpu.VMEM((16, 16, 256), BF16),
            pltpu.VMEM((8, 32, 256), BF16),
            pltpu.VMEM((8, 32, 256), BF16),
            pltpu.VMEM((8, 32, 128), F32),
            pltpu.VMEM((7, 32, 128), F32),
            pltpu.VMEM((8, 8, 128), F32),
            pltpu.VMEM((7, 8, 128), F32),
            pltpu.VMEM((8, 128), F32),
            pltpu.VMEM((8, 128), F32),
            pltpu.VMEM((rows, channels), BF16),
            pltpu.VMEM((rows, 2 * channels), F32),
            pltpu.VMEM((rows, channels), F32),
            pltpu.VMEM((rows, channels), F32),
            pltpu.VMEM((rows, channels), BF16),
            pltpu.VMEM((rows, channels), BF16),
            pltpu.VMEM((rows, 2 * channels), BF16),
            pltpu.VMEM((channels, 2 * channels), BF16),
            pltpu.VMEM((channels, channels), BF16),
            pltpu.VMEM((2, NX, 2, NZ, 8, 256), BF16),
            pltpu.VMEM((2, NX, 2, NZ, 8, 256), BF16),
            pltpu.VMEM((2, NX, 2, NZ, 8, 256), BF16),
            pltpu.VMEM((2, NX - 1, 2, NZ, 8, 256), BF16),
            pltpu.VMEM((2, 2, NZ, 8, 256), BF16),
            pltpu.VMEM((2, 7, 2, 8, 256), BF16),
            pltpu.VMEM((2, NY, 2, 8, 256), BF16),
            pltpu.VMEM((2, NX, 2, NZ, 8, 256), BF16),
            pltpu.VMEM((2, 8, 256), F32),
            pltpu.VMEM((2, 2, NY * NZ, 8, 256), BF16),
            pltpu.VMEM((2, 2, NY * NZ, 8, 256), BF16),
            pltpu.VMEM((2, 2, NY, NZ, 8, 256), BF16),
            pltpu.VMEM((2, 2, 7, 8, 8, 256), BF16),
            pltpu.VMEM((2, 2, 8, 8, 256), BF16),
            pltpu.VMEM((2, 2, 7, 8, 256), BF16),
            pltpu.VMEM((2 * NX, 8, 512), F32),
            pltpu.VMEM((2 * NX, 8, 768), F32),
            pltpu.VMEM((2, 2, NY, NZ, 8, 256), BF16),
            dma((6,)),
            dma((2, 2, 7)),
            dma((2, 2, 15)),
            dma((2, 2)),
            dma((2, 2, 7)),
            dma((2, 1)),
            dma((2, 2, 3)),
            dma((2, 2, 3)),
            dma((2, 2, 7)),
            dma((2, 2, 7)),
            dma((2, 7)),
            dma((2, 3)),
            dma((2, 1)),
            dma((2, 2, 2, 7)),
            dma((2, 2, 2, 7)),
            dma((2, 3)),
            dma((2, 7)),
            dma((2, 2, 7)),
            dma((2, 2, 7)),
            dma((2, 2, 8)),
        ],
        compiler_params=pltpu.CompilerParams(
            collective_id=0, has_side_effects=True, vmem_limit_bytes=60 * 1024 * 1024
        ),
    )(codes, jnp.swapaxes(neg_owner[0], 0, 1), jnp.swapaxes(neg_block[0], 0, 1), w_now, w_delay, w_pred)


def solution(mesh):
    return jax.shard_map(
        body,
        mesh=mesh,
        in_specs=(P("batch", "tm", None), P(), P(), P(), P("batch", "tm", None), P("batch", "tm", None)),
        out_specs=(P("tm", None), P("tm", None), P("batch", "tm")),
        check_vma=False,
    )
```

```python
import jax
import jax.numpy as jnp
from jax import lax
from jax.experimental import pallas as pl
from jax.experimental.pallas import tpu as pltpu
from jax.sharding import PartitionSpec as P

BLOCK = 128
KSTEP = 12
LAG = 9
NNEG = 4
RHO = 16.0
EPS = 1e-06
NY = NZ = 8
NX = 4
CH = 512
WIDE = 384
FAR_FIRST = (4, 3, 5, 2, 6, 1, 7)
NEAR_FIRST = (1, 7, 2, 6, 3, 5, 4)
FAR_FIRST_WIDE = (8, 9, 7, 6, 10, 11, 5, 4, 12, 13, 3, 2, 14, 15, 1)
F32 = jnp.float32
BF16 = jnp.bfloat16


def contract_rows(left, right):
    return lax.dot_general(left, right, (((0,), (0,)), ((), ())), preferred_element_type=F32)


def times_transposed(left, right):
    return lax.dot_general(left, right, (((1,), (1,)), ((), ())), preferred_element_type=F32)


def product(left, right):
    return jnp.dot(left, right, preferred_element_type=F32)


def send(src, dst, sems, index, tm, batch):
    copy = pltpu.make_async_remote_copy(
        src_ref=src,
        dst_ref=dst,
        send_sem=sems.at[0, index],
        recv_sem=sems.at[1, index],
        device_id={"tm": tm, "batch": batch},
        device_id_type=pl.DeviceIdType.MESH,
    )
    copy.start()
    return copy


def residue_of(yy, zz, cc):
    turn = jnp.where((yy & 1) == 0, zz, 2 * NZ - 1 - zz)
    return ((yy >> 1) + KSTEP * (2 * turn + cc)) & (BLOCK - 1)


def ring_place(row, spot):
    chip, cc = spot // 2, spot % 2
    back = chip // NZ
    zz = jnp.where(back == 0, chip, 2 * NZ - 1 - chip)
    return ((2 * row + back) * NZ + zz) * 2 + cc


def picker(wanted, count):
    return jnp.where(lax.broadcasted_iota(jnp.int32, (count, count), 0) == wanted, 1.0, 0.0).astype(BF16)


def step_kernel(
    codes_hbm,
    owner_hbm,
    block_hbm,
    w_now_hbm,
    w_delay_hbm,
    w_pred_hbm,
    grad_delay_ref,
    grad_pred_ref,
    frame_loss_ref,
    codes_ref,
    owner_ref,
    block_ref,
    w_now_ref,
    w_delay_ref,
    w_pred_ref,
    mine_ref,
    target_ref,
    chosen_ref,
    out_a1_ref,
    in_a1_ref,
    out_a2_ref,
    in_a2_ref,
    out_b1_ref,
    in_b1_ref,
    out_b2_ref,
    in_b2_ref,
    loss_y_ref,
    loss_y_in_ref,
    loss_z_ref,
    loss_z_in_ref,
    loss_c_ref,
    loss_c_in_ref,
    delayed_ref,
    pre_now_ref,
    tanh_ref,
    gate_ref,
    context_ref,
    d_pred_ref,
    d_pre_ref,
    delay_up_ref,
    pred_up_ref,
    pred_part_ref,
    pred_core_ref,
    pred_sum_ref,
    pred_wide_ref,
    pred_half_ref,
    pred_thin_ref,
    tail_ref,
    pred_whole_ref,
    pred_last_ref,
    part_ref,
    core_ref,
    sum_ref,
    wide_ref,
    half_ref,
    thin_ref,
    across_ref,
    final_ref,
    whole_ref,
    weight_sems,
    rows_y_sems,
    rows_v_sems,
    ring_sems,
    loss_sems,
    loss_core_sems,
    core_sems,
    pred_wide_sems,
    pred_thin_sems,
    tail_sems,
    pred_first_sems,
    pred_second_sems,
    pred_third_sems,
    wide_sems,
    thin_sems,
    across_sems,
    final_sems,
    first_sems,
    second_sems,
    third_sems,
):
    me = lax.axis_index("tm")
    x = lax.axis_index("batch")
    y, z, c = me // (2 * NZ), (me // 2) % NZ, me % 2

    def place(yy, zz, cc):
        return (yy * NZ + zz) * 2 + cc

    others_y = [lax.rem(y + k, NY) for k in range(1, NY)]
    others_z = [lax.rem(z + k, NZ) for k in range(1, NZ)]
    u = x * 2 + c
    others_u = [lax.rem(u + k, 2 * NX) for k in range(1, 2 * NX)]
    v = z * 2 + c
    others_v = [lax.rem(v + k, 2 * NZ) for k in range(1, 2 * NZ)]
    row = y // 2
    spot = 2 * jnp.where(y % 2 == 0, z, 2 * NZ - 1 - z) + c
    ring_before = ring_place(row, lax.rem(spot + 4 * NZ - 1, 4 * NZ))
    ring_after = ring_place(row, lax.rem(spot + 1, 4 * NZ))
    residue = residue_of(y, z, c)

    barrier = pltpu.get_barrier_semaphore()

    def greet(tm, batch):
        pl.semaphore_signal(
            barrier, inc=1, device_id={"tm": tm, "batch": batch}, device_id_type=pl.DeviceIdType.MESH
        )

    for k in FAR_FIRST:
        greet(place(others_y[k - 1], z, c), x)
    for k in FAR_FIRST_WIDE:
        greet(y * 2 * NZ + others_v[k - 1], x)
    for k in range(1, NX):
        for cc in range(2):
            greet(place(y, z, cc), lax.rem(x + k, NX))
    greet(ring_before, x)
    greet(ring_after, x)

    loads = [
        pltpu.make_async_copy(src, dst, weight_sems.at[i])
        for i, (src, dst) in enumerate(
            [
                (codes_hbm, codes_ref),
                (owner_hbm, owner_ref),
                (block_hbm, block_ref),
                (w_now_hbm, w_now_ref),
                (w_delay_hbm, w_delay_ref),
                (w_pred_hbm, w_pred_ref),
            ]
        )
    ]
    for load in loads:
        load.start()

    rows, channels = codes_hbm.shape
    cut_a = WIDE
    order = lax.broadcasted_iota(jnp.int32, (1, rows), 1)
    flag = order & 1
    from_vy = picker((((order >> 1) & 7) << 5) + ((order >> 5) << 2) + (((order >> 4) & 1) << 1) + flag, rows)
    from_yv = picker((((order >> 2) & 7) << 5) + (((order >> 1) & 1) << 4) + ((order >> 5) << 1) + flag, rows)
    seat = (11 * ((order & (BLOCK - 1)) >> 2)) & 31
    chip, side, half = seat >> 1, seat & 1, order >> 7
    back = chip >> 3
    goal_y = 2 * (order & 3) + back
    goal_z = jnp.where(back == 0, chip, 2 * NZ - 1 - chip)
    to_yv = picker((goal_y << 5) + (goal_z << 2) + (side << 1) + half, rows)
    to_vy = picker((goal_z << 5) + (side << 4) + (goal_y << 1) + half, rows)

    for load in loads[:3]:
        load.wait()
    names = (owner_ref[...] * 2 + block_ref[...]).astype(F32)
    names = jnp.concatenate([names, jnp.zeros((128 - NNEG, rows), F32)], 0).astype(BF16)
    out_a1_ref[...] = product(to_yv, codes_ref[:, :cut_a]).astype(BF16).reshape(out_a1_ref.shape)
    out_b1_ref[:, :, :128] = product(to_vy, codes_ref[:, cut_a:]).astype(BF16).reshape(2 * NZ, 2 * NY, 128)
    out_b1_ref[:, :, 128:] = times_transposed(to_vy, names).astype(BF16).reshape(2 * NZ, 2 * NY, 128)
    pl.semaphore_wait(barrier, 30)

    def over_y(src_ref, dst_ref, turn):
        dst_ref[y] = src_ref[y]
        return [
            send(
                src_ref.at[others_y[k - 1]],
                dst_ref.at[y],
                rows_y_sems.at[turn],
                k - 1,
                place(others_y[k - 1], z, c),
                x,
            )
            for k in FAR_FIRST
        ]

    def over_v(src_ref, dst_ref, turn):
        dst_ref[v] = src_ref[v]
        return [
            send(
                src_ref.at[others_v[k - 1]],
                dst_ref.at[v],
                rows_v_sems.at[turn],
                k - 1,
                y * 2 * NZ + others_v[k - 1],
                x,
            )
            for k in FAR_FIRST_WIDE
        ]

    def finish(copies):
        for copy in copies:
            copy.wait()

    going_a = over_y(out_a1_ref, in_a1_ref, 0)
    going_b = over_v(out_b1_ref, in_b1_ref, 0)
    finish(going_a)
    out_a2_ref[...] = product(from_yv, in_a1_ref[...].reshape(rows, cut_a)).astype(BF16).reshape(out_a2_ref.shape)
    going_a = over_v(out_a2_ref, in_a2_ref, 1)
    finish(going_b)
    out_b2_ref[...] = product(from_vy, in_b1_ref[...].reshape(rows, 256)).astype(BF16).reshape(out_b2_ref.shape)
    going_b = over_y(out_b2_ref, in_b2_ref, 1)
    finish(going_a)
    mine_ref[:, :cut_a] = product(from_vy, in_a2_ref[...].reshape(rows, cut_a)).astype(BF16)
    ahead = [send(mine_ref.at[:, :cut_a], target_ref.at[:, :cut_a], ring_sems, 0, ring_before, x)]
    finish(going_b)
    mine_ref[:, cut_a:] = in_b2_ref[:, :, :128].reshape(rows, 128)
    chosen_ref[...] = in_b2_ref[:, :, 128:].reshape(rows, 128).astype(F32).astype(jnp.int32)
    ahead.append(send(mine_ref.at[:, cut_a:], target_ref.at[:, cut_a:], ring_sems, 1, ring_before, x))

    inv_root = channels ** (-0.5)
    loss_weight = (channels / (NX * (BLOCK * rows - KSTEP))) ** 0.5
    row_of = lax.broadcasted_iota(jnp.int32, (rows, 1), 0)
    wraps = residue >= BLOCK - KSTEP
    valid = jnp.where(wraps & (row_of == rows - 1), 0.0, 1.0).astype(F32)
    column_of = lax.broadcasted_iota(jnp.int32, (rows, rows), 1)

    shifted = pltpu.roll(mine_ref[...].astype(F32), LAG, 0)
    delayed_ref[...] = jnp.where(row_of >= LAG, shifted, 0.0).astype(BF16)
    for load in loads[3:]:
        load.wait()
    pre_now_ref[...] = product(mine_ref[...], w_now_ref[...])
    lane = lax.broadcasted_iota(jnp.int32, (8, 128), 1)

    def gradient(delay_ref, pred_ref, turn):
        filt = pre_now_ref[:, :channels] + product(delayed_ref[...], delay_ref[:, :channels])
        gate = pre_now_ref[:, channels:] + product(delayed_ref[...], delay_ref[:, channels:])
        tanh_part = jnp.tanh(filt)
        gate_part = jax.nn.sigmoid(gate)
        tanh_ref[...] = tanh_part
        gate_ref[...] = gate_part
        context_ref[...] = (mine_ref[...].astype(F32) + tanh_part * gate_part).astype(BF16)
        predicted = product(context_ref[...], pred_ref[...]).astype(BF16)
        pairs = times_transposed(predicted, mine_ref[...])
        names = chosen_ref[...]
        hot = [column_of == names[:, n : n + 1] for n in range(NNEG)]
        against = [
            jnp.sum(jnp.where(hot[n], pairs, 0.0), axis=1, keepdims=True) * inv_root for n in range(NNEG)
        ]
        peak = against[0]
        for score in against[1:]:
            peak = jnp.maximum(peak, score)
        lifts = [jnp.exp(score - peak) for score in against]
        spread = jnp.zeros((rows, rows), F32)
        for n in range(NNEG):
            spread = spread + jnp.where(hot[n], lifts[n], 0.0)
        high = spread.astype(BF16)
        low = (spread - high.astype(F32)).astype(BF16)
        pulled = product(high, mine_ref[...]) + product(low, mine_ref[...])
        if turn == 0:
            finish(ahead)
            raw = target_ref[...].astype(F32)
            moved = jnp.where(row_of < rows - 1, pltpu.roll(raw, rows - 1, 0), 0.0)
            target_ref[...] = jnp.where(wraps, moved, raw).astype(BF16)
        goal = target_ref[...].astype(F32)
        positive = jnp.sum(predicted.astype(F32) * goal, axis=1, keepdims=True) * inv_root
        top = jnp.maximum(peak, positive)
        total = (lifts[0] + lifts[1] + lifts[2] + lifts[3]) * jnp.exp(peak - top) + jnp.exp(positive - top)
        lse = top + jnp.log(total)
        if turn == 1:
            losses = jnp.broadcast_to(valid * (lse - positive), (rows, 128))
            loss_y_ref[...] = losses.reshape(NY, 32, 128)
            for k, yy in enumerate(others_y):
                loss_going.append(
                    send(loss_y_ref.at[yy], loss_y_in_ref.at[k], loss_sems.at[0], k, place(yy, z, c), x)
                )
        scale = loss_weight * valid
        d_pos = scale * (jnp.exp(positive - lse) - 1.0)
        d_neg = scale * jnp.exp(peak - lse)
        d_pred_ref[...] = ((d_pos * goal + d_neg * pulled) * inv_root).astype(BF16)
        swap_pred(turn)
        own_pred = pred_part(c)
        d_context = times_transposed(d_pred_ref[...], pred_ref[...])
        tanh_part = tanh_ref[...]
        gate_part = gate_ref[...]
        d_pre_ref[:, :channels] = (d_context * (1.0 - tanh_part * tanh_part) * gate_part).astype(BF16)
        d_pre_ref[:, channels:] = (d_context * tanh_part * gate_part * (1.0 - gate_part)).astype(BF16)
        swap_delay(turn, 0)
        swap_delay(turn, 1)
        start_pred(turn, own_pred)
        for j in range(2):
            start_wide(turn, j, delay_part(j, c))

    def pred_part(cc):
        cols = pl.ds(pl.multiple_of(256 * cc, 256), 256)
        return contract_rows(context_ref[...], d_pred_ref[:, cols])

    def delay_part(j, cc):
        cols = pl.ds(pl.multiple_of(512 * cc + 256 * j, 256), 256)
        return contract_rows(delayed_ref[...], d_pre_ref[:, cols])

    mate = place(y, z, 1 - c)
    swaps = {}
    wide = {}
    thin = {}

    def swap_pred(turn):
        pred_part_ref[turn] = pred_part(1 - c).astype(BF16).reshape(NX, 2, NZ, 8, 256)
        swaps[turn, 2] = send(pred_part_ref.at[turn], pred_core_ref.at[turn], core_sems.at[turn], 2, mate, x)

    def swap_delay(turn, j):
        part_ref[turn, j] = delay_part(j, 1 - c).astype(BF16).reshape(NY * NZ, 8, 256)
        swaps[turn, j] = send(part_ref.at[turn, j], core_ref.at[turn, j], core_sems.at[turn], j, mate, x)

    def start_pred(turn, value):
        swaps[turn, 2].wait()
        both = value.reshape(NX, 2, NZ, 8, 256) + pred_core_ref[turn].astype(F32)
        pred_sum_ref[turn] = both.astype(BF16)
        for k in (2, 1, 3):
            there = lax.rem(x + k, NX)
            wide[turn, 2, k] = send(
                pred_sum_ref.at[turn, there], pred_wide_ref.at[turn, k - 1], pred_wide_sems.at[turn], k - 1, me, there
            )

    def start_wide(turn, j, value):
        swaps[turn, j].wait()
        both = value.reshape(NY * NZ, 8, 256) + core_ref[turn, j].astype(F32)
        sum_ref[turn, j] = both.astype(BF16).reshape(NY, NZ, 8, 256)
        for k in FAR_FIRST:
            if j == 0:
                there = others_y[k - 1]
                src, tm = sum_ref.at[turn, j, there], place(there, z, c)
            else:
                there = others_z[k - 1]
                src, tm = sum_ref.at[turn, j, :, there], place(y, there, c)
            wide[turn, j, k] = send(src, wide_ref.at[turn, j, k - 1], wide_sems.at[turn, j], k - 1, tm, x)

    def settle_pred_wide(turn):
        total = pred_sum_ref[turn, x].astype(F32)
        for k in (1, 3, 2):
            wide[turn, 2, k].wait()
            total = total + pred_wide_ref[turn, k - 1].astype(F32)
        pred_half_ref[turn] = total.astype(BF16)
        for k in FAR_FIRST:
            there = others_z[k - 1]
            thin[turn, 2, k] = send(
                pred_half_ref.at[turn, :, there],
                pred_thin_ref.at[turn, k - 1],
                pred_thin_sems.at[turn],
                k - 1,
                place(y, there, c),
                x,
            )

    tail = {}

    def settle_pred_thin(turn):
        total = pred_half_ref[turn, :, z].astype(F32)
        for k in NEAR_FIRST:
            thin[turn, 2, k].wait()
            total = total + pred_thin_ref[turn, k - 1].astype(F32)
        tail_ref[turn, y] = total.astype(BF16)
        for k in FAR_FIRST:
            there = others_y[k - 1]
            spot = tail_ref.at[turn, y]
            tail[turn, k] = send(spot, spot, tail_sems.at[turn], k - 1, place(there, z, c), x)

    def pred_total(turn):
        for k in NEAR_FIRST:
            tail[turn, k].wait()
        total = tail_ref[turn, 0].astype(F32)
        for yy in range(1, NY):
            total = total + tail_ref[turn, yy].astype(F32)
        return total

    def settle_wide(turn):
        for j in range(2):
            own = sum_ref[turn, j, y] if j == 0 else sum_ref[turn, j, :, z]
            total = own.astype(F32)
            for k in NEAR_FIRST:
                wide[turn, j, k].wait()
                total = total + wide_ref[turn, j, k - 1].astype(F32)
            half_ref[turn, j] = total.astype(BF16)
            for k in FAR_FIRST:
                there = others_z[k - 1] if j == 0 else others_y[k - 1]
                tm = place(y, there, c) if j == 0 else place(there, z, c)
                thin[turn, j, k] = send(
                    half_ref.at[turn, j, there],
                    thin_ref.at[turn, j, k - 1],
                    thin_sems.at[turn, j],
                    k - 1,
                    tm,
                    x,
                )

    def settle_thin(turn, keep_ref):
        for j in range(2):
            total = half_ref[turn, j, z if j == 0 else y].astype(F32)
            for k in NEAR_FIRST:
                thin[turn, j, k].wait()
                total = total + thin_ref[turn, j, k - 1].astype(F32)
            keep_ref[u, :, 256 * j : 256 * (j + 1)] = total.astype(BF16)

    def cross(keep_ref, sems, peers):
        spot = keep_ref.at[u]
        return [send(spot, spot, sems, k, place(y, z, cc), xx) for k, (cc, xx) in enumerate(peers)]

    def along(j, at, spare):
        return place(at, z, c) if (j == 0) == spare else place(y, at, c)

    loss_going = []

    def loss_to_z():
        finish(loss_going)
        own = jnp.broadcast_to(((lane & 7) == y)[:1], (32, 128))
        held = jnp.where(own, loss_y_ref[y], 0.0)
        for k in range(7):
            source = lax.rem(y + 7 - k, NY)
            came = jnp.broadcast_to(((lane & 7) == source)[:1], (32, 128))
            held = jnp.where(came, loss_y_in_ref[k], held)
        loss_z_ref[...] = jnp.zeros(loss_z_ref.shape, F32)
        for zz in range(NZ):
            loss_z_ref[zz, :4] = held[4 * zz : 4 * zz + 4]
        loss_going[:] = [
            send(loss_z_ref.at[zz], loss_z_in_ref.at[k], loss_sems.at[1], k, place(y, zz, c), x)
            for k, zz in enumerate(others_z)
        ]

    def loss_to_core():
        finish(loss_going)
        held = jnp.where((lane >> 3) == z, loss_z_ref[z], 0.0)
        for k in range(7):
            source = lax.rem(z + 7 - k, NZ)
            held = jnp.where((lane >> 3) == source, loss_z_in_ref[k], held)
        loss_c_ref[...] = held
        loss_going[:] = [send(loss_c_ref, loss_c_in_ref, loss_core_sems, 0, place(y, z, 1 - c), x)]

    gradient(w_delay_ref, w_pred_ref, 0)
    settle_pred_wide(0)
    settle_wide(0)
    settle_pred_thin(0)
    settle_thin(0, across_ref)
    crossing = cross(across_ref, across_sems, [(c, lax.rem(x + k, NX)) for k in (2, 1, 3)])

    first = {}
    second = {}
    pred_whole_ref[c, x, :, z] = pred_total(0).astype(BF16)
    for k in FAR_FIRST:
        spot = pred_whole_ref.at[c, x, :, z]
        first[2, k] = send(spot, spot, pred_first_sems, k - 1, place(y, others_z[k - 1], c), x)
    finish(crossing)
    total = across_ref[c].astype(F32)
    for xx in range(1, NX):
        total = total + across_ref[2 * xx + c].astype(F32)
    for j in range(2):
        whole_ref[c, j, y, z] = total[:, 256 * j : 256 * (j + 1)].astype(BF16)
    for k in FAR_FIRST:
        for j in range(2):
            there = others_z[k - 1] if j == 0 else others_y[k - 1]
            spot = whole_ref.at[c, j, y, z]
            first[j, k] = send(spot, spot, first_sems.at[j], k - 1, along(j, there, False), x)
    for k in NEAR_FIRST:
        first[2, k].wait()
    for k in (2, 1, 3):
        spot = pred_whole_ref.at[c, x]
        second[2, k] = send(spot, spot, pred_second_sems, k - 1, me, lax.rem(x + k, NX))

    def stripe(j, at):
        return whole_ref.at[c, j, at] if j == 0 else whole_ref.at[c, j, :, at]

    for j in range(2):
        for k in NEAR_FIRST:
            first[j, k].wait()
        for k in FAR_FIRST:
            there = others_y[k - 1] if j == 0 else others_z[k - 1]
            spot = stripe(j, y if j == 0 else z)
            second[j, k] = send(spot, spot, second_sems.at[j], k - 1, along(j, there, True), x)
    third = []
    for j in range(2):
        spot = stripe(j, y if j == 0 else z)
        third.append(send(spot, spot, third_sems.at[j], 0, mate, x))
    for k in (1, 3, 2):
        second[2, k].wait()
    pred_third = send(pred_whole_ref.at[c], pred_whole_ref.at[c], pred_third_sems, 0, mate, x)
    for k in NEAR_FIRST:
        for j in range(2):
            second[j, k].wait()
            spot = stripe(j, lax.rem((y if j == 0 else z) + 8 - k, 8))
            third.append(send(spot, spot, third_sems.at[j], k, mate, x))

    def squares_of(ref, *at):
        piece = ref[at].astype(F32).reshape(NY * NZ, 8, 256)
        return jnp.sum(piece * piece, axis=0)

    own_squares = squares_of(whole_ref, c, 0) + squares_of(whole_ref, c, 1)
    pred_third.wait()
    squares = squares_of(pred_whole_ref, 0) + squares_of(pred_whole_ref, 1)
    finish(third)
    squares = squares + (own_squares + (squares_of(whole_ref, 1 - c, 0) + squares_of(whole_ref, 1 - c, 1)))
    norm = jnp.sqrt(jnp.sum(squares))
    step = RHO / (norm + EPS)
    for cc in range(2):
        for j in range(2):
            piece = whole_ref[cc, j].astype(F32).reshape(channels, 256) * step
            low = 512 * cc + 256 * j
            delay_up_ref[:, low : low + 256] = (w_delay_ref[:, low : low + 256].astype(F32) + piece).astype(BF16)
        piece = pred_whole_ref[cc].astype(F32).reshape(channels, 256) * step
        low = 256 * cc
        pred_up_ref[:, low : low + 256] = (w_pred_ref[:, low : low + 256].astype(F32) + piece).astype(BF16)

    gradient(delay_up_ref, pred_up_ref, 1)
    settle_pred_wide(1)
    settle_wide(1)
    settle_pred_thin(1)
    loss_to_z()
    settle_thin(1, final_ref)
    loss_to_core()
    pred_last_ref[...] = pred_total(1)
    final_ref[u, :, 512:] = pred_last_ref[y & 1].astype(BF16)
    crossing = cross(final_ref, final_sems, [(uu % 2, uu // 2) for uu in others_u])
    finish(loss_going)
    seat = lax.broadcasted_iota(jnp.int32, (128, 128), 0)
    column = lax.broadcasted_iota(jnp.int32, (128, 128), 1)
    back = jnp.zeros((8, 128), F32)
    for held_ref, cc in ((loss_c_ref, c), (loss_c_in_ref, 1 - c)):
        spread = (seat < NY * NZ) & (residue_of(seat & 7, (seat >> 3) & 7, cc) == column)
        back = back + jnp.dot(
            held_ref[...],
            jnp.where(spread, 1.0, 0.0),
            preferred_element_type=F32,
            precision=lax.Precision.HIGHEST,
        )
    kept = jnp.where(c == 0, back[:2], back[2:4])
    frame_loss_ref[:, :BLOCK] = kept[:1]
    frame_loss_ref[:, BLOCK:] = kept[1:2]
    finish(crossing)
    for cc in range(2):
        total = final_ref[cc, :, :512].astype(F32)
        for xx in range(1, NX):
            total = total + final_ref[2 * xx + cc, :, :512].astype(F32)
        kept = jnp.where(c == 0, total[:4], total[4:])
        grad_delay_ref[:, 512 * cc : 512 * (cc + 1)] = kept
        total = final_ref[2 * (y // 2) + cc, :, 512:].astype(F32)
        kept = jnp.where(c == 0, total[:4], total[4:])
        grad_pred_ref[:, 256 * cc : 256 * (cc + 1)] = kept


def body(latents, w_now, w_delay, w_pred, neg_owner, neg_block):
    codes = latents[0]
    rows, channels = codes.shape
    vmem = pl.BlockSpec(memory_space=pltpu.VMEM)
    stay = pl.BlockSpec(memory_space=pltpu.HBM)
    dma = pltpu.SemaphoreType.DMA
    return pl.pallas_call(
        step_kernel,
        out_shape=(
            jax.ShapeDtypeStruct((4, 2 * channels), F32),
            jax.ShapeDtypeStruct((4, channels), F32),
            jax.ShapeDtypeStruct((1, rows), F32),
        ),
        in_specs=[stay] * 6,
        out_specs=(vmem, vmem, vmem),
        scratch_shapes=[
            pltpu.VMEM((rows, channels), BF16),
            pltpu.VMEM((NNEG, rows), jnp.int32),
            pltpu.VMEM((NNEG, rows), jnp.int32),
            pltpu.VMEM((channels, 2 * channels), BF16),
            pltpu.VMEM((channels, 2 * channels), BF16),
            pltpu.VMEM((channels, channels), BF16),
            pltpu.VMEM((rows, channels), BF16),
            pltpu.VMEM((rows, channels), BF16),
            pltpu.VMEM((rows, 128), jnp.int32),
            pltpu.VMEM((8, 32, WIDE), BF16),
            pltpu.VMEM((8, 32, WIDE), BF16),
            pltpu.VMEM((16, 16, WIDE), BF16),
            pltpu.VMEM((16, 16, WIDE), BF16),
            pltpu.VMEM((16, 16, 256), BF16),
            pltpu.VMEM((16, 16, 256), BF16),
            pltpu.VMEM((8, 32, 256), BF16),
            pltpu.VMEM((8, 32, 256), BF16),
            pltpu.VMEM((8, 32, 128), F32),
            pltpu.VMEM((7, 32, 128), F32),
            pltpu.VMEM((8, 8, 128), F32),
            pltpu.VMEM((7, 8, 128), F32),
            pltpu.VMEM((8, 128), F32),
            pltpu.VMEM((8, 128), F32),
            pltpu.VMEM((rows, channels), BF16),
            pltpu.VMEM((rows, 2 * channels), F32),
            pltpu.VMEM((rows, channels), F32),
            pltpu.VMEM((rows, channels), F32),
            pltpu.VMEM((rows, channels), BF16),
            pltpu.VMEM((rows, channels), BF16),
            pltpu.VMEM((rows, 2 * channels), BF16),
            pltpu.VMEM((channels, 2 * channels), BF16),
            pltpu.VMEM((channels, channels), BF16),
            pltpu.VMEM((2, NX, 2, NZ, 8, 256), BF16),
            pltpu.VMEM((2, NX, 2, NZ, 8, 256), BF16),
            pltpu.VMEM((2, NX, 2, NZ, 8, 256), BF16),
            pltpu.VMEM((2, NX - 1, 2, NZ, 8, 256), BF16),
            pltpu.VMEM((2, 2, NZ, 8, 256), BF16),
            pltpu.VMEM((2, 7, 2, 8, 256), BF16),
            pltpu.VMEM((2, NY, 2, 8, 256), BF16),
            pltpu.VMEM((2, NX, 2, NZ, 8, 256), BF16),
            pltpu.VMEM((2, 8, 256), F32),
            pltpu.VMEM((2, 2, NY * NZ, 8, 256), BF16),
            pltpu.VMEM((2, 2, NY * NZ, 8, 256), BF16),
            pltpu.VMEM((2, 2, NY, NZ, 8, 256), BF16),
            pltpu.VMEM((2, 2, 7, 8, 8, 256), BF16),
            pltpu.VMEM((2, 2, 8, 8, 256), BF16),
            pltpu.VMEM((2, 2, 7, 8, 256), BF16),
            pltpu.VMEM((2 * NX, 8, 512), BF16),
            pltpu.VMEM((2 * NX, 8, 768), BF16),
            pltpu.VMEM((2, 2, NY, NZ, 8, 256), BF16),
            dma((6,)),
            dma((2, 2, 7)),
            dma((2, 2, 15)),
            dma((2, 2)),
            dma((2, 2, 7)),
            dma((2, 1)),
            dma((2, 2, 3)),
            dma((2, 2, 3)),
            dma((2, 2, 7)),
            dma((2, 2, 7)),
            dma((2, 7)),
            dma((2, 3)),
            dma((2, 1)),
            dma((2, 2, 2, 7)),
            dma((2, 2, 2, 7)),
            dma((2, 3)),
            dma((2, 7)),
            dma((2, 2, 7)),
            dma((2, 2, 7)),
            dma((2, 2, 8)),
        ],
        compiler_params=pltpu.CompilerParams(
            collective_id=0, has_side_effects=True, vmem_limit_bytes=48 * 1024 * 1024
        ),
    )(
        *(
            pltpu.with_memory_space_constraint(value, pltpu.HBM)
            for value in (
                codes,
                jnp.swapaxes(neg_owner[0], 0, 1),
                jnp.swapaxes(neg_block[0], 0, 1),
                w_now,
                w_delay,
                w_pred,
            )
        )
    )


def solution(mesh):
    return jax.shard_map(
        body,
        mesh=mesh,
        in_specs=(P("batch", "tm", None), P(), P(), P(), P("batch", "tm", None), P("batch", "tm", None)),
        out_specs=(P("tm", None), P("tm", None), P("batch", "tm")),
        check_vma=False,
    )
```

```python
import jax
import jax.numpy as jnp
from jax import lax
from jax.experimental import pallas as pl
from jax.experimental.pallas import tpu as pltpu
from jax.sharding import PartitionSpec as P

BLOCK = 128
KSTEP = 12
LAG = 9
NNEG = 4
RHO = 16.0
EPS = 1e-06
NY = NZ = 8
NX = 4
CH = 512
WIDE = 384
FAR_FIRST = (4, 3, 5, 2, 6, 1, 7)
NEAR_FIRST = (1, 7, 2, 6, 3, 5, 4)
FAR_FIRST_WIDE = (8, 9, 7, 6, 10, 11, 5, 4, 12, 13, 3, 2, 14, 15, 1)
F32 = jnp.float32
BF16 = jnp.bfloat16


def contract_rows(left, right):
    return lax.dot_general(left, right, (((0,), (0,)), ((), ())), preferred_element_type=F32)


def times_transposed(left, right):
    return lax.dot_general(left, right, (((1,), (1,)), ((), ())), preferred_element_type=F32)


def product(left, right):
    return jnp.dot(left, right, preferred_element_type=F32)


def send(src, dst, sems, index, tm, batch):
    copy = pltpu.make_async_remote_copy(
        src_ref=src,
        dst_ref=dst,
        send_sem=sems.at[0, index],
        recv_sem=sems.at[1, index],
        device_id={"tm": tm, "batch": batch},
        device_id_type=pl.DeviceIdType.MESH,
    )
    copy.start()
    return copy


def residue_of(yy, zz, cc):
    turn = jnp.where((yy & 1) == 0, zz, 2 * NZ - 1 - zz)
    return ((yy >> 1) + KSTEP * (2 * turn + cc)) & (BLOCK - 1)


def ring_place(row, spot):
    chip, cc = spot // 2, spot % 2
    back = chip // NZ
    zz = jnp.where(back == 0, chip, 2 * NZ - 1 - chip)
    return ((2 * row + back) * NZ + zz) * 2 + cc


def picker(wanted, count):
    return jnp.where(lax.broadcasted_iota(jnp.int32, (count, count), 0) == wanted, 1.0, 0.0).astype(BF16)


def step_kernel(
    codes_hbm,
    owner_hbm,
    block_hbm,
    w_now_hbm,
    w_delay_hbm,
    w_pred_hbm,
    grad_delay_ref,
    grad_pred_ref,
    frame_loss_ref,
    codes_ref,
    owner_ref,
    block_ref,
    w_now_ref,
    w_delay_ref,
    w_pred_ref,
    mine_ref,
    target_ref,
    chosen_ref,
    out_a1_ref,
    in_a1_ref,
    out_a2_ref,
    in_a2_ref,
    out_b1_ref,
    in_b1_ref,
    out_b2_ref,
    in_b2_ref,
    loss_y_ref,
    loss_y_in_ref,
    loss_z_ref,
    loss_z_in_ref,
    loss_c_ref,
    loss_c_in_ref,
    delayed_ref,
    pre_now_ref,
    tanh_ref,
    gate_ref,
    context_ref,
    d_pred_ref,
    d_pre_ref,
    delay_up_ref,
    pred_up_ref,
    pred_part_ref,
    pred_core_ref,
    pred_sum_ref,
    pred_wide_ref,
    pred_half_ref,
    pred_thin_ref,
    tail_ref,
    pred_whole_ref,
    pred_last_ref,
    part_ref,
    core_ref,
    sum_ref,
    wide_ref,
    half_ref,
    thin_ref,
    across_ref,
    final_ref,
    whole_ref,
    weight_sems,
    rows_y_sems,
    rows_v_sems,
    ring_sems,
    loss_sems,
    loss_core_sems,
    core_sems,
    pred_wide_sems,
    pred_thin_sems,
    tail_sems,
    pred_first_sems,
    pred_second_sems,
    pred_third_sems,
    wide_sems,
    thin_sems,
    across_sems,
    final_sems,
    first_sems,
    second_sems,
    third_sems,
):
    me = lax.axis_index("tm")
    x = lax.axis_index("batch")
    y, z, c = me // (2 * NZ), (me // 2) % NZ, me % 2

    def place(yy, zz, cc):
        return (yy * NZ + zz) * 2 + cc

    others_y = [lax.rem(y + k, NY) for k in range(1, NY)]
    others_z = [lax.rem(z + k, NZ) for k in range(1, NZ)]
    u = x * 2 + c
    others_u = [lax.rem(u + k, 2 * NX) for k in range(1, 2 * NX)]
    v = z * 2 + c
    others_v = [lax.rem(v + k, 2 * NZ) for k in range(1, 2 * NZ)]
    row = y // 2
    spot = 2 * jnp.where(y % 2 == 0, z, 2 * NZ - 1 - z) + c
    ring_before = ring_place(row, lax.rem(spot + 4 * NZ - 1, 4 * NZ))
    ring_after = ring_place(row, lax.rem(spot + 1, 4 * NZ))
    residue = residue_of(y, z, c)

    barrier = pltpu.get_barrier_semaphore()

    def greet(tm, batch):
        pl.semaphore_signal(
            barrier, inc=1, device_id={"tm": tm, "batch": batch}, device_id_type=pl.DeviceIdType.MESH
        )

    for k in FAR_FIRST:
        greet(place(others_y[k - 1], z, c), x)
    for k in FAR_FIRST_WIDE:
        greet(y * 2 * NZ + others_v[k - 1], x)
    for k in range(1, NX):
        for cc in range(2):
            greet(place(y, z, cc), lax.rem(x + k, NX))
    greet(ring_before, x)
    greet(ring_after, x)

    loads = [
        pltpu.make_async_copy(src, dst, weight_sems.at[i])
        for i, (src, dst) in enumerate(
            [
                (codes_hbm, codes_ref),
                (owner_hbm, owner_ref),
                (block_hbm, block_ref),
                (w_now_hbm, w_now_ref),
                (w_delay_hbm, w_delay_ref),
                (w_pred_hbm, w_pred_ref),
            ]
        )
    ]
    for load in loads:
        load.start()

    rows, channels = codes_hbm.shape
    cut_a = WIDE
    order = lax.broadcasted_iota(jnp.int32, (1, rows), 1)
    flag = order & 1
    from_vy = picker((((order >> 1) & 7) << 5) + ((order >> 5) << 2) + (((order >> 4) & 1) << 1) + flag, rows)
    from_yv = picker((((order >> 2) & 7) << 5) + (((order >> 1) & 1) << 4) + ((order >> 5) << 1) + flag, rows)
    seat = (11 * ((order & (BLOCK - 1)) >> 2)) & 31
    chip, side, half = seat >> 1, seat & 1, order >> 7
    back = chip >> 3
    goal_y = 2 * (order & 3) + back
    goal_z = jnp.where(back == 0, chip, 2 * NZ - 1 - chip)
    to_yv = picker((goal_y << 5) + (goal_z << 2) + (side << 1) + half, rows)
    to_vy = picker((goal_z << 5) + (side << 4) + (goal_y << 1) + half, rows)

    for load in loads[:3]:
        load.wait()
    names = (owner_ref[...] * 2 + block_ref[...]).astype(F32)
    names = jnp.concatenate([names, jnp.zeros((128 - NNEG, rows), F32)], 0).astype(BF16)
    out_a1_ref[...] = product(to_yv, codes_ref[:, :cut_a]).astype(BF16).reshape(out_a1_ref.shape)
    out_b1_ref[:, :, :128] = product(to_vy, codes_ref[:, cut_a:]).astype(BF16).reshape(2 * NZ, 2 * NY, 128)
    out_b1_ref[:, :, 128:] = times_transposed(to_vy, names).astype(BF16).reshape(2 * NZ, 2 * NY, 128)
    pl.semaphore_wait(barrier, 30)

    def over_y(src_ref, dst_ref, turn):
        dst_ref[y] = src_ref[y]
        return [
            send(
                src_ref.at[others_y[k - 1]],
                dst_ref.at[y],
                rows_y_sems.at[turn],
                k - 1,
                place(others_y[k - 1], z, c),
                x,
            )
            for k in FAR_FIRST
        ]

    def over_v(src_ref, dst_ref, turn):
        dst_ref[v] = src_ref[v]
        return [
            send(
                src_ref.at[others_v[k - 1]],
                dst_ref.at[v],
                rows_v_sems.at[turn],
                k - 1,
                y * 2 * NZ + others_v[k - 1],
                x,
            )
            for k in FAR_FIRST_WIDE
        ]

    def finish(copies):
        for copy in copies:
            copy.wait()

    going_a = over_y(out_a1_ref, in_a1_ref, 0)
    going_b = over_v(out_b1_ref, in_b1_ref, 0)
    finish(going_b)
    out_b2_ref[...] = product(from_vy, in_b1_ref[...].reshape(rows, 256)).astype(BF16).reshape(out_b2_ref.shape)
    later_b = over_y(out_b2_ref, in_b2_ref, 1)
    finish(going_a)
    out_a2_ref[...] = product(from_yv, in_a1_ref[...].reshape(rows, cut_a)).astype(BF16).reshape(out_a2_ref.shape)
    later_a = over_v(out_a2_ref, in_a2_ref, 1)
    finish(later_a)
    mine_ref[:, :cut_a] = product(from_vy, in_a2_ref[...].reshape(rows, cut_a)).astype(BF16)
    ahead = [send(mine_ref.at[:, :cut_a], target_ref.at[:, :cut_a], ring_sems, 0, ring_before, x)]
    finish(later_b)
    mine_ref[:, cut_a:] = in_b2_ref[:, :, :128].reshape(rows, 128)
    chosen_ref[...] = in_b2_ref[:, :, 128:].reshape(rows, 128).astype(F32).astype(jnp.int32)
    ahead.append(send(mine_ref.at[:, cut_a:], target_ref.at[:, cut_a:], ring_sems, 1, ring_before, x))

    inv_root = channels ** (-0.5)
    loss_weight = (channels / (NX * (BLOCK * rows - KSTEP))) ** 0.5
    row_of = lax.broadcasted_iota(jnp.int32, (rows, 1), 0)
    wraps = residue >= BLOCK - KSTEP
    valid = jnp.where(wraps & (row_of == rows - 1), 0.0, 1.0).astype(F32)
    column_of = lax.broadcasted_iota(jnp.int32, (rows, rows), 1)

    shifted = pltpu.roll(mine_ref[...].astype(F32), LAG, 0)
    delayed_ref[...] = jnp.where(row_of >= LAG, shifted, 0.0).astype(BF16)
    for load in loads[3:]:
        load.wait()
    pre_now_ref[...] = product(mine_ref[...], w_now_ref[...])
    lane = lax.broadcasted_iota(jnp.int32, (8, 128), 1)

    def gradient(delay_ref, pred_ref, turn):
        filt = pre_now_ref[:, :channels] + product(delayed_ref[...], delay_ref[:, :channels])
        gate = pre_now_ref[:, channels:] + product(delayed_ref[...], delay_ref[:, channels:])
        tanh_part = jnp.tanh(filt)
        gate_part = jax.nn.sigmoid(gate)
        tanh_ref[...] = tanh_part
        gate_ref[...] = gate_part
        context_ref[...] = (mine_ref[...].astype(F32) + tanh_part * gate_part).astype(BF16)
        predicted = product(context_ref[...], pred_ref[...]).astype(BF16)
        pairs = times_transposed(predicted, mine_ref[...])
        names = chosen_ref[...]
        hot = [column_of == names[:, n : n + 1] for n in range(NNEG)]
        against = [
            jnp.sum(jnp.where(hot[n], pairs, 0.0), axis=1, keepdims=True) * inv_root for n in range(NNEG)
        ]
        peak = against[0]
        for score in against[1:]:
            peak = jnp.maximum(peak, score)
        lifts = [jnp.exp(score - peak) for score in against]
        spread = jnp.zeros((rows, rows), F32)
        for n in range(NNEG):
            spread = spread + jnp.where(hot[n], lifts[n], 0.0)
        high = spread.astype(BF16)
        low = (spread - high.astype(F32)).astype(BF16)
        pulled = product(high, mine_ref[...]) + product(low, mine_ref[...])
        if turn == 0:
            finish(ahead)
            raw = target_ref[...].astype(F32)
            moved = jnp.where(row_of < rows - 1, pltpu.roll(raw, rows - 1, 0), 0.0)
            target_ref[...] = jnp.where(wraps, moved, raw).astype(BF16)
        goal = target_ref[...].astype(F32)
        positive = jnp.sum(predicted.astype(F32) * goal, axis=1, keepdims=True) * inv_root
        top = jnp.maximum(peak, positive)
        total = (lifts[0] + lifts[1] + lifts[2] + lifts[3]) * jnp.exp(peak - top) + jnp.exp(positive - top)
        lse = top + jnp.log(total)
        if turn == 1:
            losses = jnp.broadcast_to(valid * (lse - positive), (rows, 128))
            loss_y_ref[...] = losses.reshape(NY, 32, 128)
            for k, yy in enumerate(others_y):
                loss_going.append(
                    send(loss_y_ref.at[yy], loss_y_in_ref.at[k], loss_sems.at[0], k, place(yy, z, c), x)
                )
        scale = loss_weight * valid
        d_pos = scale * (jnp.exp(positive - lse) - 1.0)
        d_neg = scale * jnp.exp(peak - lse)
        d_pred_ref[...] = ((d_pos * goal + d_neg * pulled) * inv_root).astype(BF16)
        swap_pred(turn)
        d_context = times_transposed(d_pred_ref[...], pred_ref[...])
        tanh_part = tanh_ref[...]
        gate_part = gate_ref[...]
        d_pre_ref[:, :channels] = (d_context * (1.0 - tanh_part * tanh_part) * gate_part).astype(BF16)
        d_pre_ref[:, channels:] = (d_context * tanh_part * gate_part * (1.0 - gate_part)).astype(BF16)
        swap_delay(turn, 0)
        swap_delay(turn, 1)
        start_pred(turn, pred_part(c))
        for j in range(2):
            start_wide(turn, j, delay_part(j, c))

    def pred_part(cc):
        cols = pl.ds(pl.multiple_of(256 * cc, 256), 256)
        return contract_rows(context_ref[...], d_pred_ref[:, cols])

    def delay_part(j, cc):
        cols = pl.ds(pl.multiple_of(512 * cc + 256 * j, 256), 256)
        return contract_rows(delayed_ref[...], d_pre_ref[:, cols])

    mate = place(y, z, 1 - c)
    swaps = {}
    wide = {}
    thin = {}

    def swap_pred(turn):
        pred_part_ref[turn] = pred_part(1 - c).astype(BF16).reshape(NX, 2, NZ, 8, 256)
        swaps[turn, 2] = send(pred_part_ref.at[turn], pred_core_ref.at[turn], core_sems.at[turn], 2, mate, x)

    def swap_delay(turn, j):
        part_ref[turn, j] = delay_part(j, 1 - c).astype(BF16).reshape(NY * NZ, 8, 256)
        swaps[turn, j] = send(part_ref.at[turn, j], core_ref.at[turn, j], core_sems.at[turn], j, mate, x)

    def start_pred(turn, value):
        swaps[turn, 2].wait()
        both = value.reshape(NX, 2, NZ, 8, 256) + pred_core_ref[turn].astype(F32)
        pred_sum_ref[turn] = both.astype(BF16)
        for k in (2, 1, 3):
            there = lax.rem(x + k, NX)
            wide[turn, 2, k] = send(
                pred_sum_ref.at[turn, there], pred_wide_ref.at[turn, k - 1], pred_wide_sems.at[turn], k - 1, me, there
            )

    def start_wide(turn, j, value):
        swaps[turn, j].wait()
        both = value.reshape(NY * NZ, 8, 256) + core_ref[turn, j].astype(F32)
        sum_ref[turn, j] = both.astype(BF16).reshape(NY, NZ, 8, 256)
        for k in FAR_FIRST:
            if j == 0:
                there = others_y[k - 1]
                src, tm = sum_ref.at[turn, j, there], place(there, z, c)
            else:
                there = others_z[k - 1]
                src, tm = sum_ref.at[turn, j, :, there], place(y, there, c)
            wide[turn, j, k] = send(src, wide_ref.at[turn, j, k - 1], wide_sems.at[turn, j], k - 1, tm, x)

    def settle_pred_wide(turn):
        total = pred_sum_ref[turn, x].astype(F32)
        for k in (1, 3, 2):
            wide[turn, 2, k].wait()
            total = total + pred_wide_ref[turn, k - 1].astype(F32)
        pred_half_ref[turn] = total.astype(BF16)
        for k in FAR_FIRST:
            there = others_z[k - 1]
            thin[turn, 2, k] = send(
                pred_half_ref.at[turn, :, there],
                pred_thin_ref.at[turn, k - 1],
                pred_thin_sems.at[turn],
                k - 1,
                place(y, there, c),
                x,
            )

    tail = {}

    def settle_pred_thin(turn):
        total = pred_half_ref[turn, :, z].astype(F32)
        for k in NEAR_FIRST:
            thin[turn, 2, k].wait()
            total = total + pred_thin_ref[turn, k - 1].astype(F32)
        tail_ref[turn, y] = total.astype(BF16)
        for k in FAR_FIRST:
            there = others_y[k - 1]
            spot = tail_ref.at[turn, y]
            tail[turn, k] = send(spot, spot, tail_sems.at[turn], k - 1, place(there, z, c), x)

    def pred_total(turn):
        for k in NEAR_FIRST:
            tail[turn, k].wait()
        total = tail_ref[turn, 0].astype(F32)
        for yy in range(1, NY):
            total = total + tail_ref[turn, yy].astype(F32)
        return total

    def settle_wide(turn):
        for j in range(2):
            own = sum_ref[turn, j, y] if j == 0 else sum_ref[turn, j, :, z]
            total = own.astype(F32)
            for k in NEAR_FIRST:
                wide[turn, j, k].wait()
                total = total + wide_ref[turn, j, k - 1].astype(F32)
            half_ref[turn, j] = total.astype(BF16)
            for k in FAR_FIRST:
                there = others_z[k - 1] if j == 0 else others_y[k - 1]
                tm = place(y, there, c) if j == 0 else place(there, z, c)
                thin[turn, j, k] = send(
                    half_ref.at[turn, j, there],
                    thin_ref.at[turn, j, k - 1],
                    thin_sems.at[turn, j],
                    k - 1,
                    tm,
                    x,
                )

    def settle_thin(turn, keep_ref):
        for j in range(2):
            total = half_ref[turn, j, z if j == 0 else y].astype(F32)
            for k in NEAR_FIRST:
                thin[turn, j, k].wait()
                total = total + thin_ref[turn, j, k - 1].astype(F32)
            keep_ref[u, :, 256 * j : 256 * (j + 1)] = total.astype(BF16)

    def cross(keep_ref, sems, peers):
        spot = keep_ref.at[u]
        return [send(spot, spot, sems, k, place(y, z, cc), xx) for k, (cc, xx) in enumerate(peers)]

    def along(j, at, spare):
        return place(at, z, c) if (j == 0) == spare else place(y, at, c)

    loss_going = []

    def loss_to_z():
        finish(loss_going)
        own = jnp.broadcast_to(((lane & 7) == y)[:1], (32, 128))
        held = jnp.where(own, loss_y_ref[y], 0.0)
        for k in range(7):
            source = lax.rem(y + 7 - k, NY)
            came = jnp.broadcast_to(((lane & 7) == source)[:1], (32, 128))
            held = jnp.where(came, loss_y_in_ref[k], held)
        loss_z_ref[...] = jnp.zeros(loss_z_ref.shape, F32)
        for zz in range(NZ):
            loss_z_ref[zz, :4] = held[4 * zz : 4 * zz + 4]
        loss_going[:] = [
            send(loss_z_ref.at[zz], loss_z_in_ref.at[k], loss_sems.at[1], k, place(y, zz, c), x)
            for k, zz in enumerate(others_z)
        ]

    def loss_to_core():
        finish(loss_going)
        held = jnp.where((lane >> 3) == z, loss_z_ref[z], 0.0)
        for k in range(7):
            source = lax.rem(z + 7 - k, NZ)
            held = jnp.where((lane >> 3) == source, loss_z_in_ref[k], held)
        loss_c_ref[...] = held
        loss_going[:] = [send(loss_c_ref, loss_c_in_ref, loss_core_sems, 0, place(y, z, 1 - c), x)]

    gradient(w_delay_ref, w_pred_ref, 0)
    settle_pred_wide(0)
    settle_wide(0)
    settle_pred_thin(0)
    settle_thin(0, across_ref)
    crossing = cross(across_ref, across_sems, [(c, lax.rem(x + k, NX)) for k in (2, 1, 3)])

    first = {}
    second = {}
    pred_whole_ref[c, x, :, z] = pred_total(0).astype(BF16)
    for k in FAR_FIRST:
        spot = pred_whole_ref.at[c, x, :, z]
        first[2, k] = send(spot, spot, pred_first_sems, k - 1, place(y, others_z[k - 1], c), x)
    finish(crossing)
    total = across_ref[c].astype(F32)
    for xx in range(1, NX):
        total = total + across_ref[2 * xx + c].astype(F32)
    for j in range(2):
        whole_ref[c, j, y, z] = total[:, 256 * j : 256 * (j + 1)].astype(BF16)
    for k in FAR_FIRST:
        for j in range(2):
            there = others_z[k - 1] if j == 0 else others_y[k - 1]
            spot = whole_ref.at[c, j, y, z]
            first[j, k] = send(spot, spot, first_sems.at[j], k - 1, along(j, there, False), x)
    for k in NEAR_FIRST:
        first[2, k].wait()
    for k in (2, 1, 3):
        spot = pred_whole_ref.at[c, x]
        second[2, k] = send(spot, spot, pred_second_sems, k - 1, me, lax.rem(x + k, NX))

    def stripe(j, at):
        return whole_ref.at[c, j, at] if j == 0 else whole_ref.at[c, j, :, at]

    for j in range(2):
        for k in NEAR_FIRST:
            first[j, k].wait()
        for k in FAR_FIRST:
            there = others_y[k - 1] if j == 0 else others_z[k - 1]
            spot = stripe(j, y if j == 0 else z)
            second[j, k] = send(spot, spot, second_sems.at[j], k - 1, along(j, there, True), x)
    third = []
    for j in range(2):
        spot = stripe(j, y if j == 0 else z)
        third.append(send(spot, spot, third_sems.at[j], 0, mate, x))
    for k in (1, 3, 2):
        second[2, k].wait()
    pred_third = send(pred_whole_ref.at[c], pred_whole_ref.at[c], pred_third_sems, 0, mate, x)
    for k in NEAR_FIRST:
        for j in range(2):
            second[j, k].wait()
            spot = stripe(j, lax.rem((y if j == 0 else z) + 8 - k, 8))
            third.append(send(spot, spot, third_sems.at[j], k, mate, x))

    def squares_of(ref, *at):
        piece = ref[at].astype(F32).reshape(NY * NZ, 8, 256)
        return jnp.sum(piece * piece, axis=0)

    own_squares = squares_of(whole_ref, c, 0) + squares_of(whole_ref, c, 1)
    pred_third.wait()
    squares = squares_of(pred_whole_ref, 0) + squares_of(pred_whole_ref, 1)
    finish(third)
    squares = squares + (own_squares + (squares_of(whole_ref, 1 - c, 0) + squares_of(whole_ref, 1 - c, 1)))
    norm = jnp.sqrt(jnp.sum(squares))
    step = RHO / (norm + EPS)
    for cc in range(2):
        for j in range(2):
            piece = whole_ref[cc, j].astype(F32).reshape(channels, 256) * step
            low = 512 * cc + 256 * j
            delay_up_ref[:, low : low + 256] = (w_delay_ref[:, low : low + 256].astype(F32) + piece).astype(BF16)
        piece = pred_whole_ref[cc].astype(F32).reshape(channels, 256) * step
        low = 256 * cc
        pred_up_ref[:, low : low + 256] = (w_pred_ref[:, low : low + 256].astype(F32) + piece).astype(BF16)

    gradient(delay_up_ref, pred_up_ref, 1)
    settle_pred_wide(1)
    settle_wide(1)
    settle_pred_thin(1)
    loss_to_z()
    settle_thin(1, final_ref)
    loss_to_core()
    pred_last_ref[...] = pred_total(1)
    final_ref[u, :, 512:] = pred_last_ref[y & 1].astype(BF16)
    crossing = cross(final_ref, final_sems, [(uu % 2, uu // 2) for uu in others_u])
    finish(loss_going)
    seat = lax.broadcasted_iota(jnp.int32, (128, 128), 0)
    column = lax.broadcasted_iota(jnp.int32, (128, 128), 1)
    back = jnp.zeros((8, 128), F32)
    for held_ref, cc in ((loss_c_ref, c), (loss_c_in_ref, 1 - c)):
        spread = (seat < NY * NZ) & (residue_of(seat & 7, (seat >> 3) & 7, cc) == column)
        back = back + jnp.dot(
            held_ref[...],
            jnp.where(spread, 1.0, 0.0),
            preferred_element_type=F32,
            precision=lax.Precision.HIGHEST,
        )
    kept = jnp.where(c == 0, back[:2], back[2:4])
    frame_loss_ref[:, :BLOCK] = kept[:1]
    frame_loss_ref[:, BLOCK:] = kept[1:2]
    finish(crossing)
    for cc in range(2):
        total = final_ref[cc, :, :512].astype(F32)
        for xx in range(1, NX):
            total = total + final_ref[2 * xx + cc, :, :512].astype(F32)
        kept = jnp.where(c == 0, total[:4], total[4:])
        grad_delay_ref[:, 512 * cc : 512 * (cc + 1)] = kept
        total = final_ref[2 * (y // 2) + cc, :, 512:].astype(F32)
        kept = jnp.where(c == 0, total[:4], total[4:])
        grad_pred_ref[:, 256 * cc : 256 * (cc + 1)] = kept


def body(latents, w_now, w_delay, w_pred, neg_owner, neg_block):
    codes = latents[0]
    rows, channels = codes.shape
    vmem = pl.BlockSpec(memory_space=pltpu.VMEM)
    stay = pl.BlockSpec(memory_space=pltpu.HBM)
    dma = pltpu.SemaphoreType.DMA
    return pl.pallas_call(
        step_kernel,
        out_shape=(
            jax.ShapeDtypeStruct((4, 2 * channels), F32),
            jax.ShapeDtypeStruct((4, channels), F32),
            jax.ShapeDtypeStruct((1, rows), F32),
        ),
        in_specs=[stay] * 6,
        out_specs=(vmem, vmem, vmem),
        scratch_shapes=[
            pltpu.VMEM((rows, channels), BF16),
            pltpu.VMEM((NNEG, rows), jnp.int32),
            pltpu.VMEM((NNEG, rows), jnp.int32),
            pltpu.VMEM((channels, 2 * channels), BF16),
            pltpu.VMEM((channels, 2 * channels), BF16),
            pltpu.VMEM((channels, channels), BF16),
            pltpu.VMEM((rows, channels), BF16),
            pltpu.VMEM((rows, channels), BF16),
            pltpu.VMEM((rows, 128), jnp.int32),
            pltpu.VMEM((8, 32, WIDE), BF16),
            pltpu.VMEM((8, 32, WIDE), BF16),
            pltpu.VMEM((16, 16, WIDE), BF16),
            pltpu.VMEM((16, 16, WIDE), BF16),
            pltpu.VMEM((16, 16, 256), BF16),
            pltpu.VMEM((16, 16, 256), BF16),
            pltpu.VMEM((8, 32, 256), BF16),
            pltpu.VMEM((8, 32, 256), BF16),
            pltpu.VMEM((8, 32, 128), F32),
            pltpu.VMEM((7, 32, 128), F32),
            pltpu.VMEM((8, 8, 128), F32),
            pltpu.VMEM((7, 8, 128), F32),
            pltpu.VMEM((8, 128), F32),
            pltpu.VMEM((8, 128), F32),
            pltpu.VMEM((rows, channels), BF16),
            pltpu.VMEM((rows, 2 * channels), F32),
            pltpu.VMEM((rows, channels), F32),
            pltpu.VMEM((rows, channels), F32),
            pltpu.VMEM((rows, channels), BF16),
            pltpu.VMEM((rows, channels), BF16),
            pltpu.VMEM((rows, 2 * channels), BF16),
            pltpu.VMEM((channels, 2 * channels), BF16),
            pltpu.VMEM((channels, channels), BF16),
            pltpu.VMEM((2, NX, 2, NZ, 8, 256), BF16),
            pltpu.VMEM((2, NX, 2, NZ, 8, 256), BF16),
            pltpu.VMEM((2, NX, 2, NZ, 8, 256), BF16),
            pltpu.VMEM((2, NX - 1, 2, NZ, 8, 256), BF16),
            pltpu.VMEM((2, 2, NZ, 8, 256), BF16),
            pltpu.VMEM((2, 7, 2, 8, 256), BF16),
            pltpu.VMEM((2, NY, 2, 8, 256), BF16),
            pltpu.VMEM((2, NX, 2, NZ, 8, 256), BF16),
            pltpu.VMEM((2, 8, 256), F32),
            pltpu.VMEM((2, 2, NY * NZ, 8, 256), BF16),
            pltpu.VMEM((2, 2, NY * NZ, 8, 256), BF16),
            pltpu.VMEM((2, 2, NY, NZ, 8, 256), BF16),
            pltpu.VMEM((2, 2, 7, 8, 8, 256), BF16),
            pltpu.VMEM((2, 2, 8, 8, 256), BF16),
            pltpu.VMEM((2, 2, 7, 8, 256), BF16),
            pltpu.VMEM((2 * NX, 8, 512), BF16),
            pltpu.VMEM((2 * NX, 8, 768), BF16),
            pltpu.VMEM((2, 2, NY, NZ, 8, 256), BF16),
            dma((6,)),
            dma((2, 2, 7)),
            dma((2, 2, 15)),
            dma((2, 2)),
            dma((2, 2, 7)),
            dma((2, 1)),
            dma((2, 2, 3)),
            dma((2, 2, 3)),
            dma((2, 2, 7)),
            dma((2, 2, 7)),
            dma((2, 7)),
            dma((2, 3)),
            dma((2, 1)),
            dma((2, 2, 2, 7)),
            dma((2, 2, 2, 7)),
            dma((2, 3)),
            dma((2, 7)),
            dma((2, 2, 7)),
            dma((2, 2, 7)),
            dma((2, 2, 8)),
        ],
        compiler_params=pltpu.CompilerParams(
            collective_id=0, has_side_effects=True, vmem_limit_bytes=48 * 1024 * 1024
        ),
    )(
        *(
            pltpu.with_memory_space_constraint(value, pltpu.HBM)
            for value in (
                codes,
                jnp.swapaxes(neg_owner[0], 0, 1),
                jnp.swapaxes(neg_block[0], 0, 1),
                w_now,
                w_delay,
                w_pred,
            )
        )
    )


def solution(mesh):
    return jax.shard_map(
        body,
        mesh=mesh,
        in_specs=(P("batch", "tm", None), P(), P(), P(), P("batch", "tm", None), P("batch", "tm", None)),
        out_specs=(P("tm", None), P("tm", None), P("batch", "tm")),
        check_vma=False,
    )
```
